256 devices in a mesh: seq: 32 (over x, y, core), head: 8 (over z).
Axes of the slice: x: 4, y: 4, z: 8, core: 2. Of those that a mesh axis runs over, the one named last changes fastest.
Arguments:
- positions: int32 [16384], P('seq'), may hold values from 65535 to 98301, as said below
- queries: bfloat16 [16384, 32, 128], P('seq', 'head'), may hold values from -16 to 16
- keys: bfloat16 [16384, 16, 128], P('seq', 'head'), may hold values from -16 to 16
- values: bfloat16 [16384, 16, 128], P('seq', 'head'), may hold values from -6 to 6
- out_weight: bfloat16 [4096, 5376], P('head', 'seq'), may hold values from -0.1875 to 0.1875
- post_gain: float32 [5376], P('head'), may hold values from 0.25 to 1.75
- residual: bfloat16 [16384, 5376], P('seq', 'head'), may hold values from -6 to 6
Outputs:
- layer_out: bfloat16 [16384, 5376], P('seq', 'head')
The draws below stay inside these ranges and needn't reach their ends.
Inputs may be any that keep to these rules, and one draw needn't show every extreme that they name: `positions`: strictly rising, by 1 or 2 from one token to the next; the last token's position is the most.
All inputs are finite; a program needn't handle non-finite values.
Results may differ from the reference program's by a relative error of at most 0.015.
Values may be sent and summed in bfloat16 or wider, within the bound.
No kernel may reach another device: no remote copies, remote signals or barrier semaphores. Data moves between devices by JAX's collectives and lax.ppermute only.
A program may use at most 64 MiB of HBM per device.

```python
import jax
import jax.numpy as jnp
from jax import lax

D = 5376
QUERY_HEADS = 32
KEY_VALUE_HEADS = 16
HEAD_SIZE = 128
VISIBLE_SPAN = 1024
SLAB_TOKENS = 16384
N_HEAD = 8


def draw_positions(key, part):
    spacing = jax.random.randint(jax.random.fold_in(key, 22), (SLAB_TOKENS,), 1, 3).astype(jnp.int32)
    after = jnp.cumsum(spacing[::-1])[::-1] - spacing
    last_position = 65535 + 2 * SLAB_TOKENS - 2
    return (last_position - after).astype(jnp.int32)


def draw_keys(key, part):
    drawn_output = jnp.clip(jax.random.normal(jax.random.fold_in(key, 11), (SLAB_TOKENS, KEY_VALUE_HEADS, HEAD_SIZE), jnp.float32), -16.0, 16.0)
    return drawn_output.astype(jnp.bfloat16)


def draw_queries(key, part):
    drawn_output = jnp.clip(jax.random.normal(jax.random.fold_in(key, 12), (SLAB_TOKENS, QUERY_HEADS, HEAD_SIZE), jnp.float32), -16.0, 16.0)
    return drawn_output.astype(jnp.bfloat16)


def spiked(values, rng, source, target, shards_of, factor):
    def block_of(position):
        return (jnp.arange(values.shape[position]) // (values.shape[position] // shards_of)).reshape((-1,) + (1,) * (values.ndim - 1 - position))

    near = jax.random.permutation(rng, shards_of)[block_of(target)]
    other_side = (block_of(target) + shards_of // 2) % shards_of
    return jnp.where((block_of(source) == near) | (block_of(source) == other_side), factor * values, values)


def shard_levels(key, shape, shards, least, largest):
    gain, own = 1.0, jax.random.fold_in(key, 6)
    for dim, parts in shards:
        steps = jnp.exp(jax.random.uniform(jax.random.fold_in(own, dim), (parts,), jnp.float32, least / len(shards), largest / len(shards)))
        gain = gain * jnp.repeat(steps, shape[dim] // parts).reshape([-1 if axis == dim else 1 for axis in range(len(shape))])
    return gain


def gaussian(own_key, extent, scale, bound, pieces=(), kind=jnp.bfloat16):
    array = scale * jax.random.normal(own_key, extent, jnp.float32)
    if pieces:
        array = array * shard_levels(own_key, extent, pieces, -0.22, 0.18)
    return jnp.clip(array, -bound, bound).astype(kind)


def heavy_noise(stream_key, shape, deviation, most, cuts, heavy, kind=jnp.bfloat16):
    entries = deviation * jax.random.normal(stream_key, shape, jnp.float32)
    if cuts:
        entries = entries * shard_levels(stream_key, shape, cuts, -0.22, 0.18)
    return jnp.clip(spiked(entries, jax.random.fold_in(stream_key, 3), *heavy), -most, most).astype(kind)


def setup_inputs(seed: int = 0) -> dict:
    key_of = jax.random.split(jax.random.key(seed), 8)
    positions = draw_positions(jax.random.fold_in(key_of[7], 71), 0)
    queries = draw_queries(jax.random.fold_in(key_of[7], 71), 0)
    keys = draw_keys(jax.random.fold_in(key_of[7], 71), 0)
    values = gaussian(key_of[3], (SLAB_TOKENS, KEY_VALUE_HEADS, HEAD_SIZE), 1.0, 6.0, ((0, 32), (1, 8)))
    out_weight = heavy_noise(key_of[4], (QUERY_HEADS * HEAD_SIZE, D), (QUERY_HEADS * HEAD_SIZE) ** -0.5, 0.1875, ((0, 8), (1, 32)), (0, 1, 32, 2.75))
    post_gain = jnp.clip(1.0 + 0.15 * jax.random.normal(key_of[5], (D,), jnp.float32), 0.25, 1.75)
    residual = gaussian(key_of[6], (SLAB_TOKENS, D), 1.0, 6.0, ((0, 32), (1, 8)))
    return dict(positions=positions, queries=queries, keys=keys, values=values, out_weight=out_weight, post_gain=post_gain, residual=residual)


EPS = 1e-06
SCALE = 168.0 ** (-0.5)

def rotate(x, positions):
    half = x.shape[-1] // 2
    inverse = 10000.0 ** (-2.0 * jnp.arange(half, dtype=jnp.float32) / x.shape[-1])
    angle = positions.astype(jnp.float32)[:, None] * inverse[None, :]
    cosine = jnp.concatenate([jnp.cos(angle), jnp.cos(angle)], -1)[:, None, :]
    sine = jnp.concatenate([jnp.sin(angle), jnp.sin(angle)], -1)[:, None, :]
    source = x.astype(jnp.float32)
    turned = jnp.concatenate([-source[..., half:], source[..., :half]], -1)
    return (source * cosine + turned * sine).astype(jnp.bfloat16)

def reference(positions, queries, keys, values, out_weight, post_gain, residual):
    q_rot = rotate(queries, positions)
    k_rot = rotate(keys, positions)
    query_groups = QUERY_HEADS // KEY_VALUE_HEADS
    padding_length = jnp.zeros((VISIBLE_SPAN, KEY_VALUE_HEADS, HEAD_SIZE), jnp.bfloat16)
    key_pad = jnp.concatenate([padding_length, k_rot], 0)
    value_pad = jnp.concatenate([padding_length, values], 0)
    block_length = min(512, SLAB_TOKENS)

    def attend(number):
        first = (number * block_length).astype(jnp.int32)
        query_tile_rows = lax.dynamic_slice_in_dim(q_rot, first, block_length, 0).astype(jnp.float32)
        query_tile_rows = query_tile_rows.reshape(block_length, KEY_VALUE_HEADS, query_groups, HEAD_SIZE)
        key_block = lax.dynamic_slice_in_dim(key_pad, first, block_length + VISIBLE_SPAN, 0).astype(jnp.float32)
        value_block = lax.dynamic_slice_in_dim(value_pad, first, block_length + VISIBLE_SPAN, 0).astype(jnp.float32)
        scores = jnp.einsum('qhgd,khd->hgqk', query_tile_rows, key_block) * SCALE
        query_index = jnp.arange(block_length, dtype=jnp.int32)
        key_index = jnp.arange(block_length + VISIBLE_SPAN, dtype=jnp.int32)
        gap = VISIBLE_SPAN + query_index[:, None] - key_index[None, :]
        token_of_key = first - VISIBLE_SPAN + key_index
        allowed = (gap >= 0) & (gap < VISIBLE_SPAN) & (token_of_key[None, :] >= 0)
        scores = jnp.where(allowed, scores, -1e+30)
        top = lax.optimization_barrier(jnp.max(scores, axis=-1, keepdims=True))
        weights = jnp.exp(scores - top)
        probs = (weights / lax.optimization_barrier(jnp.sum(weights, axis=-1, keepdims=True))).astype(jnp.bfloat16)
        context = jnp.einsum('hgqk,khd->qhgd', probs.astype(jnp.float32), value_block)
        return context.astype(jnp.bfloat16).reshape(block_length, QUERY_HEADS * HEAD_SIZE)
    context = lax.map(attend, jnp.arange(SLAB_TOKENS // block_length, dtype=jnp.int32)).reshape(SLAB_TOKENS, QUERY_HEADS * HEAD_SIZE)
    width = QUERY_HEADS * HEAD_SIZE // N_HEAD
    attended = jnp.zeros((SLAB_TOKENS, D), jnp.float32)
    for group in range(N_HEAD):
        partial_value = jnp.dot(context[:, group * width:(group + 1) * width], out_weight[group * width:(group + 1) * width], preferred_element_type=jnp.float32)
        attended = attended + partial_value.astype(jnp.bfloat16).astype(jnp.float32)
    mean_square = lax.optimization_barrier(jnp.mean(attended * attended, axis=1, keepdims=True))
    result = residual.astype(jnp.float32) + post_gain[None, :] * attended * lax.rsqrt(mean_square + EPS)
    return result.astype(jnp.bfloat16)
```

```python
import math

import jax
import jax.numpy as jnp
from jax import lax
from jax.experimental import pallas as pl
from jax.experimental.pallas import tpu as pltpu
from jax.sharding import PartitionSpec as P

D = 5376
HEAD_SIZE = 128
VISIBLE_SPAN = 1024
EPS = 1e-06
SCALE = 168.0 ** (-0.5)
LOG2E = math.log2(math.e)
ROWS = 512
KV = 2
GROUP = 2
N_SEQ = 32
N_HEAD = 8
FEATURES = D // N_HEAD
SHARD = D // N_SEQ
QB = 256
LOW = -1e30


def rotated(x, cosine, sine):
    x = x.astype(jnp.float32)
    return (x * cosine + pltpu.roll(x, 64, 1) * sine).astype(jnp.bfloat16)


def prepare_kernel(k_ref, v_ref, cos_ref, sin_ref, *out_refs):
    cosine = cos_ref[...]
    sine = sin_ref[...]
    for g in range(KV):
        out_refs[g][0] = rotated(k_ref[g], cosine, sine)
        out_refs[g][1] = v_ref[g]


def prepare(k, v, cosine, sine):
    shape = jax.ShapeDtypeStruct((2, ROWS, HEAD_SIZE), jnp.bfloat16)
    return pl.pallas_call(
        prepare_kernel,
        out_shape=[shape] * KV,
        name="rotate_keys",
    )(k, v, cosine, sine)


def dot_nt(a, b):
    return lax.dot_general(a, b, (((1,), (1,)), ((), ())), preferred_element_type=jnp.float32)


def attend_kernel(place_ref, q_ref, cos_ref, sin_ref, own_ref, prev_ref, far_ref, out_ref):
    place = place_ref[0]
    prev_bias = jnp.where(place >= 1, 0.0, LOW)
    far_bias = jnp.where(place >= 2, 0.0, LOW)
    c = SCALE * LOG2E
    cosine = cos_ref[...]
    sine = sin_ref[...]
    v_own = own_ref[1].T
    v_prev = prev_ref[1].T
    v_far = far_ref[1].T
    row = lax.broadcasted_iota(jnp.int32, (QB, QB), 0)
    col = lax.broadcasted_iota(jnp.int32, (QB, QB), 1)
    seen = row <= col
    blocks = ROWS // QB
    for n in range(GROUP):
        q_all = rotated(q_ref[:, n * HEAD_SIZE : (n + 1) * HEAD_SIZE], cosine, sine)
        for b in range(blocks):
            q = q_all[b * QB : (b + 1) * QB]
            lo, hi = b * QB, (b + 1) * QB
            prev = dot_nt(prev_ref[0], q)
            own = dot_nt(own_ref[0, 0:hi, :], q)
            far = dot_nt(far_ref[0, lo:ROWS, :], q)
            mixed = jnp.where(seen, own[lo:hi], far[0:QB] + far_bias)
            top = jnp.maximum(
                jnp.max(prev, axis=0, keepdims=True) + prev_bias,
                jnp.max(mixed, axis=0, keepdims=True),
            )
            if lo > 0:
                top = jnp.maximum(top, jnp.max(own[0:lo], axis=0, keepdims=True))
            if hi < ROWS:
                top = jnp.maximum(top, jnp.max(far[QB:], axis=0, keepdims=True) + far_bias)
            top = top * c
            p_prev = jnp.exp2(prev * c - (top - prev_bias))
            p_mixed = jnp.exp2(mixed * c - top)
            total = jnp.sum(p_prev, axis=0, keepdims=True) + jnp.sum(p_mixed, axis=0, keepdims=True)
            own_parts = [jnp.where(seen, p_mixed, 0.0).astype(jnp.bfloat16)]
            far_parts = [jnp.where(seen, 0.0, p_mixed).astype(jnp.bfloat16)]
            if lo > 0:
                p = jnp.exp2(own[0:lo] * c - top)
                total = total + jnp.sum(p, axis=0, keepdims=True)
                own_parts.insert(0, p.astype(jnp.bfloat16))
            if hi < ROWS:
                p = jnp.exp2(far[QB:] * c - (top - far_bias))
                total = total + jnp.sum(p, axis=0, keepdims=True)
                far_parts.append(p.astype(jnp.bfloat16))
            context = jnp.dot(v_prev, p_prev.astype(jnp.bfloat16), preferred_element_type=jnp.float32)
            context += jnp.dot(
                v_own[:, 0:hi], jnp.concatenate(own_parts, 0), preferred_element_type=jnp.float32
            )
            context += jnp.dot(
                v_far[:, lo:], jnp.concatenate(far_parts, 0), preferred_element_type=jnp.float32
            )
            out_ref[n * HEAD_SIZE : (n + 1) * HEAD_SIZE, lo:hi] = (context / total).astype(jnp.bfloat16)


def attend(g, place, q, cosine, sine, own, prev, far):
    whole = lambda *shape: pl.BlockSpec(shape, lambda _: (0,) * len(shape))
    width = GROUP * HEAD_SIZE
    kv = whole(2, ROWS, HEAD_SIZE)
    return pl.pallas_call(
        attend_kernel,
        grid=(1,),
        in_specs=[
            pl.BlockSpec(memory_space=pltpu.SMEM),
            pl.BlockSpec((ROWS, width), lambda _: (0, g)),
            whole(ROWS, HEAD_SIZE),
            whole(ROWS, HEAD_SIZE),
            kv,
            kv,
            kv,
        ],
        out_specs=whole(width, ROWS),
        out_shape=jax.ShapeDtypeStruct((width, ROWS), jnp.bfloat16),
        compiler_params=pltpu.CompilerParams(vmem_limit_bytes=32 * 1024 * 1024),
        name="attend",
    )(place, q, cosine, sine, own, prev, far)


def project_kernel(order_ref, w_ref, *refs):
    ctx_refs, (acc_ref, sq_ref) = refs[: KV * N_HEAD], refs[KV * N_HEAD :]
    step = pl.program_id(0)
    width = GROUP * HEAD_SIZE
    for k in range(N_HEAD):

        @pl.when(step == k)
        def _(k=k):
            value = sum(
                jnp.dot(
                    w_ref[0, :, g * width : (g + 1) * width],
                    ctx_refs[k * KV + g][...],
                    preferred_element_type=jnp.float32,
                )
                for g in range(KV)
            )
            if k > 0:
                value = acc_ref[...] + value
            acc_ref[...] = value
            if k == N_HEAD - 1:
                sq_ref[...] = jnp.sum(value * value, axis=0, keepdims=True)


def project(order, weights, blocks):
    width = GROUP * HEAD_SIZE
    return pl.pallas_call(
        project_kernel,
        grid_spec=pltpu.PrefetchScalarGridSpec(
            num_scalar_prefetch=1,
            grid=(N_HEAD,),
            in_specs=[pl.BlockSpec((1, FEATURES, KV * width), lambda k, order: (order[k], 0, 0))]
            + [pl.BlockSpec((width, ROWS), lambda k, order: (0, 0))] * (KV * N_HEAD),
            out_specs=[
                pl.BlockSpec((FEATURES, ROWS), lambda k, order: (0, 0)),
                pl.BlockSpec((1, ROWS), lambda k, order: (0, 0)),
            ],
        ),
        out_shape=[
            jax.ShapeDtypeStruct((FEATURES, ROWS), jnp.float32),
            jax.ShapeDtypeStruct((1, ROWS), jnp.float32),
        ],
        compiler_params=pltpu.CompilerParams(vmem_limit_bytes=40 * 1024 * 1024),
        name="project",
    )(order, weights, *blocks)


def of_everyone(array, axis):
    length = lax.axis_size(axis)
    return lax.all_to_all(
        jnp.broadcast_to(array[None], (length, *array.shape)), axis, 0, 0, tiled=True
    ).sum(axis=0)


def on_device(positions, queries, keys, values, out_weight, post_gain, residual):
    seq = lax.axis_index("seq")
    head = lax.axis_index("head")
    spread = [
        (s * N_HEAD + h, (h * 4 + s % 4) * N_HEAD + s // 4)
        for s in range(N_SEQ)
        for h in range(N_HEAD)
    ]
    shard = lax.ppermute(out_weight.T, ("seq", "head"), spread)
    weights = lax.all_gather(shard, "seq", axis=0).reshape(N_HEAD, FEATURES, KV * GROUP * HEAD_SIZE)

    half = HEAD_SIZE // 2
    inverse = 10000.0 ** (-2.0 * jnp.arange(half, dtype=jnp.float32) / HEAD_SIZE)
    angle = positions.astype(jnp.float32)[:, None] * inverse[None, :]
    cosine, sine = jnp.cos(angle), jnp.sin(angle)
    cosine = jnp.concatenate([cosine, cosine], -1)
    sine = jnp.concatenate([-sine, sine], -1)

    own = prepare(keys.transpose(1, 0, 2), values.transpose(1, 0, 2), cosine, sine)
    onward = [(i, i + 1) for i in range(N_SEQ - 1)]
    prev = [lax.ppermute(x, "seq", onward) for x in own]
    far = [lax.ppermute(x, "seq", onward) for x in prev]
    place = seq.astype(jnp.int32).reshape(1)
    q = queries.reshape(ROWS, KV * GROUP * HEAD_SIZE)

    ring = [
        (s * N_HEAD + h, s * N_HEAD + (h + (1 if s % 2 == 0 else -1)) % N_HEAD)
        for s in range(N_SEQ)
        for h in range(N_HEAD)
    ]
    blocks = [[None] * KV for _ in range(N_HEAD)]
    for g in range(KV):
        carried = attend(g, place, q, cosine, sine, own[g], prev[g], far[g])
        blocks[0][g] = carried
        for k in range(1, N_HEAD):
            carried = lax.ppermute(carried, ("seq", "head"), ring)
            blocks[k][g] = carried
    sign = jnp.where(seq % 2 == 0, -1, 1)
    order = ((head + sign * jnp.arange(N_HEAD, dtype=jnp.int32)) % N_HEAD).astype(jnp.int32)
    attended, squares = project(order, weights, [x for pair in blocks for x in pair])
    squares = of_everyone(squares, "head")
    scaled = attended * lax.rsqrt(squares / D + EPS)
    result = residual.T.astype(jnp.float32) + post_gain[:, None] * scaled
    return result.astype(jnp.bfloat16).T


def solution(mesh):
    return jax.shard_map(
        on_device,
        mesh=mesh,
        in_specs=(
            P("seq"),
            P("seq", "head", None),
            P("seq", "head", None),
            P("seq", "head", None),
            P("head", "seq"),
            P("head"),
            P("seq", "head"),
        ),
        out_specs=P("seq", "head"),
        check_vma=False,
    )
```

```python
import math

import jax
import jax.numpy as jnp
from jax import lax
from jax.experimental import pallas as pl
from jax.experimental.pallas import tpu as pltpu
from jax.sharding import PartitionSpec as P

D = 5376
HEAD_SIZE = 128
VISIBLE_SPAN = 1024
EPS = 1e-06
SCALE = 168.0 ** (-0.5)
LOG2E = math.log2(math.e)
ROWS = 512
KV = 2
GROUP = 2
N_SEQ = 32
N_HEAD = 8
FEATURES = D // N_HEAD
SHARD = D // N_SEQ
QB = 256
LOW = -1e30


def rotated(x, cosine, sine):
    x = x.astype(jnp.float32)
    return (x * cosine + pltpu.roll(x, 64, 1) * sine).astype(jnp.bfloat16)


def twice(x, sign):
    return jnp.concatenate([sign * x, x], -1)


def dot_nt(a, b):
    return lax.dot_general(a, b, (((1,), (1,)), ((), ())), preferred_element_type=jnp.float32)


def attend_kernel(place_ref, q_ref, cos_ref, sin_ref, own_ref, prev_ref, far_ref, out_ref):
    place = place_ref[0]
    prev_bias = jnp.where(place >= 1, 0.0, LOW)
    far_bias = jnp.where(place >= 2, 0.0, LOW)
    c = SCALE * LOG2E
    cosine = twice(cos_ref[0], 1.0)
    sine = twice(sin_ref[0], -1.0)
    k_own = rotated(own_ref[0], cosine, sine)
    k_prev = rotated(prev_ref[0], twice(cos_ref[1], 1.0), twice(sin_ref[1], -1.0))
    k_far = rotated(far_ref[0], twice(cos_ref[2], 1.0), twice(sin_ref[2], -1.0))
    v_own = own_ref[1].T
    v_prev = prev_ref[1].T
    v_far = far_ref[1].T
    row = lax.broadcasted_iota(jnp.int32, (QB, QB), 0)
    col = lax.broadcasted_iota(jnp.int32, (QB, QB), 1)
    seen = row <= col
    blocks = ROWS // QB
    for n in range(GROUP):
        q_all = rotated(q_ref[:, n * HEAD_SIZE : (n + 1) * HEAD_SIZE], cosine, sine)
        for b in range(blocks):
            q = q_all[b * QB : (b + 1) * QB]
            lo, hi = b * QB, (b + 1) * QB
            prev = dot_nt(k_prev, q)
            own = dot_nt(k_own[0:hi], q)
            far = dot_nt(k_far[lo:ROWS], q)
            mixed = jnp.where(seen, own[lo:hi], far[0:QB] + far_bias)
            top = jnp.maximum(
                jnp.max(prev, axis=0, keepdims=True) + prev_bias,
                jnp.max(mixed, axis=0, keepdims=True),
            )
            if lo > 0:
                top = jnp.maximum(top, jnp.max(own[0:lo], axis=0, keepdims=True))
            if hi < ROWS:
                top = jnp.maximum(top, jnp.max(far[QB:], axis=0, keepdims=True) + far_bias)
            top = top * c
            p_prev = jnp.exp2(prev * c - (top - prev_bias))
            p_mixed = jnp.exp2(mixed * c - top)
            total = jnp.sum(p_prev, axis=0, keepdims=True) + jnp.sum(p_mixed, axis=0, keepdims=True)
            own_parts = [jnp.where(seen, p_mixed, 0.0).astype(jnp.bfloat16)]
            far_parts = [jnp.where(seen, 0.0, p_mixed).astype(jnp.bfloat16)]
            if lo > 0:
                p = jnp.exp2(own[0:lo] * c - top)
                total = total + jnp.sum(p, axis=0, keepdims=True)
                own_parts.insert(0, p.astype(jnp.bfloat16))
            if hi < ROWS:
                p = jnp.exp2(far[QB:] * c - (top - far_bias))
                total = total + jnp.sum(p, axis=0, keepdims=True)
                far_parts.append(p.astype(jnp.bfloat16))
            context = jnp.dot(v_prev, p_prev.astype(jnp.bfloat16), preferred_element_type=jnp.float32)
            context += jnp.dot(
                v_own[:, 0:hi], jnp.concatenate(own_parts, 0), preferred_element_type=jnp.float32
            )
            context += jnp.dot(
                v_far[:, lo:], jnp.concatenate(far_parts, 0), preferred_element_type=jnp.float32
            )
            out_ref[n * HEAD_SIZE : (n + 1) * HEAD_SIZE, lo:hi] = (context / total).astype(jnp.bfloat16)


def attend(g, place, q, cosine, sine, own, prev, far):
    whole = lambda *shape: pl.BlockSpec(shape, lambda _: (0,) * len(shape))
    width = GROUP * HEAD_SIZE
    kv = whole(2, ROWS, HEAD_SIZE)
    return pl.pallas_call(
        attend_kernel,
        grid=(1,),
        in_specs=[
            pl.BlockSpec(memory_space=pltpu.SMEM),
            pl.BlockSpec((ROWS, width), lambda _: (0, g)),
            whole(3, ROWS, HEAD_SIZE // 2),
            whole(3, ROWS, HEAD_SIZE // 2),
            kv,
            kv,
            kv,
        ],
        out_specs=whole(width, ROWS),
        out_shape=jax.ShapeDtypeStruct((width, ROWS), jnp.bfloat16),
        compiler_params=pltpu.CompilerParams(vmem_limit_bytes=24 * 1024 * 1024),
        name="attend",
    )(place, q, cosine, sine, own, prev, far)


def project_kernel(order_ref, w_ref, *refs):
    ctx_refs = refs[: KV * N_HEAD]
    acc_ref, sq_ref, buffer, arrived = refs[KV * N_HEAD :]
    width = GROUP * HEAD_SIZE
    copies = [
        pltpu.make_async_copy(w_ref.at[order_ref[k]], buffer.at[k], arrived.at[k])
        for k in range(N_HEAD)
    ]
    for copy in copies:
        copy.start()
    for k in range(N_HEAD):
        copies[k].wait()
        value = sum(
            jnp.dot(
                buffer[k, :, g * width : (g + 1) * width],
                ctx_refs[k * KV + g][...],
                preferred_element_type=jnp.float32,
            )
            for g in range(KV)
        )
        if k > 0:
            value = acc_ref[...] + value
        acc_ref[...] = value
        if k == N_HEAD - 1:
            sq_ref[...] = jnp.sum(value * value, axis=0, keepdims=True)


def project(order, weights, blocks):
    width = GROUP * HEAD_SIZE
    vmem = pl.BlockSpec(memory_space=pltpu.VMEM)
    return pl.pallas_call(
        project_kernel,
        in_specs=[pl.BlockSpec(memory_space=pltpu.SMEM), pl.BlockSpec(memory_space=pltpu.HBM)]
        + [vmem] * (KV * N_HEAD),
        out_specs=[vmem, vmem],
        out_shape=[
            jax.ShapeDtypeStruct((FEATURES, ROWS), jnp.float32),
            jax.ShapeDtypeStruct((1, ROWS), jnp.float32),
        ],
        scratch_shapes=[
            pltpu.VMEM((N_HEAD, FEATURES, KV * width), jnp.bfloat16),
            pltpu.SemaphoreType.DMA((N_HEAD,)),
        ],
        compiler_params=pltpu.CompilerParams(vmem_limit_bytes=16 * 1024 * 1024),
        name="project",
    )(order, weights, *blocks)


def finish_kernel(acc_ref, sq_ref, gain_ref, res_ref, out_ref):
    squares = jnp.sum(sq_ref[...], axis=0)
    scale = lax.rsqrt(squares / D + EPS)
    value = res_ref[...].astype(jnp.float32) + gain_ref[...] * (acc_ref[...] * scale)
    out_ref[...] = value.astype(jnp.bfloat16)


def finish(attended, squares, gain, residual):
    return pl.pallas_call(
        finish_kernel,
        out_shape=jax.ShapeDtypeStruct((FEATURES, ROWS), jnp.bfloat16),
        compiler_params=pltpu.CompilerParams(vmem_limit_bytes=12 * 1024 * 1024),
        name="finish",
    )(attended, squares, gain, residual)


def for_everyone(array, axis):
    length = lax.axis_size(axis)
    return lax.all_to_all(
        jnp.broadcast_to(array[None], (length, *array.shape)), axis, 0, 0, tiled=True
    )


def on_device(positions, queries, keys, values, out_weight, post_gain, residual):
    seq = lax.axis_index("seq")
    head = lax.axis_index("head")
    spread = [
        (s * N_HEAD + h, ((s // 4 + h) % N_HEAD * 4 + s % 4) * N_HEAD + s // 4)
        for s in range(N_SEQ)
        for h in range(N_HEAD)
    ]
    shard = lax.ppermute(out_weight.T, ("seq", "head"), spread)

    onward = [(i, i + 1) for i in range(N_SEQ - 1)]
    beyond = [(i, i + 2) for i in range(N_SEQ - 2)]
    places = jnp.stack(
        [positions, lax.ppermute(positions, "seq", onward), lax.ppermute(positions, "seq", beyond)]
    )
    own = [jnp.stack([keys[:, g], values[:, g]]) for g in range(KV)]
    prev = [lax.ppermute(x, "seq", onward) for x in own]
    far = [lax.ppermute(x, "seq", onward) for x in prev]
    weights = lax.all_gather(shard, "seq", axis=0).reshape(N_HEAD, FEATURES, KV * GROUP * HEAD_SIZE)

    half = HEAD_SIZE // 2
    inverse = 10000.0 ** (-2.0 * jnp.arange(half, dtype=jnp.float32) / HEAD_SIZE)
    angle = places.astype(jnp.float32)[:, :, None] * inverse[None, None, :]
    cosine, sine = jnp.cos(angle), jnp.sin(angle)
    place = seq.astype(jnp.int32).reshape(1)
    q = queries.reshape(ROWS, KV * GROUP * HEAD_SIZE)

    ring = [
        (s * N_HEAD + h, s * N_HEAD + (h + (1 if s % 2 == 0 else -1)) % N_HEAD)
        for s in range(N_SEQ)
        for h in range(N_HEAD)
    ]
    blocks = [[None] * KV for _ in range(N_HEAD)]
    for g in range(KV):
        carried = attend(g, place, q, cosine, sine, own[g], prev[g], far[g])
        blocks[0][g] = carried
        for k in range(1, N_HEAD):
            carried = lax.ppermute(carried, ("seq", "head"), ring)
            blocks[k][g] = carried
    sign = jnp.where(seq % 2 == 0, -1, 1)
    source = head + sign * jnp.arange(N_HEAD, dtype=jnp.int32)
    order = ((source + head) % N_HEAD).astype(jnp.int32)
    attended, squares = project(order, weights, [x for pair in blocks for x in pair])
    squares = for_everyone(squares, "head")
    return finish(attended, squares, post_gain[:, None], residual.T).T


def solution(mesh):
    return jax.shard_map(
        on_device,
        mesh=mesh,
        in_specs=(
            P("seq"),
            P("seq", "head", None),
            P("seq", "head", None),
            P("seq", "head", None),
            P("head", "seq"),
            P("head"),
            P("seq", "head"),
        ),
        out_specs=P("seq", "head"),
        check_vma=False,
    )
```

```python
import math

import jax
import jax.numpy as jnp
from jax import lax
from jax.experimental import pallas as pl
from jax.experimental.pallas import tpu as pltpu
from jax.sharding import PartitionSpec as P

D = 5376
HEAD_SIZE = 128
VISIBLE_SPAN = 1024
EPS = 1e-06
SCALE = 168.0 ** (-0.5)
LOG2E = math.log2(math.e)
ROWS = 512
KV = 2
GROUP = 2
N_SEQ = 32
N_HEAD = 8
FEATURES = D // N_HEAD
SHARD = D // N_SEQ
QB = 256
LOW = -1e30


def rotated(x, cosine, sine):
    x = x.astype(jnp.float32)
    return (x * cosine + pltpu.roll(x, 64, 1) * sine).astype(jnp.bfloat16)


def twice(x, sign):
    return jnp.concatenate([sign * x, x], -1)


def dot_nt(a, b):
    return lax.dot_general(a, b, (((1,), (1,)), ((), ())), preferred_element_type=jnp.float32)


def hold_kernel(first_ref, *refs):
    pass


def held(array, *others):
    hbm = pl.BlockSpec(memory_space=pl.ANY)
    return pl.pallas_call(
        hold_kernel,
        in_specs=[hbm] * (1 + len(others)),
        out_specs=hbm,
        out_shape=jax.ShapeDtypeStruct(array.shape, array.dtype),
        input_output_aliases={0: 0},
        name="hold",
    )(array, *others)


def attend_kernel(place_ref, q_ref, cos_ref, sin_ref, own_ref, prev_ref, far_ref, out_ref):
    place = place_ref[0]
    prev_bias = jnp.where(place >= 1, 0.0, LOW)
    far_bias = jnp.where(place >= 2, 0.0, LOW)
    c = SCALE * LOG2E
    cosine = twice(cos_ref[0], 1.0)
    sine = twice(sin_ref[0], -1.0)
    k_own = rotated(own_ref[0], cosine, sine)
    k_prev = rotated(prev_ref[0], twice(cos_ref[1], 1.0), twice(sin_ref[1], -1.0))
    k_far = rotated(far_ref[0], twice(cos_ref[2], 1.0), twice(sin_ref[2], -1.0))
    v_own = own_ref[1].T
    v_prev = prev_ref[1].T
    v_far = far_ref[1].T
    row = lax.broadcasted_iota(jnp.int32, (QB, QB), 0)
    col = lax.broadcasted_iota(jnp.int32, (QB, QB), 1)
    seen = row <= col
    blocks = ROWS // QB
    for n in range(GROUP):
        q_all = rotated(q_ref[:, n * HEAD_SIZE : (n + 1) * HEAD_SIZE], cosine, sine)
        for b in range(blocks):
            q = q_all[b * QB : (b + 1) * QB]
            lo, hi = b * QB, (b + 1) * QB
            prev = dot_nt(k_prev, q)
            own = dot_nt(k_own[0:hi], q)
            far = dot_nt(k_far[lo:ROWS], q)
            mixed = jnp.where(seen, own[lo:hi], far[0:QB] + far_bias)
            top = jnp.maximum(
                jnp.max(prev, axis=0, keepdims=True) + prev_bias,
                jnp.max(mixed, axis=0, keepdims=True),
            )
            if lo > 0:
                top = jnp.maximum(top, jnp.max(own[0:lo], axis=0, keepdims=True))
            if hi < ROWS:
                top = jnp.maximum(top, jnp.max(far[QB:], axis=0, keepdims=True) + far_bias)
            top = top * c
            p_prev = jnp.exp2(prev * c - (top - prev_bias))
            p_mixed = jnp.exp2(mixed * c - top)
            total = jnp.sum(p_prev, axis=0, keepdims=True) + jnp.sum(p_mixed, axis=0, keepdims=True)
            own_parts = [jnp.where(seen, p_mixed, 0.0).astype(jnp.bfloat16)]
            far_parts = [jnp.where(seen, 0.0, p_mixed).astype(jnp.bfloat16)]
            if lo > 0:
                p = jnp.exp2(own[0:lo] * c - top)
                total = total + jnp.sum(p, axis=0, keepdims=True)
                own_parts.insert(0, p.astype(jnp.bfloat16))
            if hi < ROWS:
                p = jnp.exp2(far[QB:] * c - (top - far_bias))
                total = total + jnp.sum(p, axis=0, keepdims=True)
                far_parts.append(p.astype(jnp.bfloat16))
            context = jnp.dot(v_prev, p_prev.astype(jnp.bfloat16), preferred_element_type=jnp.float32)
            context += jnp.dot(
                v_own[:, 0:hi], jnp.concatenate(own_parts, 0), preferred_element_type=jnp.float32
            )
            context += jnp.dot(
                v_far[:, lo:], jnp.concatenate(far_parts, 0), preferred_element_type=jnp.float32
            )
            out_ref[n * HEAD_SIZE : (n + 1) * HEAD_SIZE, lo:hi] = (context / total).astype(jnp.bfloat16)


def attend(g, place, q, cosine, sine, own, prev, far):
    whole = lambda *shape: pl.BlockSpec(shape, lambda _: (0,) * len(shape))
    width = GROUP * HEAD_SIZE
    kv = whole(2, ROWS, HEAD_SIZE)
    return pl.pallas_call(
        attend_kernel,
        grid=(1,),
        in_specs=[
            pl.BlockSpec(memory_space=pltpu.SMEM),
            pl.BlockSpec((ROWS, width), lambda _: (0, g)),
            whole(3, ROWS, HEAD_SIZE // 2),
            whole(3, ROWS, HEAD_SIZE // 2),
            kv,
            kv,
            kv,
        ],
        out_specs=whole(width, ROWS),
        out_shape=jax.ShapeDtypeStruct((width, ROWS), jnp.bfloat16),
        compiler_params=pltpu.CompilerParams(vmem_limit_bytes=24 * 1024 * 1024),
        name="attend",
    )(place, q, cosine, sine, own, prev, far)


def project_kernel(order_ref, w_ref, *refs):
    ctx_refs = refs[: KV * N_HEAD]
    acc_ref, sq_ref, w_buffer, ctx_buffer, arrived = refs[KV * N_HEAD :]
    width = GROUP * HEAD_SIZE
    copies = []
    for k in range(N_HEAD):
        copies.append(
            [pltpu.make_async_copy(w_ref.at[order_ref[k]], w_buffer.at[k], arrived.at[k, KV])]
            + [
                pltpu.make_async_copy(
                    ctx_refs[k * KV + g],
                    ctx_buffer.at[k, g * width : (g + 1) * width],
                    arrived.at[k, g],
                )
                for g in range(KV)
            ]
        )
        for copy in copies[k]:
            copy.start()
    for k in range(N_HEAD):
        for copy in copies[k]:
            copy.wait()
        value = jnp.dot(w_buffer[k], ctx_buffer[k], preferred_element_type=jnp.float32)
        if k > 0:
            value = acc_ref[...] + value
        acc_ref[...] = value
        if k == N_HEAD - 1:
            sq_ref[...] = jnp.sum(value * value, axis=0, keepdims=True)


def project(order, weights, blocks):
    width = KV * GROUP * HEAD_SIZE
    vmem = pl.BlockSpec(memory_space=pltpu.VMEM)
    hbm = pl.BlockSpec(memory_space=pltpu.HBM)
    weights = pltpu.with_memory_space_constraint(weights, pltpu.HBM)
    blocks = [pltpu.with_memory_space_constraint(x, pltpu.HBM) for x in blocks]
    return pl.pallas_call(
        project_kernel,
        in_specs=[pl.BlockSpec(memory_space=pltpu.SMEM), hbm] + [hbm] * (KV * N_HEAD),
        out_specs=[vmem, vmem],
        out_shape=[
            jax.ShapeDtypeStruct((FEATURES, ROWS), jnp.float32),
            jax.ShapeDtypeStruct((1, ROWS), jnp.float32),
        ],
        scratch_shapes=[
            pltpu.VMEM((N_HEAD, FEATURES, width), jnp.bfloat16),
            pltpu.VMEM((N_HEAD, width, ROWS), jnp.bfloat16),
            pltpu.SemaphoreType.DMA((N_HEAD, KV + 1)),
        ],
        compiler_params=pltpu.CompilerParams(vmem_limit_bytes=24 * 1024 * 1024),
        name="project",
    )(order, weights, *blocks)


def finish_kernel(acc_ref, sq_ref, gain_ref, res_ref, out_ref):
    squares = jnp.sum(sq_ref[...], axis=0)
    scale = lax.rsqrt(squares / D + EPS)
    value = res_ref[...].astype(jnp.float32) + gain_ref[...] * (acc_ref[...] * scale)
    out_ref[...] = value.astype(jnp.bfloat16)


def finish(attended, squares, gain, residual):
    return pl.pallas_call(
        finish_kernel,
        out_shape=jax.ShapeDtypeStruct((FEATURES, ROWS), jnp.bfloat16),
        compiler_params=pltpu.CompilerParams(vmem_limit_bytes=12 * 1024 * 1024),
        name="finish",
    )(attended, squares, gain, residual)


def for_everyone(array, axis):
    length = lax.axis_size(axis)
    return lax.all_to_all(
        jnp.broadcast_to(array[None], (length, *array.shape)), axis, 0, 0, tiled=True
    )


def on_device(positions, queries, keys, values, out_weight, post_gain, residual):
    seq = lax.axis_index("seq")
    head = lax.axis_index("head")
    spread = [
        (s * N_HEAD + h, ((s // 4 + h) % N_HEAD * 4 + s % 4) * N_HEAD + s // 4)
        for s in range(N_SEQ)
        for h in range(N_HEAD)
    ]
    shard = lax.ppermute(out_weight.T, ("seq", "head"), spread)

    onward = [(i, i + 1) for i in range(N_SEQ - 1)]
    beyond = [(i, i + 2) for i in range(N_SEQ - 2)]
    places = jnp.stack(
        [positions, lax.ppermute(positions, "seq", onward), lax.ppermute(positions, "seq", beyond)]
    )
    own = [jnp.stack([keys[:, g], values[:, g]]) for g in range(KV)]
    prev = [lax.ppermute(x, "seq", onward) for x in own]
    far = [lax.ppermute(x, "seq", onward) for x in prev]
    shard = held(shard, *prev)
    weights = lax.all_gather(shard, "seq", axis=0).reshape(N_HEAD, FEATURES, KV * GROUP * HEAD_SIZE)

    half = HEAD_SIZE // 2
    inverse = 10000.0 ** (-2.0 * jnp.arange(half, dtype=jnp.float32) / HEAD_SIZE)
    angle = places.astype(jnp.float32)[:, :, None] * inverse[None, None, :]
    cosine, sine = jnp.cos(angle), jnp.sin(angle)
    place = seq.astype(jnp.int32).reshape(1)
    q = queries.reshape(ROWS, KV * GROUP * HEAD_SIZE)

    ring = [
        (s * N_HEAD + h, s * N_HEAD + (h + (1 if s % 2 == 0 else -1)) % N_HEAD)
        for s in range(N_SEQ)
        for h in range(N_HEAD)
    ]
    blocks = [[None] * KV for _ in range(N_HEAD)]
    for g in range(KV):
        carried = attend(g, place, q, cosine, sine, own[g], prev[g], far[g])
        blocks[0][g] = carried
        for k in range(1, N_HEAD):
            carried = lax.ppermute(carried, ("seq", "head"), ring)
            blocks[k][g] = carried
    sign = jnp.where(seq % 2 == 0, -1, 1)
    source = head + sign * jnp.arange(N_HEAD, dtype=jnp.int32)
    order = ((source + head) % N_HEAD).astype(jnp.int32)
    attended, squares = project(order, weights, [x for pair in blocks for x in pair])
    squares = for_everyone(squares, "head")
    return finish(attended, squares, post_gain[:, None], residual.T).T


def solution(mesh):
    return jax.shard_map(
        on_device,
        mesh=mesh,
        in_specs=(
            P("seq"),
            P("seq", "head", None),
            P("seq", "head", None),
            P("seq", "head", None),
            P("head", "seq"),
            P("head"),
            P("seq", "head"),
        ),
        out_specs=P("seq", "head"),
        check_vma=False,
    )
```

```python
import functools
import math

import jax
import jax.numpy as jnp
from jax import lax
from jax.experimental import pallas as pl
from jax.experimental.pallas import tpu as pltpu
from jax.sharding import PartitionSpec as P

D = 5376
HEAD_SIZE = 128
VISIBLE_SPAN = 1024
EPS = 1e-06
SCALE = 168.0 ** (-0.5)
LOG2E = math.log2(math.e)
ROWS = 512
KV = 2
GROUP = 2
N_SEQ = 32
N_HEAD = 8
FEATURES = D // N_HEAD
SHARD = D // N_SEQ
QB = 256
WIDTH = KV * GROUP * HEAD_SIZE
PIECE = 128
PIECES = WIDTH // PIECE
LOW = -1e30
VMEM = pl.BlockSpec(memory_space=pltpu.VMEM)


def cos_and_sin(angle):
    turns = jnp.floor(angle * (2.0 / math.pi) + 0.5)
    x = angle - turns * 1.5703125
    x = x - turns * 4.8351287841796875e-4
    x = x - turns * 3.1385570764541626e-07
    x = x - turns * 6.0771005065061922e-11
    z = x * x
    sine = ((-1.9515295891e-4 * z + 8.3321608736e-3) * z - 1.6666654611e-1) * z * x + x
    cosine = ((2.443315711809948e-5 * z - 1.388731625493765e-3) * z + 4.166664568298827e-2) * z * z
    cosine = cosine - 0.5 * z + 1.0
    quadrant = turns.astype(jnp.int32) & 3
    odd = (quadrant & 1) == 1
    first = jnp.where(odd, sine, cosine)
    second = jnp.where(odd, cosine, sine)
    first = jnp.where((quadrant == 1) | (quadrant == 2), -first, first)
    second = jnp.where(quadrant >= 2, -second, second)
    return first, second


def rotated(x, cosine, sine):
    x = x.astype(jnp.float32)
    return (x * cosine + pltpu.roll(x, 64, 1) * sine).astype(jnp.bfloat16)


def prepare_kernel(pos_ref, inverse_ref, k_ref, v_ref, kv_ref, cos_ref, sin_ref):
    place = jnp.broadcast_to(pos_ref[...].astype(jnp.float32), (HEAD_SIZE, ROWS)).T
    cosine, sine = cos_and_sin(place * inverse_ref[...])
    lane = lax.broadcasted_iota(jnp.int32, (ROWS, HEAD_SIZE), 1)
    sine = jnp.where(lane < HEAD_SIZE // 2, -sine, sine)
    cos_ref[...] = cosine
    sin_ref[...] = sine
    for g in range(KV):
        kv_ref[g, 0] = rotated(k_ref[g], cosine, sine)
        kv_ref[g, 1] = v_ref[g]


def prepare(positions, inverse, k, v):
    payload = jax.ShapeDtypeStruct((KV, 2, ROWS, HEAD_SIZE), jnp.bfloat16)
    table = jax.ShapeDtypeStruct((ROWS, HEAD_SIZE), jnp.float32)
    return pl.pallas_call(
        prepare_kernel,
        in_specs=[VMEM] * 4,
        out_specs=[VMEM] * 3,
        out_shape=[payload, table, table],
        compiler_params=pltpu.CompilerParams(vmem_limit_bytes=8 * 1024 * 1024),
        name="prepare",
    )(positions, inverse, k, v)


def dot_nt(a, b):
    return lax.dot_general(a, b, (((1,), (1,)), ((), ())), preferred_element_type=jnp.float32)


def hold_kernel(first_ref, *refs):
    pass


def held(array, *others):
    hbm = pl.BlockSpec(memory_space=pltpu.HBM)
    others = [pltpu.with_memory_space_constraint(x, pltpu.VMEM) for x in others]
    return pl.pallas_call(
        hold_kernel,
        in_specs=[hbm] + [VMEM] * len(others),
        out_specs=hbm,
        out_shape=jax.ShapeDtypeStruct(array.shape, array.dtype),
        input_output_aliases={0: 0},
        compiler_params=pltpu.CompilerParams(vmem_limit_bytes=1024 * 1024),
        name="hold",
    )(array, *others)


def attend_kernel(g, place_ref, q_ref, cos_ref, sin_ref, own_ref, prev_ref, far_ref, *out_refs):
    place = place_ref[0]
    prev_bias = jnp.where(place >= 1, 0.0, LOW)
    far_bias = jnp.where(place >= 2, 0.0, LOW)
    c = SCALE * LOG2E
    cosine = cos_ref[...]
    sine = sin_ref[...]
    k_own, k_prev, k_far = own_ref[g, 0], prev_ref[g, 0], far_ref[g, 0]
    v_own = own_ref[g, 1].T
    v_prev = prev_ref[g, 1].T
    v_far = far_ref[g, 1].T
    row = lax.broadcasted_iota(jnp.int32, (QB, QB), 0)
    col = lax.broadcasted_iota(jnp.int32, (QB, QB), 1)
    seen = row <= col
    blocks = ROWS // QB
    for n in range(GROUP):
        head = g * GROUP + n
        q_all = rotated(q_ref[:, head * HEAD_SIZE : (head + 1) * HEAD_SIZE], cosine, sine)
        for b in range(blocks):
            q = q_all[b * QB : (b + 1) * QB]
            lo, hi = b * QB, (b + 1) * QB
            prev = dot_nt(k_prev, q)
            own = dot_nt(k_own[0:hi], q)
            far = dot_nt(k_far[lo:ROWS], q)
            mixed = jnp.where(seen, own[lo:hi], far[0:QB] + far_bias)
            top = jnp.maximum(
                jnp.max(prev, axis=0, keepdims=True) + prev_bias,
                jnp.max(mixed, axis=0, keepdims=True),
            )
            if lo > 0:
                top = jnp.maximum(top, jnp.max(own[0:lo], axis=0, keepdims=True))
            if hi < ROWS:
                top = jnp.maximum(top, jnp.max(far[QB:], axis=0, keepdims=True) + far_bias)
            top = top * c
            p_prev = jnp.exp2(prev * c - (top - prev_bias))
            p_mixed = jnp.exp2(mixed * c - top)
            total = jnp.sum(p_prev, axis=0, keepdims=True) + jnp.sum(p_mixed, axis=0, keepdims=True)
            own_parts = [jnp.where(seen, p_mixed, 0.0).astype(jnp.bfloat16)]
            far_parts = [jnp.where(seen, 0.0, p_mixed).astype(jnp.bfloat16)]
            if lo > 0:
                p = jnp.exp2(own[0:lo] * c - top)
                total = total + jnp.sum(p, axis=0, keepdims=True)
                own_parts.insert(0, p.astype(jnp.bfloat16))
            if hi < ROWS:
                p = jnp.exp2(far[QB:] * c - (top - far_bias))
                total = total + jnp.sum(p, axis=0, keepdims=True)
                far_parts.append(p.astype(jnp.bfloat16))
            context = jnp.dot(v_prev, p_prev.astype(jnp.bfloat16), preferred_element_type=jnp.float32)
            context += jnp.dot(
                v_own[:, 0:hi], jnp.concatenate(own_parts, 0), preferred_element_type=jnp.float32
            )
            context += jnp.dot(
                v_far[:, lo:], jnp.concatenate(far_parts, 0), preferred_element_type=jnp.float32
            )
            first = n * HEAD_SIZE % PIECE
            out_refs[n * HEAD_SIZE // PIECE][first : first + HEAD_SIZE, lo:hi] = (
                context / total
            ).astype(jnp.bfloat16)


def attend(g, place, *arrays):
    width = GROUP * HEAD_SIZE
    arrays = [pltpu.with_memory_space_constraint(x, pltpu.VMEM) for x in arrays]
    return pl.pallas_call(
        functools.partial(attend_kernel, g),
        in_specs=[pl.BlockSpec(memory_space=pltpu.SMEM)] + [VMEM] * len(arrays),
        out_specs=[VMEM] * (width // PIECE),
        out_shape=[jax.ShapeDtypeStruct((PIECE, ROWS), jnp.bfloat16)] * (width // PIECE),
        compiler_params=pltpu.CompilerParams(vmem_limit_bytes=20 * 1024 * 1024),
        name="attend",
    )(place, *arrays)


def project_kernel(order_ref, w_ref, *refs):
    ctx_refs = refs[: PIECES * N_HEAD]
    acc_ref, sq_ref, w_buffer, ctx_buffer, arrived = refs[PIECES * N_HEAD :]
    copies = []
    for k in range(N_HEAD):
        copies.append(
            [pltpu.make_async_copy(w_ref.at[order_ref[k]], w_buffer.at[k], arrived.at[k, PIECES])]
            + [
                pltpu.make_async_copy(
                    ctx_refs[k * PIECES + g],
                    ctx_buffer.at[k, g * PIECE : (g + 1) * PIECE],
                    arrived.at[k, g],
                )
                for g in range(PIECES)
            ]
        )
        for copy in copies[k]:
            copy.start()
    for k in range(N_HEAD):
        for copy in copies[k]:
            copy.wait()
        value = jnp.dot(w_buffer[k], ctx_buffer[k], preferred_element_type=jnp.float32)
        if k > 0:
            value = acc_ref[...] + value
        acc_ref[...] = value
        if k == N_HEAD - 1:
            sq_ref[...] = jnp.sum(value * value, axis=0, keepdims=True)


def project(order, weights, blocks):
    hbm = pl.BlockSpec(memory_space=pltpu.HBM)
    weights = pltpu.with_memory_space_constraint(weights, pltpu.HBM)
    blocks = [pltpu.with_memory_space_constraint(x, pltpu.HBM) for x in blocks]
    return pl.pallas_call(
        project_kernel,
        in_specs=[pl.BlockSpec(memory_space=pltpu.SMEM), hbm] + [hbm] * (PIECES * N_HEAD),
        out_specs=[VMEM, VMEM],
        out_shape=[
            jax.ShapeDtypeStruct((FEATURES, ROWS), jnp.float32),
            jax.ShapeDtypeStruct((1, ROWS), jnp.float32),
        ],
        scratch_shapes=[
            pltpu.VMEM((N_HEAD, FEATURES, WIDTH), jnp.bfloat16),
            pltpu.VMEM((N_HEAD, WIDTH, ROWS), jnp.bfloat16),
            pltpu.SemaphoreType.DMA((N_HEAD, PIECES + 1)),
        ],
        compiler_params=pltpu.CompilerParams(vmem_limit_bytes=24 * 1024 * 1024),
        name="project",
    )(order, weights, *blocks)


def finish_kernel(acc_ref, sq_ref, gain_ref, res_ref, out_ref):
    squares = jnp.sum(sq_ref[...], axis=0)
    scale = lax.rsqrt(squares / D + EPS)
    value = res_ref[...].astype(jnp.float32) + gain_ref[...] * (acc_ref[...] * scale)
    out_ref[...] = value.astype(jnp.bfloat16)


def finish(attended, squares, gain, residual):
    return pl.pallas_call(
        finish_kernel,
        in_specs=[VMEM] * 4,
        out_shape=jax.ShapeDtypeStruct((FEATURES, ROWS), jnp.bfloat16),
        compiler_params=pltpu.CompilerParams(vmem_limit_bytes=12 * 1024 * 1024),
        name="finish",
    )(attended, squares, gain, residual)


def for_everyone(array, axis):
    length = lax.axis_size(axis)
    return lax.all_to_all(
        jnp.broadcast_to(array[None], (length, *array.shape)), axis, 0, 0, tiled=True
    )


def on_device(positions, queries, keys, values, out_weight, post_gain, residual):
    seq = lax.axis_index("seq")
    head = lax.axis_index("head")
    spread = [
        (s * N_HEAD + h, ((s // 4 + h) % N_HEAD * 4 + s % 4) * N_HEAD + s // 4)
        for s in range(N_SEQ)
        for h in range(N_HEAD)
    ]
    shard = lax.ppermute(out_weight.T, ("seq", "head"), spread)

    half = HEAD_SIZE // 2
    inverse = 10000.0 ** (-2.0 * jnp.arange(half, dtype=jnp.float32) / HEAD_SIZE)
    inverse = jnp.concatenate([inverse, inverse])[None]
    own, cosine, sine = prepare(
        positions[None], inverse, keys.transpose(1, 0, 2), values.transpose(1, 0, 2)
    )
    onward = [(i, i + 1) for i in range(N_SEQ - 1)]
    beyond = [(i, i + 2) for i in range(N_SEQ - 2)]
    prev = lax.ppermute(own, "seq", onward)
    far = lax.ppermute(own, "seq", beyond)
    shard = held(shard, prev, far)
    weights = lax.all_gather(shard, "seq", axis=0).reshape(N_HEAD, FEATURES, WIDTH)
    place = seq.astype(jnp.int32).reshape(1)
    q = queries.reshape(ROWS, WIDTH)

    ring = [
        (s * N_HEAD + h, s * N_HEAD + (h + (1 if s % 2 == 0 else -1)) % N_HEAD)
        for s in range(N_SEQ)
        for h in range(N_HEAD)
    ]
    blocks = [[] for _ in range(N_HEAD)]
    for g in range(KV):
        pieces = attend(g, place, q, cosine, sine, own, prev, far)
        for carried in pieces:
            blocks[0].append(carried)
            for k in range(1, N_HEAD):
                carried = lax.ppermute(carried, ("seq", "head"), ring)
                blocks[k].append(carried)
    sign = jnp.where(seq % 2 == 0, -1, 1)
    source = head + sign * jnp.arange(N_HEAD, dtype=jnp.int32)
    order = ((source + head) % N_HEAD).astype(jnp.int32)
    attended, squares = project(order, weights, [x for row in blocks for x in row])
    squares = for_everyone(squares, "head")
    return finish(attended, squares, post_gain[:, None], residual.T).T


def solution(mesh):
    return jax.shard_map(
        on_device,
        mesh=mesh,
        in_specs=(
            P("seq"),
            P("seq", "head", None),
            P("seq", "head", None),
            P("seq", "head", None),
            P("head", "seq"),
            P("head"),
            P("seq", "head"),
        ),
        out_specs=P("seq", "head"),
        check_vma=False,
    )
```

```python
import functools
import math

import jax
import jax.numpy as jnp
from jax import lax
from jax.experimental import pallas as pl
from jax.experimental.pallas import tpu as pltpu
from jax.sharding import PartitionSpec as P

D = 5376
HEAD_SIZE = 128
VISIBLE_SPAN = 1024
EPS = 1e-06
SCALE = 168.0 ** (-0.5)
LOG2E = math.log2(math.e)
ROWS = 512
KV = 2
GROUP = 2
N_SEQ = 32
N_HEAD = 8
FEATURES = D // N_HEAD
SHARD = D // N_SEQ
QB = 256
WIDTH = KV * GROUP * HEAD_SIZE
PIECE = 128
PIECES = WIDTH // PIECE
LOW = -1e30
VMEM = pl.BlockSpec(memory_space=pltpu.VMEM)


def cos_and_sin(angle):
    turns = jnp.floor(angle * (2.0 / math.pi) + 0.5)
    x = angle - turns * 1.5703125
    x = x - turns * 4.8351287841796875e-4
    x = x - turns * 3.1385570764541626e-07
    x = x - turns * 6.0771005065061922e-11
    z = x * x
    sine = ((-1.9515295891e-4 * z + 8.3321608736e-3) * z - 1.6666654611e-1) * z * x + x
    cosine = ((2.443315711809948e-5 * z - 1.388731625493765e-3) * z + 4.166664568298827e-2) * z * z
    cosine = cosine - 0.5 * z + 1.0
    quadrant = turns.astype(jnp.int32) & 3
    odd = (quadrant & 1) == 1
    first = jnp.where(odd, sine, cosine)
    second = jnp.where(odd, cosine, sine)
    first = jnp.where((quadrant == 1) | (quadrant == 2), -first, first)
    second = jnp.where(quadrant >= 2, -second, second)
    return first, second


def rotated(x, cosine, sine):
    x = x.astype(jnp.float32)
    return (x * cosine + pltpu.roll(x, 64, 1) * sine).astype(jnp.bfloat16)


def prepare_kernel(pos_ref, inverse_ref, k_ref, v_ref, kv_ref, cos_ref, sin_ref):
    place = jnp.broadcast_to(pos_ref[...].astype(jnp.float32), (HEAD_SIZE, ROWS)).T
    cosine, sine = cos_and_sin(place * inverse_ref[...])
    lane = lax.broadcasted_iota(jnp.int32, (ROWS, HEAD_SIZE), 1)
    sine = jnp.where(lane < HEAD_SIZE // 2, -sine, sine)
    cos_ref[...] = cosine
    sin_ref[...] = sine
    for g in range(KV):
        kv_ref[g, 0] = rotated(k_ref[g], cosine, sine)
        kv_ref[g, 1] = v_ref[g]


def prepare(positions, inverse, k, v):
    payload = jax.ShapeDtypeStruct((KV, 2, ROWS, HEAD_SIZE), jnp.bfloat16)
    table = jax.ShapeDtypeStruct((ROWS, HEAD_SIZE), jnp.float32)
    return pl.pallas_call(
        prepare_kernel,
        in_specs=[VMEM] * 4,
        out_specs=[VMEM] * 3,
        out_shape=[payload, table, table],
        compiler_params=pltpu.CompilerParams(vmem_limit_bytes=8 * 1024 * 1024),
        name="prepare",
    )(positions, inverse, k, v)


def rotate_kernel(q_ref, cos_ref, sin_ref, out_ref):
    for n in range(KV * GROUP):
        part = slice(n * HEAD_SIZE, (n + 1) * HEAD_SIZE)
        out_ref[:, part] = rotated(q_ref[:, part], cos_ref[...], sin_ref[...])


def rotate(q, cosine, sine):
    return pl.pallas_call(
        rotate_kernel,
        in_specs=[VMEM] * 3,
        out_specs=VMEM,
        out_shape=jax.ShapeDtypeStruct(q.shape, q.dtype),
        compiler_params=pltpu.CompilerParams(vmem_limit_bytes=4 * 1024 * 1024),
        name="rotate",
    )(q, cosine, sine)


def dot_nt(a, b):
    return lax.dot_general(a, b, (((1,), (1,)), ((), ())), preferred_element_type=jnp.float32)


def hold_kernel(first_ref, *refs):
    pass


def held(array, *others):
    hbm = pl.BlockSpec(memory_space=pltpu.HBM)
    others = [pltpu.with_memory_space_constraint(x, pltpu.VMEM) for x in others]
    return pl.pallas_call(
        hold_kernel,
        in_specs=[hbm] + [VMEM] * len(others),
        out_specs=hbm,
        out_shape=jax.ShapeDtypeStruct(array.shape, array.dtype),
        input_output_aliases={0: 0},
        compiler_params=pltpu.CompilerParams(vmem_limit_bytes=1024 * 1024),
        name="hold",
    )(array, *others)


def attend_kernel(n, place_ref, q_ref, own_ref, prev_ref, far_ref, out_ref):
    g = n // GROUP
    place = place_ref[0]
    prev_bias = jnp.where(place >= 1, 0.0, LOW)
    far_bias = jnp.where(place >= 2, 0.0, LOW)
    c = SCALE * LOG2E
    k_own, k_prev, k_far = own_ref[g, 0], prev_ref[g, 0], far_ref[g, 0]
    v_own = own_ref[g, 1].T
    v_prev = prev_ref[g, 1].T
    v_far = far_ref[g, 1].T
    row = lax.broadcasted_iota(jnp.int32, (QB, QB), 0)
    col = lax.broadcasted_iota(jnp.int32, (QB, QB), 1)
    seen = row <= col
    blocks = ROWS // QB
    q_all = q_ref[:, n * HEAD_SIZE : (n + 1) * HEAD_SIZE]
    for b in range(blocks):
        q = q_all[b * QB : (b + 1) * QB]
        lo, hi = b * QB, (b + 1) * QB
        prev = dot_nt(k_prev, q)
        own = dot_nt(k_own[0:hi], q)
        far = dot_nt(k_far[lo:ROWS], q)
        mixed = jnp.where(seen, own[lo:hi], far[0:QB] + far_bias)
        top = jnp.maximum(
            jnp.max(prev, axis=0, keepdims=True) + prev_bias,
            jnp.max(mixed, axis=0, keepdims=True),
        )
        if lo > 0:
            top = jnp.maximum(top, jnp.max(own[0:lo], axis=0, keepdims=True))
        if hi < ROWS:
            top = jnp.maximum(top, jnp.max(far[QB:], axis=0, keepdims=True) + far_bias)
        top = top * c
        p_prev = jnp.exp2(prev * c - (top - prev_bias))
        p_mixed = jnp.exp2(mixed * c - top)
        total = jnp.sum(p_prev, axis=0, keepdims=True) + jnp.sum(p_mixed, axis=0, keepdims=True)
        own_parts = [jnp.where(seen, p_mixed, 0.0).astype(jnp.bfloat16)]
        far_parts = [jnp.where(seen, 0.0, p_mixed).astype(jnp.bfloat16)]
        if lo > 0:
            p = jnp.exp2(own[0:lo] * c - top)
            total = total + jnp.sum(p, axis=0, keepdims=True)
            own_parts.insert(0, p.astype(jnp.bfloat16))
        if hi < ROWS:
            p = jnp.exp2(far[QB:] * c - (top - far_bias))
            total = total + jnp.sum(p, axis=0, keepdims=True)
            far_parts.append(p.astype(jnp.bfloat16))
        context = jnp.dot(v_prev, p_prev.astype(jnp.bfloat16), preferred_element_type=jnp.float32)
        context += jnp.dot(
            v_own[:, 0:hi], jnp.concatenate(own_parts, 0), preferred_element_type=jnp.float32
        )
        context += jnp.dot(
            v_far[:, lo:], jnp.concatenate(far_parts, 0), preferred_element_type=jnp.float32
        )
        out_ref[:, lo:hi] = (context / total).astype(jnp.bfloat16)


def attend(n, place, *arrays):
    arrays = [pltpu.with_memory_space_constraint(x, pltpu.VMEM) for x in arrays]
    return pl.pallas_call(
        functools.partial(attend_kernel, n),
        in_specs=[pl.BlockSpec(memory_space=pltpu.SMEM)] + [VMEM] * len(arrays),
        out_specs=VMEM,
        out_shape=jax.ShapeDtypeStruct((PIECE, ROWS), jnp.bfloat16),
        compiler_params=pltpu.CompilerParams(vmem_limit_bytes=16 * 1024 * 1024),
        name="attend",
    )(place, *arrays)


def project_kernel(order_ref, w_ref, *refs):
    ctx_refs = refs[: PIECES * N_HEAD]
    acc_ref, sq_ref, w_buffer, ctx_buffer, arrived = refs[PIECES * N_HEAD :]
    copies = []
    for k in range(N_HEAD):
        copies.append(
            [
                pltpu.make_async_copy(
                    w_ref.at[order_ref[0, k], order_ref[1, k] ^ part],
                    w_buffer.at[k, part],
                    arrived.at[k, PIECES + part],
                )
                for part in range(2)
            ]
            + [
                pltpu.make_async_copy(
                    ctx_refs[k * PIECES + g],
                    ctx_buffer.at[k, g * PIECE : (g + 1) * PIECE],
                    arrived.at[k, g],
                )
                for g in range(PIECES)
            ]
        )
        for copy in copies[k]:
            copy.start()
    for k in range(N_HEAD):
        for copy in copies[k]:
            copy.wait()
        total = 0.0
        for part in range(2):
            rows = slice(part * FEATURES // 2, (part + 1) * FEATURES // 2)
            value = jnp.dot(w_buffer[k, part], ctx_buffer[k], preferred_element_type=jnp.float32)
            if k > 0:
                value = acc_ref[rows] + value
            acc_ref[rows] = value
            if k == N_HEAD - 1:
                total = total + jnp.sum(value * value, axis=0, keepdims=True)
        if k == N_HEAD - 1:
            sq_ref[...] = jnp.broadcast_to(total[None], sq_ref.shape)


def project(order, weights, blocks):
    hbm = pl.BlockSpec(memory_space=pltpu.HBM)
    weights = pltpu.with_memory_space_constraint(weights, pltpu.HBM)
    blocks = [pltpu.with_memory_space_constraint(x, pltpu.HBM) for x in blocks]
    return pl.pallas_call(
        project_kernel,
        in_specs=[pl.BlockSpec(memory_space=pltpu.SMEM), hbm] + [hbm] * (PIECES * N_HEAD),
        out_specs=[VMEM, VMEM],
        out_shape=[
            jax.ShapeDtypeStruct((FEATURES, ROWS), jnp.float32),
            jax.ShapeDtypeStruct((N_HEAD, 1, ROWS), jnp.float32),
        ],
        scratch_shapes=[
            pltpu.VMEM((N_HEAD, 2, FEATURES // 2, WIDTH), jnp.bfloat16),
            pltpu.VMEM((N_HEAD, WIDTH, ROWS), jnp.bfloat16),
            pltpu.SemaphoreType.DMA((N_HEAD, PIECES + 2)),
        ],
        compiler_params=pltpu.CompilerParams(vmem_limit_bytes=24 * 1024 * 1024),
        name="project",
    )(order, weights, *blocks)


def finish_kernel(acc_ref, sq_ref, gain_ref, res_ref, out_ref):
    squares = jnp.sum(sq_ref[...], axis=0)
    scale = lax.rsqrt(squares / D + EPS)
    value = res_ref[...].astype(jnp.float32) + gain_ref[...] * (acc_ref[...] * scale)
    out_ref[...] = value.astype(jnp.bfloat16)


def finish(attended, squares, gain, residual):
    return pl.pallas_call(
        finish_kernel,
        in_specs=[VMEM] * 4,
        out_shape=jax.ShapeDtypeStruct((FEATURES, ROWS), jnp.bfloat16),
        compiler_params=pltpu.CompilerParams(vmem_limit_bytes=12 * 1024 * 1024),
        name="finish",
    )(attended, squares, gain, residual)


def on_device(positions, queries, keys, values, out_weight, post_gain, residual):
    seq = lax.axis_index("seq")
    head = lax.axis_index("head")
    across, along = [], []
    for s in range(N_SEQ):
        for h in range(N_HEAD):
            group = s // 4
            middle = (group + h) % N_HEAD * 4 + (s % 4 if (h % 2 == 0) else s % 4 ^ 2)
            across.append((s * N_HEAD + h, middle * N_HEAD + h))
            along.append((middle * N_HEAD + h, middle * N_HEAD + group))
    shard = lax.ppermute(out_weight.T, ("seq", "head"), across)
    shard = lax.ppermute(shard, ("seq", "head"), along)

    half = HEAD_SIZE // 2
    inverse = 10000.0 ** (-2.0 * jnp.arange(half, dtype=jnp.float32) / HEAD_SIZE)
    inverse = jnp.concatenate([inverse, inverse])[None]
    own, cosine, sine = prepare(
        positions[None], inverse, keys.transpose(1, 0, 2), values.transpose(1, 0, 2)
    )
    onward = [(i, i + 1) for i in range(N_SEQ - 1)]
    beyond = [(i, i + 2) for i in range(N_SEQ - 2)]
    prev = lax.ppermute(own, "seq", onward)
    far = lax.ppermute(own, "seq", beyond)
    q = rotate(queries.reshape(ROWS, WIDTH), cosine, sine)
    shard = held(shard, prev, far, q)
    weights = lax.all_gather(shard, "seq", axis=0).reshape(N_HEAD, 2, FEATURES // 2, WIDTH)
    place = seq.astype(jnp.int32).reshape(1)

    ring = [
        (s * N_HEAD + h, s * N_HEAD + (h + (1 if s % 2 == 0 else -1)) % N_HEAD)
        for s in range(N_SEQ)
        for h in range(N_HEAD)
    ]
    blocks = [[] for _ in range(N_HEAD)]
    for n in range(PIECES):
        carried = attend(n, place, q, own, prev, far)
        blocks[0].append(carried)
        for k in range(1, N_HEAD):
            carried = lax.ppermute(carried, ("seq", "head"), ring)
            blocks[k].append(carried)
    sign = jnp.where(seq % 2 == 0, -1, 1)
    source = head + sign * jnp.arange(N_HEAD, dtype=jnp.int32)
    source = source % N_HEAD
    order = jnp.stack([(source + head) % N_HEAD, source % 2]).astype(jnp.int32)
    attended, squares = project(order, weights, [x for row in blocks for x in row])
    squares = lax.all_to_all(squares, "head", 0, 0, tiled=True)
    return finish(attended, squares, post_gain[:, None], residual.T).T


def solution(mesh):
    return jax.shard_map(
        on_device,
        mesh=mesh,
        in_specs=(
            P("seq"),
            P("seq", "head", None),
            P("seq", "head", None),
            P("seq", "head", None),
            P("head", "seq"),
            P("head"),
            P("seq", "head"),
        ),
        out_specs=P("seq", "head"),
        check_vma=False,
    )
```

```python
import functools
import math

import jax
import jax.numpy as jnp
from jax import lax
from jax.experimental import pallas as pl
from jax.experimental.pallas import tpu as pltpu
from jax.sharding import PartitionSpec as P

D = 5376
HEAD_SIZE = 128
VISIBLE_SPAN = 1024
EPS = 1e-06
SCALE = 168.0 ** (-0.5)
LOG2E = math.log2(math.e)
ROWS = 512
KV = 2
GROUP = 2
N_SEQ = 32
N_HEAD = 8
FEATURES = D // N_HEAD
SHARD = D // N_SEQ
QB = 256
WIDTH = KV * GROUP * HEAD_SIZE
PIECE = 128
PIECES = WIDTH // PIECE
LOW = -1e30
VMEM = pl.BlockSpec(memory_space=pltpu.VMEM)


def cos_and_sin(angle):
    turns = jnp.floor(angle * (2.0 / math.pi) + 0.5)
    x = angle - turns * 1.5703125
    x = x - turns * 4.8351287841796875e-4
    x = x - turns * 3.1385570764541626e-07
    x = x - turns * 6.0771005065061922e-11
    z = x * x
    sine = ((-1.9515295891e-4 * z + 8.3321608736e-3) * z - 1.6666654611e-1) * z * x + x
    cosine = ((2.443315711809948e-5 * z - 1.388731625493765e-3) * z + 4.166664568298827e-2) * z * z
    cosine = cosine - 0.5 * z + 1.0
    quadrant = turns.astype(jnp.int32) & 3
    odd = (quadrant & 1) == 1
    first = jnp.where(odd, sine, cosine)
    second = jnp.where(odd, cosine, sine)
    first = jnp.where((quadrant == 1) | (quadrant == 2), -first, first)
    second = jnp.where(quadrant >= 2, -second, second)
    return first, second


def rotated(x, cosine, sine):
    x = x.astype(jnp.float32)
    return (x * cosine + pltpu.roll(x, 64, 1) * sine).astype(jnp.bfloat16)


def prepare_kernel(pos_ref, inverse_ref, k_ref, v_ref, kv_ref, cos_ref, sin_ref):
    place = jnp.broadcast_to(pos_ref[...].astype(jnp.float32), (HEAD_SIZE, ROWS)).T
    cosine, sine = cos_and_sin(place * inverse_ref[...])
    lane = lax.broadcasted_iota(jnp.int32, (ROWS, HEAD_SIZE), 1)
    sine = jnp.where(lane < HEAD_SIZE // 2, -sine, sine)
    cos_ref[...] = cosine
    sin_ref[...] = sine
    for g in range(KV):
        kv_ref[g, 0] = rotated(k_ref[g], cosine, sine)
        kv_ref[g, 1] = v_ref[g]


def prepare(positions, inverse, k, v):
    payload = jax.ShapeDtypeStruct((KV, 2, ROWS, HEAD_SIZE), jnp.bfloat16)
    table = jax.ShapeDtypeStruct((ROWS, HEAD_SIZE), jnp.float32)
    return pl.pallas_call(
        prepare_kernel,
        in_specs=[VMEM] * 4,
        out_specs=[VMEM] * 3,
        out_shape=[payload, table, table],
        compiler_params=pltpu.CompilerParams(vmem_limit_bytes=8 * 1024 * 1024),
        name="prepare",
    )(positions, inverse, k, v)


def rotate_kernel(q_ref, cos_ref, sin_ref, out_ref):
    for n in range(KV * GROUP):
        part = slice(n * HEAD_SIZE, (n + 1) * HEAD_SIZE)
        out_ref[:, part] = rotated(q_ref[:, part], cos_ref[...], sin_ref[...])


def rotate(q, cosine, sine):
    return pl.pallas_call(
        rotate_kernel,
        in_specs=[VMEM] * 3,
        out_specs=VMEM,
        out_shape=jax.ShapeDtypeStruct(q.shape, q.dtype),
        compiler_params=pltpu.CompilerParams(vmem_limit_bytes=4 * 1024 * 1024),
        name="rotate",
    )(q, cosine, sine)


def dot_nt(a, b):
    return lax.dot_general(a, b, (((1,), (1,)), ((), ())), preferred_element_type=jnp.float32)


def hold_kernel(first_ref, *refs):
    pass


def held(array, *others):
    hbm = pl.BlockSpec(memory_space=pltpu.HBM)
    others = [pltpu.with_memory_space_constraint(x, pltpu.VMEM) for x in others]
    return pl.pallas_call(
        hold_kernel,
        in_specs=[hbm] + [VMEM] * len(others),
        out_specs=hbm,
        out_shape=jax.ShapeDtypeStruct(array.shape, array.dtype),
        input_output_aliases={0: 0},
        compiler_params=pltpu.CompilerParams(vmem_limit_bytes=1024 * 1024),
        name="hold",
    )(array, *others)


def attend_kernel(n, place_ref, q_ref, own_ref, prev_ref, far_ref, out_ref):
    g = n // GROUP
    place = place_ref[0]
    prev_bias = jnp.where(place >= 1, 0.0, LOW)
    far_bias = jnp.where(place >= 2, 0.0, LOW)
    c = SCALE * LOG2E
    k_own, k_prev, k_far = own_ref[g, 0], prev_ref[g, 0], far_ref[g, 0]
    v_own = own_ref[g, 1].T
    v_prev = prev_ref[g, 1].T
    v_far = far_ref[g, 1].T
    row = lax.broadcasted_iota(jnp.int32, (QB, QB), 0)
    col = lax.broadcasted_iota(jnp.int32, (QB, QB), 1)
    seen = row <= col
    blocks = ROWS // QB
    q_all = q_ref[:, n * HEAD_SIZE : (n + 1) * HEAD_SIZE]
    for b in range(blocks):
        q = q_all[b * QB : (b + 1) * QB]
        lo, hi = b * QB, (b + 1) * QB
        prev = dot_nt(k_prev, q)
        own = dot_nt(k_own[0:hi], q)
        far = dot_nt(k_far[lo:ROWS], q)
        mixed = jnp.where(seen, own[lo:hi], far[0:QB] + far_bias)
        top = jnp.maximum(
            jnp.max(prev, axis=0, keepdims=True) + prev_bias,
            jnp.max(mixed, axis=0, keepdims=True),
        )
        if lo > 0:
            top = jnp.maximum(top, jnp.max(own[0:lo], axis=0, keepdims=True))
        if hi < ROWS:
            top = jnp.maximum(top, jnp.max(far[QB:], axis=0, keepdims=True) + far_bias)
        top = top * c
        p_prev = jnp.exp2(prev * c - (top - prev_bias))
        p_mixed = jnp.exp2(mixed * c - top)
        total = jnp.sum(p_prev, axis=0, keepdims=True) + jnp.sum(p_mixed, axis=0, keepdims=True)
        own_parts = [jnp.where(seen, p_mixed, 0.0).astype(jnp.bfloat16)]
        far_parts = [jnp.where(seen, 0.0, p_mixed).astype(jnp.bfloat16)]
        if lo > 0:
            p = jnp.exp2(own[0:lo] * c - top)
            total = total + jnp.sum(p, axis=0, keepdims=True)
            own_parts.insert(0, p.astype(jnp.bfloat16))
        if hi < ROWS:
            p = jnp.exp2(far[QB:] * c - (top - far_bias))
            total = total + jnp.sum(p, axis=0, keepdims=True)
            far_parts.append(p.astype(jnp.bfloat16))
        context = jnp.dot(v_prev, p_prev.astype(jnp.bfloat16), preferred_element_type=jnp.float32)
        context += jnp.dot(
            v_own[:, 0:hi], jnp.concatenate(own_parts, 0), preferred_element_type=jnp.float32
        )
        context += jnp.dot(
            v_far[:, lo:], jnp.concatenate(far_parts, 0), preferred_element_type=jnp.float32
        )
        out_ref[:, lo:hi] = (context / total).astype(jnp.bfloat16)


def attend(n, place, *arrays):
    arrays = [pltpu.with_memory_space_constraint(x, pltpu.VMEM) for x in arrays]
    return pl.pallas_call(
        functools.partial(attend_kernel, n),
        in_specs=[pl.BlockSpec(memory_space=pltpu.SMEM)] + [VMEM] * len(arrays),
        out_specs=VMEM,
        out_shape=jax.ShapeDtypeStruct((PIECE, ROWS), jnp.bfloat16),
        compiler_params=pltpu.CompilerParams(vmem_limit_bytes=16 * 1024 * 1024),
        name="attend",
    )(place, *arrays)


def project_kernel(order_ref, w_ref, *refs):
    ctx_refs = refs[: PIECES * N_HEAD]
    acc_ref, sq_ref, w_buffer, ctx_buffer, arrived = refs[PIECES * N_HEAD :]
    copies = []
    for k in range(N_HEAD):
        copies.append(
            [
                pltpu.make_async_copy(
                    w_ref.at[order_ref[0, k], order_ref[1, k] ^ part],
                    w_buffer.at[k, part],
                    arrived.at[k, PIECES + part],
                )
                for part in range(2)
            ]
            + [
                pltpu.make_async_copy(
                    ctx_refs[k * PIECES + g],
                    ctx_buffer.at[k, g * PIECE : (g + 1) * PIECE],
                    arrived.at[k, g],
                )
                for g in range(PIECES)
            ]
        )
        for copy in copies[k]:
            copy.start()
    for k in range(N_HEAD):
        for copy in copies[k]:
            copy.wait()
        total = 0.0
        for part in range(2):
            rows = slice(part * FEATURES // 2, (part + 1) * FEATURES // 2)
            value = jnp.dot(w_buffer[k, part], ctx_buffer[k], preferred_element_type=jnp.float32)
            if k > 0:
                value = acc_ref[rows] + value
            acc_ref[rows] = value
            if k == N_HEAD - 1:
                total = total + jnp.sum(value * value, axis=0, keepdims=True)
        if k == N_HEAD - 1:
            sq_ref[...] = jnp.broadcast_to(total[None], sq_ref.shape)


def project(order, weights, blocks):
    hbm = pl.BlockSpec(memory_space=pltpu.HBM)
    weights = pltpu.with_memory_space_constraint(weights, pltpu.HBM)
    blocks = [pltpu.with_memory_space_constraint(x, pltpu.HBM) for x in blocks]
    return pl.pallas_call(
        project_kernel,
        in_specs=[pl.BlockSpec(memory_space=pltpu.SMEM), hbm] + [hbm] * (PIECES * N_HEAD),
        out_specs=[VMEM, VMEM],
        out_shape=[
            jax.ShapeDtypeStruct((FEATURES, ROWS), jnp.float32),
            jax.ShapeDtypeStruct((N_HEAD, 1, ROWS), jnp.float32),
        ],
        scratch_shapes=[
            pltpu.VMEM((N_HEAD, 2, FEATURES // 2, WIDTH), jnp.bfloat16),
            pltpu.VMEM((N_HEAD, WIDTH, ROWS), jnp.bfloat16),
            pltpu.SemaphoreType.DMA((N_HEAD, PIECES + 2)),
        ],
        compiler_params=pltpu.CompilerParams(vmem_limit_bytes=24 * 1024 * 1024),
        name="project",
    )(order, weights, *blocks)


def finish_kernel(acc_ref, sq_ref, gain_ref, res_ref, out_ref):
    squares = jnp.sum(sq_ref[...], axis=0)
    scale = lax.rsqrt(squares / D + EPS)
    value = res_ref[...].astype(jnp.float32) + gain_ref[...] * (acc_ref[...] * scale)
    out_ref[...] = value.astype(jnp.bfloat16)


def finish(attended, squares, gain, residual):
    return pl.pallas_call(
        finish_kernel,
        in_specs=[VMEM] * 4,
        out_shape=jax.ShapeDtypeStruct((FEATURES, ROWS), jnp.bfloat16),
        compiler_params=pltpu.CompilerParams(vmem_limit_bytes=12 * 1024 * 1024),
        name="finish",
    )(attended, squares, gain, residual)


def on_device(positions, queries, keys, values, out_weight, post_gain, residual):
    seq = lax.axis_index("seq")
    head = lax.axis_index("head")
    across, along = [], []
    for s in range(N_SEQ):
        for h in range(N_HEAD):
            group = s // 4
            middle = (group + h) % N_HEAD * 4 + (s % 4 if (h % 2 == 0) else s % 4 ^ 2)
            across.append((s * N_HEAD + h, middle * N_HEAD + h))
            along.append((middle * N_HEAD + h, middle * N_HEAD + group))
    shard = lax.ppermute(out_weight.T, ("seq", "head"), across)
    shard = lax.ppermute(shard, ("seq", "head"), along)

    half = HEAD_SIZE // 2
    inverse = 10000.0 ** (-2.0 * jnp.arange(half, dtype=jnp.float32) / HEAD_SIZE)
    inverse = jnp.concatenate([inverse, inverse])[None]
    own, cosine, sine = prepare(
        positions[None], inverse, keys.transpose(1, 0, 2), values.transpose(1, 0, 2)
    )
    onward = [(i, i + 1) for i in range(N_SEQ - 1)]
    prev = lax.ppermute(own, "seq", onward)
    far = lax.ppermute(prev, "seq", onward)
    q = rotate(queries.reshape(ROWS, WIDTH), cosine, sine)
    shard = held(shard, prev, far, q)
    weights = lax.all_gather(shard, "seq", axis=0).reshape(N_HEAD, 2, FEATURES // 2, WIDTH)
    place = seq.astype(jnp.int32).reshape(1)

    ring = [
        (s * N_HEAD + h, s * N_HEAD + (h + (1 if s % 2 == 0 else -1)) % N_HEAD)
        for s in range(N_SEQ)
        for h in range(N_HEAD)
    ]
    blocks = [[] for _ in range(N_HEAD)]
    for n in range(PIECES):
        carried = attend(n, place, q, own, prev, far)
        blocks[0].append(carried)
        for k in range(1, N_HEAD):
            carried = lax.ppermute(carried, ("seq", "head"), ring)
            blocks[k].append(carried)
    sign = jnp.where(seq % 2 == 0, -1, 1)
    source = head + sign * jnp.arange(N_HEAD, dtype=jnp.int32)
    source = source % N_HEAD
    order = jnp.stack([(source + head) % N_HEAD, source % 2]).astype(jnp.int32)
    attended, squares = project(order, weights, [x for row in blocks for x in row])
    squares = lax.all_to_all(squares, "head", 0, 0, tiled=True)
    return finish(attended, squares, post_gain[:, None], residual.T).T


def solution(mesh):
    return jax.shard_map(
        on_device,
        mesh=mesh,
        in_specs=(
            P("seq"),
            P("seq", "head", None),
            P("seq", "head", None),
            P("seq", "head", None),
            P("head", "seq"),
            P("head"),
            P("seq", "head"),
        ),
        out_specs=P("seq", "head"),
        check_vma=False,
    )
```

```python
import functools
import math

import jax
import jax.numpy as jnp
from jax import lax
from jax.experimental import pallas as pl
from jax.experimental.pallas import tpu as pltpu
from jax.sharding import PartitionSpec as P

D = 5376
HEAD_SIZE = 128
VISIBLE_SPAN = 1024
EPS = 1e-06
SCALE = 168.0 ** (-0.5)
LOG2E = math.log2(math.e)
ROWS = 512
KV = 2
GROUP = 2
N_SEQ = 32
N_HEAD = 8
FEATURES = D // N_HEAD
SHARD = D // N_SEQ
SIDE = 4
QB = 256
WIDTH = KV * GROUP * HEAD_SIZE
PIECE = 128
PIECES = WIDTH // PIECE
LOW = -1e30
VMEM = pl.BlockSpec(memory_space=pltpu.VMEM)


def cos_and_sin(angle):
    turns = jnp.floor(angle * (2.0 / math.pi) + 0.5)
    x = angle - turns * 1.5703125
    x = x - turns * 4.8351287841796875e-4
    x = x - turns * 3.1385570764541626e-07
    x = x - turns * 6.0771005065061922e-11
    z = x * x
    sine = ((-1.9515295891e-4 * z + 8.3321608736e-3) * z - 1.6666654611e-1) * z * x + x
    cosine = ((2.443315711809948e-5 * z - 1.388731625493765e-3) * z + 4.166664568298827e-2) * z * z
    cosine = cosine - 0.5 * z + 1.0
    quadrant = turns.astype(jnp.int32) & 3
    odd = (quadrant & 1) == 1
    first = jnp.where(odd, sine, cosine)
    second = jnp.where(odd, cosine, sine)
    first = jnp.where((quadrant == 1) | (quadrant == 2), -first, first)
    second = jnp.where(quadrant >= 2, -second, second)
    return first, second


def rotated(x, cosine, sine):
    x = x.astype(jnp.float32)
    return (x * cosine + pltpu.roll(x, 64, 1) * sine).astype(jnp.bfloat16)


def prepare_kernel(pos_ref, inverse_ref, k_ref, v_ref, kv_ref, cos_ref, sin_ref):
    place = jnp.broadcast_to(pos_ref[...].astype(jnp.float32), (HEAD_SIZE, ROWS)).T
    cosine, sine = cos_and_sin(place * inverse_ref[...])
    lane = lax.broadcasted_iota(jnp.int32, (ROWS, HEAD_SIZE), 1)
    sine = jnp.where(lane < HEAD_SIZE // 2, -sine, sine)
    cos_ref[...] = cosine
    sin_ref[...] = sine
    for g in range(KV):
        kv_ref[g, 0] = rotated(k_ref[g], cosine, sine)
        kv_ref[g, 1] = v_ref[g]


def prepare(positions, inverse, k, v):
    payload = jax.ShapeDtypeStruct((KV, 2, ROWS, HEAD_SIZE), jnp.bfloat16)
    table = jax.ShapeDtypeStruct((ROWS, HEAD_SIZE), jnp.float32)
    return pl.pallas_call(
        prepare_kernel,
        in_specs=[VMEM] * 4,
        out_specs=[VMEM] * 3,
        out_shape=[payload, table, table],
        compiler_params=pltpu.CompilerParams(vmem_limit_bytes=8 * 1024 * 1024),
        name="prepare",
    )(positions, inverse, k, v)


def rotate_kernel(q_ref, cos_ref, sin_ref, out_ref):
    for n in range(KV * GROUP):
        part = slice(n * HEAD_SIZE, (n + 1) * HEAD_SIZE)
        out_ref[:, part] = rotated(q_ref[:, part], cos_ref[...], sin_ref[...])


def rotate(q, cosine, sine):
    return pl.pallas_call(
        rotate_kernel,
        in_specs=[VMEM] * 3,
        out_specs=VMEM,
        out_shape=jax.ShapeDtypeStruct(q.shape, q.dtype),
        compiler_params=pltpu.CompilerParams(vmem_limit_bytes=4 * 1024 * 1024),
        name="rotate",
    )(q, cosine, sine)


def dot_nt(a, b):
    return lax.dot_general(a, b, (((1,), (1,)), ((), ())), preferred_element_type=jnp.float32)


def hold_kernel(*refs):
    pass


def held(*arrays, after=()):
    arrays = [pltpu.with_memory_space_constraint(x, pltpu.VMEM) for x in arrays]
    after = [pltpu.with_memory_space_constraint(x, pltpu.VMEM) for x in after]
    return pl.pallas_call(
        hold_kernel,
        in_specs=[VMEM] * (len(arrays) + len(after)),
        out_specs=[VMEM] * len(arrays),
        out_shape=[jax.ShapeDtypeStruct(x.shape, x.dtype) for x in arrays],
        input_output_aliases={n: n for n in range(len(arrays))},
        compiler_params=pltpu.CompilerParams(vmem_limit_bytes=1024 * 1024),
        name="hold",
    )(*arrays, *after)


def attend_kernel(n, place_ref, q_ref, own_ref, prev_ref, far_ref, out_ref):
    g = n // GROUP
    place = place_ref[0]
    prev_bias = jnp.where(place >= 1, 0.0, LOW)
    far_bias = jnp.where(place >= 2, 0.0, LOW)
    c = SCALE * LOG2E
    k_own, k_prev, k_far = own_ref[g, 0], prev_ref[g, 0], far_ref[g, 0]
    v_own = own_ref[g, 1].T
    v_prev = prev_ref[g, 1].T
    v_far = far_ref[g, 1].T
    row = lax.broadcasted_iota(jnp.int32, (QB, QB), 0)
    col = lax.broadcasted_iota(jnp.int32, (QB, QB), 1)
    seen = row <= col
    blocks = ROWS // QB
    q_all = q_ref[:, n * HEAD_SIZE : (n + 1) * HEAD_SIZE]
    for b in range(blocks):
        q = q_all[b * QB : (b + 1) * QB]
        lo, hi = b * QB, (b + 1) * QB
        prev = dot_nt(k_prev, q)
        own = dot_nt(k_own[0:hi], q)
        far = dot_nt(k_far[lo:ROWS], q)
        mixed = jnp.where(seen, own[lo:hi], far[0:QB] + far_bias)
        top = jnp.maximum(
            jnp.max(prev, axis=0, keepdims=True) + prev_bias,
            jnp.max(mixed, axis=0, keepdims=True),
        )
        if lo > 0:
            top = jnp.maximum(top, jnp.max(own[0:lo], axis=0, keepdims=True))
        if hi < ROWS:
            top = jnp.maximum(top, jnp.max(far[QB:], axis=0, keepdims=True) + far_bias)
        top = top * c
        p_prev = jnp.exp2(prev * c - (top - prev_bias))
        p_mixed = jnp.exp2(mixed * c - top)
        total = jnp.sum(p_prev, axis=0, keepdims=True) + jnp.sum(p_mixed, axis=0, keepdims=True)
        own_parts = [jnp.where(seen, p_mixed, 0.0).astype(jnp.bfloat16)]
        far_parts = [jnp.where(seen, 0.0, p_mixed).astype(jnp.bfloat16)]
        if lo > 0:
            p = jnp.exp2(own[0:lo] * c - top)
            total = total + jnp.sum(p, axis=0, keepdims=True)
            own_parts.insert(0, p.astype(jnp.bfloat16))
        if hi < ROWS:
            p = jnp.exp2(far[QB:] * c - (top - far_bias))
            total = total + jnp.sum(p, axis=0, keepdims=True)
            far_parts.append(p.astype(jnp.bfloat16))
        context = jnp.dot(v_prev, p_prev.astype(jnp.bfloat16), preferred_element_type=jnp.float32)
        context += jnp.dot(
            v_own[:, 0:hi], jnp.concatenate(own_parts, 0), preferred_element_type=jnp.float32
        )
        context += jnp.dot(
            v_far[:, lo:], jnp.concatenate(far_parts, 0), preferred_element_type=jnp.float32
        )
        out_ref[:, lo:hi] = (context / total).astype(jnp.bfloat16)


def attend(n, place, *arrays):
    arrays = [pltpu.with_memory_space_constraint(x, pltpu.VMEM) for x in arrays]
    return pl.pallas_call(
        functools.partial(attend_kernel, n),
        in_specs=[pl.BlockSpec(memory_space=pltpu.SMEM)] + [VMEM] * len(arrays),
        out_specs=VMEM,
        out_shape=jax.ShapeDtypeStruct((PIECE, ROWS), jnp.bfloat16),
        compiler_params=pltpu.CompilerParams(vmem_limit_bytes=16 * 1024 * 1024),
        name="attend",
    )(place, *arrays)


def project_kernel(table_ref, *refs):
    ctx_refs = refs[-6 - PIECES * N_HEAD : -6]
    w_refs = refs[: -6 - PIECES * N_HEAD]
    acc_ref, sq_ref, w_buffer, ctx_buffer, w_arrived, ctx_arrived = refs[-6:]
    shards = SIDE * SIDE
    own_core = table_ref[2 * shards]
    count = 0
    for w_ref in w_refs:
        for i in range(w_ref.shape[0]):
            at = count % shards
            step, pair = table_ref[2 * at], table_ref[2 * at + 1]
            core = own_core if count < shards else 1 - own_core
            count += 1
            pltpu.make_async_copy(
                w_ref.at[i], w_buffer.at[step, pair, core], w_arrived.at[step, pair, core]
            ).start()
    contexts = [
        [
            pltpu.make_async_copy(
                ctx_refs[k * PIECES + g],
                ctx_buffer.at[k, g * PIECE : (g + 1) * PIECE],
                ctx_arrived.at[k, g],
            )
            for g in range(PIECES)
        ]
        for k in range(N_HEAD)
    ]
    for copies in contexts:
        for copy in copies:
            copy.start()
    for k in range(N_HEAD):
        for pair in range(2):
            for core in range(2):
                pltpu.make_async_copy(
                    w_refs[0].at[0], w_buffer.at[k, pair, core], w_arrived.at[k, pair, core]
                ).wait()
        for copy in contexts[k]:
            copy.wait()
        value = jnp.dot(
            w_buffer[k].reshape(FEATURES, WIDTH), ctx_buffer[k], preferred_element_type=jnp.float32
        )
        if k > 0:
            value = acc_ref[...] + value
        acc_ref[...] = value
        if k == N_HEAD - 1:
            total = jnp.sum(value * value, axis=0, keepdims=True)
            sq_ref[...] = jnp.broadcast_to(total[None], sq_ref.shape)


def project(table, weights, blocks):
    hbm = pl.BlockSpec(memory_space=pltpu.HBM)
    arrays = [pltpu.with_memory_space_constraint(x, pltpu.HBM) for x in weights + blocks]
    return pl.pallas_call(
        project_kernel,
        in_specs=[pl.BlockSpec(memory_space=pltpu.SMEM)] + [hbm] * len(arrays),
        out_specs=[VMEM, VMEM],
        out_shape=[
            jax.ShapeDtypeStruct((FEATURES, ROWS), jnp.float32),
            jax.ShapeDtypeStruct((N_HEAD, 1, ROWS), jnp.float32),
        ],
        scratch_shapes=[
            pltpu.VMEM((N_HEAD, 2, 2, SHARD, WIDTH), jnp.bfloat16),
            pltpu.VMEM((N_HEAD, WIDTH, ROWS), jnp.bfloat16),
            pltpu.SemaphoreType.DMA((N_HEAD, 2, 2)),
            pltpu.SemaphoreType.DMA((N_HEAD, PIECES)),
        ],
        compiler_params=pltpu.CompilerParams(vmem_limit_bytes=20 * 1024 * 1024),
        name="project",
    )(table, *arrays)


def finish_kernel(acc_ref, sq_ref, gain_ref, res_ref, out_ref):
    squares = jnp.sum(sq_ref[...], axis=0)
    scale = lax.rsqrt(squares / D + EPS)
    value = res_ref[...].astype(jnp.float32) + gain_ref[...] * (acc_ref[...] * scale)
    out_ref[...] = value.astype(jnp.bfloat16)


def finish(attended, squares, gain, residual):
    return pl.pallas_call(
        finish_kernel,
        in_specs=[VMEM] * 4,
        out_shape=jax.ShapeDtypeStruct((FEATURES, ROWS), jnp.bfloat16),
        compiler_params=pltpu.CompilerParams(vmem_limit_bytes=12 * 1024 * 1024),
        name="finish",
    )(attended, squares, gain, residual)


def device(x, y, core, head):
    return ((x % SIDE * SIDE + y % SIDE) * 2 + core) * N_HEAD + head % N_HEAD


def moved(array, rule):
    pairs = [
        (device(x, y, core, head), device(*rule(x, y, core, head)))
        for x in range(SIDE)
        for y in range(SIDE)
        for core in range(2)
        for head in range(N_HEAD)
    ]
    return lax.ppermute(array, ("seq", "head"), pairs)


def sense(core):
    return 1 - 2 * core


def spread(x, y, core, head):
    group = (2 * x + y // 2 + head) % N_HEAD
    return group // 2, group % 2 * 2 + (y + head) % 2, core, head


def lifted(x, y, core, head):
    return x, y, core, 2 * x + y // 2 - head


def on_device(positions, queries, keys, values, out_weight, post_gain, residual):
    seq = lax.axis_index("seq").astype(jnp.int32)
    head = lax.axis_index("head").astype(jnp.int32)
    shard = moved(out_weight.T, spread)

    half = HEAD_SIZE // 2
    inverse = 10000.0 ** (-2.0 * jnp.arange(half, dtype=jnp.float32) / HEAD_SIZE)
    inverse = jnp.concatenate([inverse, inverse])[None]
    own, cosine, sine = prepare(
        positions[None], inverse, keys.transpose(1, 0, 2), values.transpose(1, 0, 2)
    )
    onward = [(i, i + 1) for i in range(N_SEQ - 1)]
    prev = lax.ppermute(own, "seq", onward)
    prev, shard = held(prev, shard)
    far = lax.ppermute(prev, "seq", onward)
    shard = moved(shard, lifted)
    q = rotate(queries.reshape(ROWS, WIDTH), cosine, sine)
    far, shard, q = held(far, shard, q)

    blocks = [[] for _ in range(N_HEAD)]
    place = seq.reshape(1)
    for n in range(PIECES):
        carried = attend(n, place, q, own, prev, far)
        blocks[0].append(carried)
        for k in range(1, N_HEAD):
            carried = moved(carried, lambda x, y, core, head: (x, y, core, head + sense(core)))
            blocks[k].append(carried)

    right = lambda x, y, core, head: (x + 1, y, core, head)
    left = lambda x, y, core, head: (x - 1, y, core, head)
    up = lambda x, y, core, head: (x, y + 1, core, head)
    down = lambda x, y, core, head: (x, y - 1, core, head)
    before, behind = moved(shard, right), moved(shard, left)
    before, behind = held(before, behind, after=blocks[1][-1:])
    row = jnp.stack([shard, before, behind, moved(before, right)])
    row = held(row, after=blocks[2][-1:])[0]
    before, behind = moved(row, up), moved(row, down)
    before, behind = held(before, behind, after=blocks[5][-1:])
    rows = [row, before, behind, moved(before[:2], up), moved(behind[2:], down)]
    others = [moved(x, lambda x, y, core, head: (x, y, 1 - core, head)) for x in rows]

    x, y, core = seq // 8, seq // 2 % SIDE, seq % 2
    offset = jnp.array([0, -1, 1, 2], jnp.int32)
    from_y = (y + offset[:, None]) % SIDE
    from_x = (x + offset[None, :]) % SIDE
    source = (2 * from_x + from_y // 2 - head) % N_HEAD
    table = jnp.stack([sense(core) * (head - source) % N_HEAD, (from_y + source) % 2], -1)
    table = jnp.concatenate([table.reshape(-1), core.reshape(1)]).astype(jnp.int32)

    attended, squares = project(table, rows + others, [x for row in blocks for x in row])
    squares = lax.all_to_all(squares, "head", 0, 0, tiled=True)
    return finish(attended, squares, post_gain[:, None], residual.T).T


def solution(mesh):
    return jax.shard_map(
        on_device,
        mesh=mesh,
        in_specs=(
            P("seq"),
            P("seq", "head", None),
            P("seq", "head", None),
            P("seq", "head", None),
            P("head", "seq"),
            P("head"),
            P("seq", "head"),
        ),
        out_specs=P("seq", "head"),
        check_vma=False,
    )
```

```python
import functools
import math

import jax
import jax.numpy as jnp
from jax import lax
from jax.experimental import pallas as pl
from jax.experimental.pallas import tpu as pltpu
from jax.sharding import PartitionSpec as P

D = 5376
HEAD_SIZE = 128
VISIBLE_SPAN = 1024
EPS = 1e-06
SCALE = 168.0 ** (-0.5)
LOG2E = math.log2(math.e)
ROWS = 512
KV = 2
GROUP = 2
N_SEQ = 32
N_HEAD = 8
FEATURES = D // N_HEAD
SHARD = D // N_SEQ
SIDE = 4
QB = 256
WIDTH = KV * GROUP * HEAD_SIZE
PIECE = 128
PIECES = WIDTH // PIECE
LOW = -1e30
VMEM = pl.BlockSpec(memory_space=pltpu.VMEM)


def cos_and_sin(angle):
    turns = jnp.floor(angle * (2.0 / math.pi) + 0.5)
    x = angle - turns * 1.5703125
    x = x - turns * 4.8351287841796875e-4
    x = x - turns * 3.1385570764541626e-07
    x = x - turns * 6.0771005065061922e-11
    z = x * x
    sine = ((-1.9515295891e-4 * z + 8.3321608736e-3) * z - 1.6666654611e-1) * z * x + x
    cosine = ((2.443315711809948e-5 * z - 1.388731625493765e-3) * z + 4.166664568298827e-2) * z * z
    cosine = cosine - 0.5 * z + 1.0
    quadrant = turns.astype(jnp.int32) & 3
    odd = (quadrant & 1) == 1
    first = jnp.where(odd, sine, cosine)
    second = jnp.where(odd, cosine, sine)
    first = jnp.where((quadrant == 1) | (quadrant == 2), -first, first)
    second = jnp.where(quadrant >= 2, -second, second)
    return first, second


def rotated(x, cosine, sine):
    x = x.astype(jnp.float32)
    return (x * cosine + pltpu.roll(x, 64, 1) * sine).astype(jnp.bfloat16)


def prepare_kernel(pos_ref, inverse_ref, k_ref, v_ref, kv_ref, cos_ref, sin_ref):
    place = jnp.broadcast_to(pos_ref[...].astype(jnp.float32), (HEAD_SIZE, ROWS)).T
    cosine, sine = cos_and_sin(place * inverse_ref[...])
    lane = lax.broadcasted_iota(jnp.int32, (ROWS, HEAD_SIZE), 1)
    sine = jnp.where(lane < HEAD_SIZE // 2, -sine, sine)
    cos_ref[...] = cosine
    sin_ref[...] = sine
    for g in range(KV):
        kv_ref[g, 0] = rotated(k_ref[g], cosine, sine)
        kv_ref[g, 1] = v_ref[g]


def prepare(positions, inverse, k, v):
    payload = jax.ShapeDtypeStruct((KV, 2, ROWS, HEAD_SIZE), jnp.bfloat16)
    table = jax.ShapeDtypeStruct((ROWS, HEAD_SIZE), jnp.float32)
    return pl.pallas_call(
        prepare_kernel,
        in_specs=[VMEM] * 4,
        out_specs=[VMEM] * 3,
        out_shape=[payload, table, table],
        compiler_params=pltpu.CompilerParams(vmem_limit_bytes=8 * 1024 * 1024),
        name="prepare",
    )(positions, inverse, k, v)


def rotate_kernel(q_ref, cos_ref, sin_ref, out_ref):
    for n in range(KV * GROUP):
        part = slice(n * HEAD_SIZE, (n + 1) * HEAD_SIZE)
        out_ref[:, part] = rotated(q_ref[:, part], cos_ref[...], sin_ref[...])


def rotate(q, cosine, sine):
    return pl.pallas_call(
        rotate_kernel,
        in_specs=[VMEM] * 3,
        out_specs=VMEM,
        out_shape=jax.ShapeDtypeStruct(q.shape, q.dtype),
        compiler_params=pltpu.CompilerParams(vmem_limit_bytes=4 * 1024 * 1024),
        name="rotate",
    )(q, cosine, sine)


def dot_nt(a, b):
    return lax.dot_general(a, b, (((1,), (1,)), ((), ())), preferred_element_type=jnp.float32)


def hold_kernel(*refs):
    pass


def held(array, after):
    hbm = pl.BlockSpec(memory_space=pltpu.HBM)
    after = [pltpu.with_memory_space_constraint(x, pltpu.VMEM) for x in after]
    return pl.pallas_call(
        hold_kernel,
        in_specs=[hbm] + [VMEM] * len(after),
        out_specs=hbm,
        out_shape=jax.ShapeDtypeStruct(array.shape, array.dtype),
        input_output_aliases={0: 0},
        compiler_params=pltpu.CompilerParams(vmem_limit_bytes=1024 * 1024),
        name="hold",
    )(array, *after)


def attend_kernel(n, place_ref, q_ref, own_ref, prev_ref, far_ref, out_ref):
    g = n // GROUP
    place = place_ref[0]
    prev_bias = jnp.where(place >= 1, 0.0, LOW)
    far_bias = jnp.where(place >= 2, 0.0, LOW)
    c = SCALE * LOG2E
    k_own, k_prev, k_far = own_ref[g, 0], prev_ref[g, 0], far_ref[g, 0]
    v_own = own_ref[g, 1].T
    v_prev = prev_ref[g, 1].T
    v_far = far_ref[g, 1].T
    row = lax.broadcasted_iota(jnp.int32, (QB, QB), 0)
    col = lax.broadcasted_iota(jnp.int32, (QB, QB), 1)
    seen = row <= col
    blocks = ROWS // QB
    q_all = q_ref[:, n * HEAD_SIZE : (n + 1) * HEAD_SIZE]
    for b in range(blocks):
        q = q_all[b * QB : (b + 1) * QB]
        lo, hi = b * QB, (b + 1) * QB
        prev = dot_nt(k_prev, q)
        own = dot_nt(k_own[0:hi], q)
        far = dot_nt(k_far[lo:ROWS], q)
        mixed = jnp.where(seen, own[lo:hi], far[0:QB] + far_bias)
        top = jnp.maximum(
            jnp.max(prev, axis=0, keepdims=True) + prev_bias,
            jnp.max(mixed, axis=0, keepdims=True),
        )
        if lo > 0:
            top = jnp.maximum(top, jnp.max(own[0:lo], axis=0, keepdims=True))
        if hi < ROWS:
            top = jnp.maximum(top, jnp.max(far[QB:], axis=0, keepdims=True) + far_bias)
        top = top * c
        p_prev = jnp.exp2(prev * c - (top - prev_bias))
        p_mixed = jnp.exp2(mixed * c - top)
        total = jnp.sum(p_prev, axis=0, keepdims=True) + jnp.sum(p_mixed, axis=0, keepdims=True)
        own_parts = [jnp.where(seen, p_mixed, 0.0).astype(jnp.bfloat16)]
        far_parts = [jnp.where(seen, 0.0, p_mixed).astype(jnp.bfloat16)]
        if lo > 0:
            p = jnp.exp2(own[0:lo] * c - top)
            total = total + jnp.sum(p, axis=0, keepdims=True)
            own_parts.insert(0, p.astype(jnp.bfloat16))
        if hi < ROWS:
            p = jnp.exp2(far[QB:] * c - (top - far_bias))
            total = total + jnp.sum(p, axis=0, keepdims=True)
            far_parts.append(p.astype(jnp.bfloat16))
        context = jnp.dot(v_prev, p_prev.astype(jnp.bfloat16), preferred_element_type=jnp.float32)
        context += jnp.dot(
            v_own[:, 0:hi], jnp.concatenate(own_parts, 0), preferred_element_type=jnp.float32
        )
        context += jnp.dot(
            v_far[:, lo:], jnp.concatenate(far_parts, 0), preferred_element_type=jnp.float32
        )
        out_ref[:, lo:hi] = (context / total).astype(jnp.bfloat16)


def attend(n, place, *arrays):
    arrays = [pltpu.with_memory_space_constraint(x, pltpu.VMEM) for x in arrays]
    return pl.pallas_call(
        functools.partial(attend_kernel, n),
        in_specs=[pl.BlockSpec(memory_space=pltpu.SMEM)] + [VMEM] * len(arrays),
        out_specs=VMEM,
        out_shape=jax.ShapeDtypeStruct((PIECE, ROWS), jnp.bfloat16),
        compiler_params=pltpu.CompilerParams(vmem_limit_bytes=16 * 1024 * 1024),
        name="attend",
    )(place, *arrays)


def project_kernel(table_ref, w_ref, *refs):
    ctx_refs = refs[: PIECES * N_HEAD]
    acc_ref, sq_ref, w_buffer, ctx_buffer, w_arrived, ctx_arrived = refs[PIECES * N_HEAD :]
    copies = []
    for k in range(N_HEAD):
        copies.append(
            [
                pltpu.make_async_copy(
                    w_ref.at[table_ref[2 * k + pair]], w_buffer.at[k, pair], w_arrived.at[k, pair]
                )
                for pair in range(2)
            ]
            + [
                pltpu.make_async_copy(
                    ctx_refs[k * PIECES + g],
                    ctx_buffer.at[k, g * PIECE : (g + 1) * PIECE],
                    ctx_arrived.at[k, g],
                )
                for g in range(PIECES)
            ]
        )
        for copy in copies[k]:
            copy.start()
    for k in range(N_HEAD):
        for copy in copies[k]:
            copy.wait()
        value = jnp.dot(
            w_buffer[k].reshape(FEATURES, WIDTH), ctx_buffer[k], preferred_element_type=jnp.float32
        )
        if k > 0:
            value = acc_ref[...] + value
        acc_ref[...] = value
        if k == N_HEAD - 1:
            total = jnp.sum(value * value, axis=0, keepdims=True)
            sq_ref[...] = jnp.broadcast_to(total[None], sq_ref.shape)


def project(table, weights, blocks):
    hbm = pl.BlockSpec(memory_space=pltpu.HBM)
    weights = weights.reshape(SIDE * SIDE, 2, SHARD, WIDTH)
    arrays = [pltpu.with_memory_space_constraint(x, pltpu.HBM) for x in [weights, *blocks]]
    return pl.pallas_call(
        project_kernel,
        in_specs=[pl.BlockSpec(memory_space=pltpu.SMEM)] + [hbm] * len(arrays),
        out_specs=[VMEM, VMEM],
        out_shape=[
            jax.ShapeDtypeStruct((FEATURES, ROWS), jnp.float32),
            jax.ShapeDtypeStruct((N_HEAD, 1, ROWS), jnp.float32),
        ],
        scratch_shapes=[
            pltpu.VMEM((N_HEAD, 2, 2, SHARD, WIDTH), jnp.bfloat16),
            pltpu.VMEM((N_HEAD, WIDTH, ROWS), jnp.bfloat16),
            pltpu.SemaphoreType.DMA((N_HEAD, 2)),
            pltpu.SemaphoreType.DMA((N_HEAD, PIECES)),
        ],
        compiler_params=pltpu.CompilerParams(vmem_limit_bytes=20 * 1024 * 1024),
        name="project",
    )(table, *arrays)


def finish_kernel(acc_ref, sq_ref, gain_ref, res_ref, out_ref):
    squares = jnp.sum(sq_ref[...], axis=0)
    scale = lax.rsqrt(squares / D + EPS)
    value = res_ref[...].astype(jnp.float32) + gain_ref[...] * (acc_ref[...] * scale)
    out_ref[...] = value.astype(jnp.bfloat16)


def finish(attended, squares, gain, residual):
    return pl.pallas_call(
        finish_kernel,
        in_specs=[VMEM] * 4,
        out_shape=jax.ShapeDtypeStruct((FEATURES, ROWS), jnp.bfloat16),
        compiler_params=pltpu.CompilerParams(vmem_limit_bytes=12 * 1024 * 1024),
        name="finish",
    )(attended, squares, gain, residual)


def device(x, y, core, head):
    return ((x % SIDE * SIDE + y % SIDE) * 2 + core) * N_HEAD + head % N_HEAD


def moved(array, rule):
    pairs = [
        (device(x, y, core, head), device(*rule(x, y, core, head)))
        for x in range(SIDE)
        for y in range(SIDE)
        for core in range(2)
        for head in range(N_HEAD)
    ]
    return lax.ppermute(array, ("seq", "head"), pairs)


def sense(core):
    return 1 - 2 * core


def spread(x, y, core, head):
    low = y // 2 * 2
    to_y = low + (1 if y % 2 else -1) - head % 2
    return x + head // 2, to_y, core, 2 * x + y // 2


def on_device(positions, queries, keys, values, out_weight, post_gain, residual):
    seq = lax.axis_index("seq").astype(jnp.int32)
    head = lax.axis_index("head").astype(jnp.int32)
    shard = moved(out_weight.T, spread)

    half = HEAD_SIZE // 2
    inverse = 10000.0 ** (-2.0 * jnp.arange(half, dtype=jnp.float32) / HEAD_SIZE)
    inverse = jnp.concatenate([inverse, inverse])[None]
    own, cosine, sine = prepare(
        positions[None], inverse, keys.transpose(1, 0, 2), values.transpose(1, 0, 2)
    )
    onward = [(i, i + 1) for i in range(N_SEQ - 1)]
    prev = lax.ppermute(own, "seq", onward)
    beyond = [(i, i + 2) for i in range(N_SEQ - 2)]
    far = lax.ppermute(own, "seq", beyond)
    q = rotate(queries.reshape(ROWS, WIDTH), cosine, sine)
    shard = held(shard, after=[prev, far, q])
    weights = lax.all_gather(shard, "seq", axis=0)

    blocks = [[] for _ in range(N_HEAD)]
    place = seq.reshape(1)
    for n in range(PIECES):
        carried = attend(n, place, q, own, prev, far)
        blocks[0].append(carried)
        for k in range(1, N_HEAD):
            carried = moved(carried, lambda x, y, core, head: (x, y, core, head + sense(core)))
            blocks[k].append(carried)

    source = (head - sense(seq % 2) * jnp.arange(N_HEAD, dtype=jnp.int32)) % N_HEAD
    at_x = (head // 2 + source // 2)[:, None] % SIDE
    at_y = (head % 2 * 2 + jnp.array([-1, 1], jnp.int32)[None, :] - source[:, None] % 2) % SIDE
    table = (at_x * SIDE + at_y).reshape(-1).astype(jnp.int32)

    attended, squares = project(table, weights, [x for row in blocks for x in row])
    squares = lax.all_to_all(squares, "head", 0, 0, tiled=True)
    return finish(attended, squares, post_gain[:, None], residual.T).T


def solution(mesh):
    return jax.shard_map(
        on_device,
        mesh=mesh,
        in_specs=(
            P("seq"),
            P("seq", "head", None),
            P("seq", "head", None),
            P("seq", "head", None),
            P("head", "seq"),
            P("head"),
            P("seq", "head"),
        ),
        out_specs=P("seq", "head"),
        check_vma=False,
    )
```

```python
import functools
import math

import jax
import jax.numpy as jnp
from jax import lax
from jax.experimental import pallas as pl
from jax.experimental.pallas import tpu as pltpu
from jax.sharding import PartitionSpec as P

D = 5376
HEAD_SIZE = 128
VISIBLE_SPAN = 1024
EPS = 1e-06
SCALE = 168.0 ** (-0.5)
LOG2E = math.log2(math.e)
ROWS = 512
KV = 2
GROUP = 2
N_SEQ = 32
N_HEAD = 8
FEATURES = D // N_HEAD
SHARD = D // N_SEQ
SIDE = 4
QB = 256
WIDTH = KV * GROUP * HEAD_SIZE
PIECE = 128
PIECES = WIDTH // PIECE
LOW = -1e30
VMEM = pl.BlockSpec(memory_space=pltpu.VMEM)


def cos_and_sin(angle):
    turns = jnp.floor(angle * (2.0 / math.pi) + 0.5)
    x = angle - turns * 1.5703125
    x = x - turns * 4.8351287841796875e-4
    x = x - turns * 3.1385570764541626e-07
    x = x - turns * 6.0771005065061922e-11
    z = x * x
    sine = ((-1.9515295891e-4 * z + 8.3321608736e-3) * z - 1.6666654611e-1) * z * x + x
    cosine = ((2.443315711809948e-5 * z - 1.388731625493765e-3) * z + 4.166664568298827e-2) * z * z
    cosine = cosine - 0.5 * z + 1.0
    quadrant = turns.astype(jnp.int32) & 3
    odd = (quadrant & 1) == 1
    first = jnp.where(odd, sine, cosine)
    second = jnp.where(odd, cosine, sine)
    first = jnp.where((quadrant == 1) | (quadrant == 2), -first, first)
    second = jnp.where(quadrant >= 2, -second, second)
    return first, second


def rotated(x, cosine, sine):
    x = x.astype(jnp.float32)
    return (x * cosine + pltpu.roll(x, 64, 1) * sine).astype(jnp.bfloat16)


def prepare_kernel(pos_ref, inverse_ref, k_ref, v_ref, kv_ref, cos_ref, sin_ref):
    place = jnp.broadcast_to(pos_ref[...].astype(jnp.float32), (HEAD_SIZE, ROWS)).T
    cosine, sine = cos_and_sin(place * inverse_ref[...])
    lane = lax.broadcasted_iota(jnp.int32, (ROWS, HEAD_SIZE), 1)
    sine = jnp.where(lane < HEAD_SIZE // 2, -sine, sine)
    cos_ref[...] = cosine
    sin_ref[...] = sine
    for g in range(KV):
        kv_ref[g, 0] = rotated(k_ref[g], cosine, sine)
        kv_ref[g, 1] = v_ref[g]


def prepare(positions, inverse, k, v):
    payload = jax.ShapeDtypeStruct((KV, 2, ROWS, HEAD_SIZE), jnp.bfloat16)
    table = jax.ShapeDtypeStruct((ROWS, HEAD_SIZE), jnp.float32)
    return pl.pallas_call(
        prepare_kernel,
        in_specs=[VMEM] * 4,
        out_specs=[VMEM] * 3,
        out_shape=[payload, table, table],
        compiler_params=pltpu.CompilerParams(vmem_limit_bytes=8 * 1024 * 1024),
        name="prepare",
    )(positions, inverse, k, v)


def rotate_kernel(q_ref, cos_ref, sin_ref, out_ref):
    for n in range(KV * GROUP):
        part = slice(n * HEAD_SIZE, (n + 1) * HEAD_SIZE)
        out_ref[:, part] = rotated(q_ref[:, part], cos_ref[...], sin_ref[...])


def rotate(q, cosine, sine):
    return pl.pallas_call(
        rotate_kernel,
        in_specs=[VMEM] * 3,
        out_specs=VMEM,
        out_shape=jax.ShapeDtypeStruct(q.shape, q.dtype),
        compiler_params=pltpu.CompilerParams(vmem_limit_bytes=4 * 1024 * 1024),
        name="rotate",
    )(q, cosine, sine)


def dot_nt(a, b):
    return lax.dot_general(a, b, (((1,), (1,)), ((), ())), preferred_element_type=jnp.float32)


def hold_kernel(*refs):
    pass


def held(array, other, after):
    hbm = pl.BlockSpec(memory_space=pltpu.HBM)
    other, *after = [pltpu.with_memory_space_constraint(x, pltpu.VMEM) for x in [other, *after]]
    return pl.pallas_call(
        hold_kernel,
        in_specs=[hbm, VMEM] + [VMEM] * len(after),
        out_specs=[hbm, VMEM],
        out_shape=[jax.ShapeDtypeStruct(x.shape, x.dtype) for x in [array, other]],
        input_output_aliases={0: 0, 1: 1},
        compiler_params=pltpu.CompilerParams(vmem_limit_bytes=1024 * 1024),
        name="hold",
    )(array, other, *after)


def attend_kernel(n, place_ref, q_ref, own_ref, prev_ref, far_ref, out_ref):
    g = n // GROUP
    place = place_ref[0]
    prev_bias = jnp.where(place >= 1, 0.0, LOW)
    far_bias = jnp.where(place >= 2, 0.0, LOW)
    c = SCALE * LOG2E
    k_own, k_prev, k_far = own_ref[g, 0], prev_ref[g, 0], far_ref[g, 0]
    v_own = own_ref[g, 1].T
    v_prev = prev_ref[g, 1].T
    v_far = far_ref[g, 1].T
    row = lax.broadcasted_iota(jnp.int32, (QB, QB), 0)
    col = lax.broadcasted_iota(jnp.int32, (QB, QB), 1)
    seen = row <= col
    blocks = ROWS // QB
    q_all = q_ref[:, n * HEAD_SIZE : (n + 1) * HEAD_SIZE]
    for b in range(blocks):
        q = q_all[b * QB : (b + 1) * QB]
        lo, hi = b * QB, (b + 1) * QB
        prev = dot_nt(k_prev, q)
        own = dot_nt(k_own[0:hi], q)
        far = dot_nt(k_far[lo:ROWS], q)
        mixed = jnp.where(seen, own[lo:hi], far[0:QB] + far_bias)
        top = jnp.maximum(
            jnp.max(prev, axis=0, keepdims=True) + prev_bias,
            jnp.max(mixed, axis=0, keepdims=True),
        )
        if lo > 0:
            top = jnp.maximum(top, jnp.max(own[0:lo], axis=0, keepdims=True))
        if hi < ROWS:
            top = jnp.maximum(top, jnp.max(far[QB:], axis=0, keepdims=True) + far_bias)
        top = top * c
        p_prev = jnp.exp2(prev * c - (top - prev_bias))
        p_mixed = jnp.exp2(mixed * c - top)
        total = jnp.sum(p_prev, axis=0, keepdims=True) + jnp.sum(p_mixed, axis=0, keepdims=True)
        own_parts = [jnp.where(seen, p_mixed, 0.0).astype(jnp.bfloat16)]
        far_parts = [jnp.where(seen, 0.0, p_mixed).astype(jnp.bfloat16)]
        if lo > 0:
            p = jnp.exp2(own[0:lo] * c - top)
            total = total + jnp.sum(p, axis=0, keepdims=True)
            own_parts.insert(0, p.astype(jnp.bfloat16))
        if hi < ROWS:
            p = jnp.exp2(far[QB:] * c - (top - far_bias))
            total = total + jnp.sum(p, axis=0, keepdims=True)
            far_parts.append(p.astype(jnp.bfloat16))
        context = jnp.dot(v_prev, p_prev.astype(jnp.bfloat16), preferred_element_type=jnp.float32)
        context += jnp.dot(
            v_own[:, 0:hi], jnp.concatenate(own_parts, 0), preferred_element_type=jnp.float32
        )
        context += jnp.dot(
            v_far[:, lo:], jnp.concatenate(far_parts, 0), preferred_element_type=jnp.float32
        )
        out_ref[:, lo:hi] = (context / total).astype(jnp.bfloat16)


def attend(n, place, *arrays):
    arrays = [pltpu.with_memory_space_constraint(x, pltpu.VMEM) for x in arrays]
    return pl.pallas_call(
        functools.partial(attend_kernel, n),
        in_specs=[pl.BlockSpec(memory_space=pltpu.SMEM)] + [VMEM] * len(arrays),
        out_specs=VMEM,
        out_shape=jax.ShapeDtypeStruct((PIECE, ROWS), jnp.bfloat16),
        compiler_params=pltpu.CompilerParams(vmem_limit_bytes=16 * 1024 * 1024),
        name="attend",
    )(place, *arrays)


def project_kernel(order_ref, w_ref, *refs):
    ctx_refs = refs[: PIECES * N_HEAD]
    acc_ref, sq_ref, w_buffer, ctx_buffer, arrived = refs[PIECES * N_HEAD :]
    copies = []
    for k in range(N_HEAD):
        copies.append(
            [pltpu.make_async_copy(w_ref.at[order_ref[k]], w_buffer.at[k], arrived.at[k, PIECES])]
            + [
                pltpu.make_async_copy(
                    ctx_refs[k * PIECES + g],
                    ctx_buffer.at[k, g * PIECE : (g + 1) * PIECE],
                    arrived.at[k, g],
                )
                for g in range(PIECES)
            ]
        )
        for copy in copies[k]:
            copy.start()
    for k in range(N_HEAD):
        for copy in copies[k]:
            copy.wait()
        value = jnp.dot(w_buffer[k], ctx_buffer[k], preferred_element_type=jnp.float32)
        if k > 0:
            value = acc_ref[...] + value
        acc_ref[...] = value
        if k == N_HEAD - 1:
            total = jnp.sum(value * value, axis=0, keepdims=True)
            sq_ref[...] = jnp.broadcast_to(total[None], sq_ref.shape)


def project(order, weights, blocks):
    hbm = pl.BlockSpec(memory_space=pltpu.HBM)
    arrays = [pltpu.with_memory_space_constraint(x, pltpu.HBM) for x in [weights, *blocks]]
    return pl.pallas_call(
        project_kernel,
        in_specs=[pl.BlockSpec(memory_space=pltpu.SMEM)] + [hbm] * len(arrays),
        out_specs=[VMEM, VMEM],
        out_shape=[
            jax.ShapeDtypeStruct((FEATURES, ROWS), jnp.float32),
            jax.ShapeDtypeStruct((N_HEAD, 1, ROWS), jnp.float32),
        ],
        scratch_shapes=[
            pltpu.VMEM((N_HEAD, FEATURES, WIDTH), jnp.bfloat16),
            pltpu.VMEM((N_HEAD, WIDTH, ROWS), jnp.bfloat16),
            pltpu.SemaphoreType.DMA((N_HEAD, PIECES + 1)),
        ],
        compiler_params=pltpu.CompilerParams(vmem_limit_bytes=20 * 1024 * 1024),
        name="project",
    )(order, *arrays)


def finish_kernel(acc_ref, sq_ref, gain_ref, res_ref, out_ref):
    squares = jnp.sum(sq_ref[...], axis=0)
    scale = lax.rsqrt(squares / D + EPS)
    value = res_ref[...].astype(jnp.float32) + gain_ref[...] * (acc_ref[...] * scale)
    out_ref[...] = value.astype(jnp.bfloat16)


def finish(attended, squares, gain, residual):
    return pl.pallas_call(
        finish_kernel,
        in_specs=[VMEM] * 4,
        out_shape=jax.ShapeDtypeStruct((FEATURES, ROWS), jnp.bfloat16),
        compiler_params=pltpu.CompilerParams(vmem_limit_bytes=12 * 1024 * 1024),
        name="finish",
    )(attended, squares, gain, residual)


def device(x, y, core, head):
    return ((x % SIDE * SIDE + y % SIDE) * 2 + core) * N_HEAD + head % N_HEAD


def moved(array, rule):
    pairs = [
        (device(x, y, core, head), device(*rule(x, y, core, head)))
        for x in range(SIDE)
        for y in range(SIDE)
        for core in range(2)
        for head in range(N_HEAD)
    ]
    return lax.ppermute(array, ("seq", "head"), pairs)


def sense(core):
    return 1 - 2 * core


def spread(x, y, core, head):
    feature = 2 * x + y // 2
    group = (feature + head) % N_HEAD
    return group // 2, group % 2 * 2 + y % 2, core, feature


def on_device(positions, queries, keys, values, out_weight, post_gain, residual):
    seq = lax.axis_index("seq").astype(jnp.int32)
    head = lax.axis_index("head").astype(jnp.int32)
    shard = moved(out_weight.T, spread)

    half = HEAD_SIZE // 2
    inverse = 10000.0 ** (-2.0 * jnp.arange(half, dtype=jnp.float32) / HEAD_SIZE)
    inverse = jnp.concatenate([inverse, inverse])[None]
    own, cosine, sine = prepare(
        positions[None], inverse, keys.transpose(1, 0, 2), values.transpose(1, 0, 2)
    )
    far = lax.ppermute(own, "seq", [(i, i + 2) for i in range(N_SEQ - 2)])
    q = rotate(queries.reshape(ROWS, WIDTH), cosine, sine)
    shard, far = held(shard, far, after=[q])
    given = jnp.where(seq % 2 == 0, own, far)
    prev = lax.ppermute(given, "seq", [(i, i ^ 1) for i in range(N_SEQ)])
    weights = lax.all_gather(shard, "seq", axis=0).reshape(N_HEAD, FEATURES, WIDTH)

    blocks = [[] for _ in range(N_HEAD)]
    place = seq.reshape(1)
    for n in range(PIECES):
        carried = attend(n, place, q, own, prev, far)
        blocks[0].append(carried)
        for k in range(1, N_HEAD):
            carried = moved(carried, lambda x, y, core, head: (x, y, core, head + sense(core)))
            blocks[k].append(carried)

    source = head - sense(seq % 2) * jnp.arange(N_HEAD, dtype=jnp.int32)
    order = ((source + head) % N_HEAD).astype(jnp.int32)
    attended, squares = project(order, weights, [x for row in blocks for x in row])
    squares = lax.all_to_all(squares, "head", 0, 0, tiled=True)
    return finish(attended, squares, post_gain[:, None], residual.T).T


def solution(mesh):
    return jax.shard_map(
        on_device,
        mesh=mesh,
        in_specs=(
            P("seq"),
            P("seq", "head", None),
            P("seq", "head", None),
            P("seq", "head", None),
            P("head", "seq"),
            P("head"),
            P("seq", "head"),
        ),
        out_specs=P("seq", "head"),
        check_vma=False,
    )
```

```python
import functools
import math

import jax
import jax.numpy as jnp
from jax import lax
from jax.experimental import pallas as pl
from jax.experimental.pallas import tpu as pltpu
from jax.sharding import PartitionSpec as P

D = 5376
HEAD_SIZE = 128
VISIBLE_SPAN = 1024
EPS = 1e-06
SCALE = 168.0 ** (-0.5)
LOG2E = math.log2(math.e)
ROWS = 512
KV = 2
GROUP = 2
N_SEQ = 32
N_HEAD = 8
FEATURES = D // N_HEAD
SHARD = D // N_SEQ
SIDE = 4
QB = 256
WIDTH = KV * GROUP * HEAD_SIZE
PIECE = 128
PIECES = WIDTH // PIECE
LOW = -1e30
VMEM = pl.BlockSpec(memory_space=pltpu.VMEM)


def cos_and_sin(angle):
    turns = jnp.floor(angle * (2.0 / math.pi) + 0.5)
    x = angle - turns * 1.5703125
    x = x - turns * 4.8351287841796875e-4
    x = x - turns * 3.1385570764541626e-07
    x = x - turns * 6.0771005065061922e-11
    z = x * x
    sine = ((-1.9515295891e-4 * z + 8.3321608736e-3) * z - 1.6666654611e-1) * z * x + x
    cosine = ((2.443315711809948e-5 * z - 1.388731625493765e-3) * z + 4.166664568298827e-2) * z * z
    cosine = cosine - 0.5 * z + 1.0
    quadrant = turns.astype(jnp.int32) & 3
    odd = (quadrant & 1) == 1
    first = jnp.where(odd, sine, cosine)
    second = jnp.where(odd, cosine, sine)
    first = jnp.where((quadrant == 1) | (quadrant == 2), -first, first)
    second = jnp.where(quadrant >= 2, -second, second)
    return first, second


def rotated(x, cosine, sine):
    x = x.astype(jnp.float32)
    return (x * cosine + pltpu.roll(x, 64, 1) * sine).astype(jnp.bfloat16)


def prepare_kernel(pos_ref, inverse_ref, k_ref, v_ref, kv_ref, cos_ref, sin_ref):
    place = jnp.broadcast_to(pos_ref[...].astype(jnp.float32), (HEAD_SIZE, ROWS)).T
    cosine, sine = cos_and_sin(place * inverse_ref[...])
    lane = lax.broadcasted_iota(jnp.int32, (ROWS, HEAD_SIZE), 1)
    sine = jnp.where(lane < HEAD_SIZE // 2, -sine, sine)
    cos_ref[...] = cosine
    sin_ref[...] = sine
    for g in range(KV):
        kv_ref[g, 0] = rotated(k_ref[g], cosine, sine)
        kv_ref[g, 1] = v_ref[g]


def prepare(positions, inverse, k, v):
    payload = jax.ShapeDtypeStruct((KV, 2, ROWS, HEAD_SIZE), jnp.bfloat16)
    table = jax.ShapeDtypeStruct((ROWS, HEAD_SIZE), jnp.float32)
    return pl.pallas_call(
        prepare_kernel,
        in_specs=[VMEM] * 4,
        out_specs=[VMEM] * 3,
        out_shape=[payload, table, table],
        compiler_params=pltpu.CompilerParams(vmem_limit_bytes=8 * 1024 * 1024),
        name="prepare",
    )(positions, inverse, k, v)


def rotate_kernel(q_ref, cos_ref, sin_ref, out_ref):
    for n in range(KV * GROUP):
        part = slice(n * HEAD_SIZE, (n + 1) * HEAD_SIZE)
        out_ref[:, part] = rotated(q_ref[:, part], cos_ref[...], sin_ref[...])


def rotate(q, cosine, sine):
    return pl.pallas_call(
        rotate_kernel,
        in_specs=[VMEM] * 3,
        out_specs=VMEM,
        out_shape=jax.ShapeDtypeStruct(q.shape, q.dtype),
        compiler_params=pltpu.CompilerParams(vmem_limit_bytes=4 * 1024 * 1024),
        name="rotate",
    )(q, cosine, sine)


def dot_nt(a, b):
    return lax.dot_general(a, b, (((1,), (1,)), ((), ())), preferred_element_type=jnp.float32)


def hold_kernel(*refs):
    pass


def held(array, after):
    hbm = pl.BlockSpec(memory_space=pltpu.HBM)
    after = [pltpu.with_memory_space_constraint(x, pltpu.VMEM) for x in after]
    return pl.pallas_call(
        hold_kernel,
        in_specs=[hbm] + [VMEM] * len(after),
        out_specs=hbm,
        out_shape=jax.ShapeDtypeStruct(array.shape, array.dtype),
        input_output_aliases={0: 0},
        compiler_params=pltpu.CompilerParams(vmem_limit_bytes=1024 * 1024),
        name="hold",
    )(array, *after)


def attend_kernel(place_ref, q_ref, own_ref, prev_ref, far_ref, *out_refs):
    place = place_ref[0]
    prev_bias = jnp.where(place >= 1, 0.0, LOW)
    far_bias = jnp.where(place >= 2, 0.0, LOW)
    c = SCALE * LOG2E
    row = lax.broadcasted_iota(jnp.int32, (QB, QB), 0)
    col = lax.broadcasted_iota(jnp.int32, (QB, QB), 1)
    seen = row <= col
    blocks = ROWS // QB
    for n in range(PIECES):
        g = n // GROUP
        k_own, k_prev, k_far = own_ref[g, 0], prev_ref[g, 0], far_ref[g, 0]
        v_own = own_ref[g, 1].T
        v_prev = prev_ref[g, 1].T
        v_far = far_ref[g, 1].T
        q_all = q_ref[:, n * HEAD_SIZE : (n + 1) * HEAD_SIZE]
        for b in range(blocks):
            q = q_all[b * QB : (b + 1) * QB]
            lo, hi = b * QB, (b + 1) * QB
            prev = dot_nt(k_prev, q)
            own = dot_nt(k_own[0:hi], q)
            far = dot_nt(k_far[lo:ROWS], q)
            mixed = jnp.where(seen, own[lo:hi], far[0:QB] + far_bias)
            top = jnp.maximum(
                jnp.max(prev, axis=0, keepdims=True) + prev_bias,
                jnp.max(mixed, axis=0, keepdims=True),
            )
            if lo > 0:
                top = jnp.maximum(top, jnp.max(own[0:lo], axis=0, keepdims=True))
            if hi < ROWS:
                top = jnp.maximum(top, jnp.max(far[QB:], axis=0, keepdims=True) + far_bias)
            top = top * c
            p_prev = jnp.exp2(prev * c - (top - prev_bias))
            p_mixed = jnp.exp2(mixed * c - top)
            total = jnp.sum(p_prev, axis=0, keepdims=True) + jnp.sum(p_mixed, axis=0, keepdims=True)
            own_parts = [jnp.where(seen, p_mixed, 0.0).astype(jnp.bfloat16)]
            far_parts = [jnp.where(seen, 0.0, p_mixed).astype(jnp.bfloat16)]
            if lo > 0:
                p = jnp.exp2(own[0:lo] * c - top)
                total = total + jnp.sum(p, axis=0, keepdims=True)
                own_parts.insert(0, p.astype(jnp.bfloat16))
            if hi < ROWS:
                p = jnp.exp2(far[QB:] * c - (top - far_bias))
                total = total + jnp.sum(p, axis=0, keepdims=True)
                far_parts.append(p.astype(jnp.bfloat16))
            context = jnp.dot(v_prev, p_prev.astype(jnp.bfloat16), preferred_element_type=jnp.float32)
            context += jnp.dot(
                v_own[:, 0:hi], jnp.concatenate(own_parts, 0), preferred_element_type=jnp.float32
            )
            context += jnp.dot(
                v_far[:, lo:], jnp.concatenate(far_parts, 0), preferred_element_type=jnp.float32
            )
            out_refs[n][:, lo:hi] = (context / total).astype(jnp.bfloat16)


def attend(place, *arrays):
    arrays = [pltpu.with_memory_space_constraint(x, pltpu.VMEM) for x in arrays]
    return pl.pallas_call(
        attend_kernel,
        in_specs=[pl.BlockSpec(memory_space=pltpu.SMEM)] + [VMEM] * len(arrays),
        out_specs=[VMEM] * PIECES,
        out_shape=[jax.ShapeDtypeStruct((PIECE, ROWS), jnp.bfloat16)] * PIECES,
        compiler_params=pltpu.CompilerParams(vmem_limit_bytes=16 * 1024 * 1024),
        name="attend",
    )(place, *arrays)


def project_kernel(order_ref, w_ref, *refs):
    ctx_refs = refs[: PIECES * N_HEAD]
    acc_ref, sq_ref, w_buffer, ctx_buffer, arrived = refs[PIECES * N_HEAD :]
    copies = []
    for k in range(N_HEAD):
        copies.append(
            [pltpu.make_async_copy(w_ref.at[order_ref[k]], w_buffer.at[k], arrived.at[k, PIECES])]
            + [
                pltpu.make_async_copy(
                    ctx_refs[k * PIECES + g],
                    ctx_buffer.at[k, g * PIECE : (g + 1) * PIECE],
                    arrived.at[k, g],
                )
                for g in range(PIECES)
            ]
        )
        for copy in copies[k]:
            copy.start()
    for k in range(N_HEAD):
        for copy in copies[k]:
            copy.wait()
        value = jnp.dot(w_buffer[k], ctx_buffer[k], preferred_element_type=jnp.float32)
        if k > 0:
            value = acc_ref[...] + value
        acc_ref[...] = value
        if k == N_HEAD - 1:
            total = jnp.sum(value * value, axis=0, keepdims=True)
            sq_ref[...] = jnp.broadcast_to(total[None], sq_ref.shape)


def project(order, weights, blocks):
    hbm = pl.BlockSpec(memory_space=pltpu.HBM)
    arrays = [pltpu.with_memory_space_constraint(x, pltpu.HBM) for x in [weights, *blocks]]
    return pl.pallas_call(
        project_kernel,
        in_specs=[pl.BlockSpec(memory_space=pltpu.SMEM)] + [hbm] * len(arrays),
        out_specs=[VMEM, VMEM],
        out_shape=[
            jax.ShapeDtypeStruct((FEATURES, ROWS), jnp.float32),
            jax.ShapeDtypeStruct((N_HEAD, 1, ROWS), jnp.float32),
        ],
        scratch_shapes=[
            pltpu.VMEM((N_HEAD, FEATURES, WIDTH), jnp.bfloat16),
            pltpu.VMEM((N_HEAD, WIDTH, ROWS), jnp.bfloat16),
            pltpu.SemaphoreType.DMA((N_HEAD, PIECES + 1)),
        ],
        compiler_params=pltpu.CompilerParams(vmem_limit_bytes=20 * 1024 * 1024),
        name="project",
    )(order, *arrays)


def finish_kernel(acc_ref, sq_ref, gain_ref, res_ref, out_ref):
    squares = jnp.sum(sq_ref[...], axis=0)
    scale = lax.rsqrt(squares / D + EPS)
    value = res_ref[...].astype(jnp.float32) + gain_ref[...] * (acc_ref[...] * scale)
    out_ref[...] = value.astype(jnp.bfloat16)


def finish(attended, squares, gain, residual):
    return pl.pallas_call(
        finish_kernel,
        in_specs=[VMEM] * 4,
        out_shape=jax.ShapeDtypeStruct((FEATURES, ROWS), jnp.bfloat16),
        compiler_params=pltpu.CompilerParams(vmem_limit_bytes=12 * 1024 * 1024),
        name="finish",
    )(attended, squares, gain, residual)


def device(x, y, core, head):
    return ((x % SIDE * SIDE + y % SIDE) * 2 + core) * N_HEAD + head % N_HEAD


def moved(array, rule):
    pairs = [
        (device(x, y, core, head), device(*rule(x, y, core, head)))
        for x in range(SIDE)
        for y in range(SIDE)
        for core in range(2)
        for head in range(N_HEAD)
    ]
    return lax.ppermute(array, ("seq", "head"), pairs)


def sense(core):
    return 1 - 2 * core


def spread(x, y, core, head):
    feature = 2 * x + y // 2
    group = (feature + head) % N_HEAD
    return group // 2, group % 2 * 2 + y % 2, core, feature


def on_device(positions, queries, keys, values, out_weight, post_gain, residual):
    seq = lax.axis_index("seq").astype(jnp.int32)
    head = lax.axis_index("head").astype(jnp.int32)
    shard = moved(out_weight.T, spread)

    half = HEAD_SIZE // 2
    inverse = 10000.0 ** (-2.0 * jnp.arange(half, dtype=jnp.float32) / HEAD_SIZE)
    inverse = jnp.concatenate([inverse, inverse])[None]
    own, cosine, sine = prepare(
        positions[None], inverse, keys.transpose(1, 0, 2), values.transpose(1, 0, 2)
    )
    prev = lax.ppermute(own, "seq", [(i, i + 1) for i in range(N_SEQ - 1)])
    far = lax.ppermute(own, "seq", [(i, i + 2) for i in range(N_SEQ - 2)])
    q = rotate(queries.reshape(ROWS, WIDTH), cosine, sine)

    blocks = [[] for _ in range(N_HEAD)]
    place = seq.reshape(1)
    for carried in attend(place, q, own, prev, far):
        blocks[0].append(carried)
        for k in range(1, N_HEAD):
            carried = moved(carried, lambda x, y, core, head: (x, y, core, head + sense(core)))
            blocks[k].append(carried)

    shard = held(shard, after=blocks[0])
    weights = lax.all_gather(shard, "seq", axis=0).reshape(N_HEAD, FEATURES, WIDTH)
    source = head - sense(seq % 2) * jnp.arange(N_HEAD, dtype=jnp.int32)
    order = ((source + head) % N_HEAD).astype(jnp.int32)
    attended, squares = project(order, weights, [x for row in blocks for x in row])
    squares = lax.all_to_all(squares, "head", 0, 0, tiled=True)
    return finish(attended, squares, post_gain[:, None], residual.T).T


def solution(mesh):
    return jax.shard_map(
        on_device,
        mesh=mesh,
        in_specs=(
            P("seq"),
            P("seq", "head", None),
            P("seq", "head", None),
            P("seq", "head", None),
            P("head", "seq"),
            P("head"),
            P("seq", "head"),
        ),
        out_specs=P("seq", "head"),
        check_vma=False,
    )
```

```python
import functools
import math

import jax
import jax.numpy as jnp
from jax import lax
from jax.experimental import pallas as pl
from jax.experimental.pallas import tpu as pltpu
from jax.sharding import PartitionSpec as P

D = 5376
HEAD_SIZE = 128
VISIBLE_SPAN = 1024
EPS = 1e-06
SCALE = 168.0 ** (-0.5)
LOG2E = math.log2(math.e)
ROWS = 512
KV = 2
GROUP = 2
N_SEQ = 32
N_HEAD = 8
FEATURES = D // N_HEAD
SHARD = D // N_SEQ
SIDE = 4
QB = 256
WIDTH = KV * GROUP * HEAD_SIZE
PIECE = 128
PIECES = WIDTH // PIECE
LOW = -1e30
VMEM = pl.BlockSpec(memory_space=pltpu.VMEM)


def cos_and_sin(angle):
    turns = jnp.floor(angle * (2.0 / math.pi) + 0.5)
    x = angle - turns * 1.5703125
    x = x - turns * 4.8351287841796875e-4
    x = x - turns * 3.1385570764541626e-07
    x = x - turns * 6.0771005065061922e-11
    z = x * x
    sine = ((-1.9515295891e-4 * z + 8.3321608736e-3) * z - 1.6666654611e-1) * z * x + x
    cosine = ((2.443315711809948e-5 * z - 1.388731625493765e-3) * z + 4.166664568298827e-2) * z * z
    cosine = cosine - 0.5 * z + 1.0
    quadrant = turns.astype(jnp.int32) & 3
    odd = (quadrant & 1) == 1
    first = jnp.where(odd, sine, cosine)
    second = jnp.where(odd, cosine, sine)
    first = jnp.where((quadrant == 1) | (quadrant == 2), -first, first)
    second = jnp.where(quadrant >= 2, -second, second)
    return first, second


def rotated(x, cosine, sine):
    x = x.astype(jnp.float32)
    return (x * cosine + pltpu.roll(x, 64, 1) * sine).astype(jnp.bfloat16)


def prepare_kernel(pos_ref, inverse_ref, k_ref, v_ref, kv_ref, cos_ref, sin_ref):
    place = jnp.broadcast_to(pos_ref[...].astype(jnp.float32), (HEAD_SIZE, ROWS)).T
    cosine, sine = cos_and_sin(place * inverse_ref[...])
    lane = lax.broadcasted_iota(jnp.int32, (ROWS, HEAD_SIZE), 1)
    sine = jnp.where(lane < HEAD_SIZE // 2, -sine, sine)
    cos_ref[...] = cosine
    sin_ref[...] = sine
    for g in range(KV):
        kv_ref[g, 0] = rotated(k_ref[g], cosine, sine)
        kv_ref[g, 1] = v_ref[g]


def prepare(positions, inverse, k, v):
    payload = jax.ShapeDtypeStruct((KV, 2, ROWS, HEAD_SIZE), jnp.bfloat16)
    table = jax.ShapeDtypeStruct((ROWS, HEAD_SIZE), jnp.float32)
    return pl.pallas_call(
        prepare_kernel,
        in_specs=[VMEM] * 4,
        out_specs=[VMEM] * 3,
        out_shape=[payload, table, table],
        compiler_params=pltpu.CompilerParams(vmem_limit_bytes=8 * 1024 * 1024),
        name="prepare",
    )(positions, inverse, k, v)


def rotate_kernel(q_ref, cos_ref, sin_ref, out_ref):
    for n in range(KV * GROUP):
        part = slice(n * HEAD_SIZE, (n + 1) * HEAD_SIZE)
        out_ref[:, part] = rotated(q_ref[:, part], cos_ref[...], sin_ref[...])


def rotate(q, cosine, sine):
    return pl.pallas_call(
        rotate_kernel,
        in_specs=[VMEM] * 3,
        out_specs=VMEM,
        out_shape=jax.ShapeDtypeStruct(q.shape, q.dtype),
        compiler_params=pltpu.CompilerParams(vmem_limit_bytes=4 * 1024 * 1024),
        name="rotate",
    )(q, cosine, sine)


def dot_nt(a, b):
    return lax.dot_general(a, b, (((1,), (1,)), ((), ())), preferred_element_type=jnp.float32)


def hold_kernel(*refs):
    pass


def held(array, other, after):
    hbm = pl.BlockSpec(memory_space=pltpu.HBM)
    other, *after = [pltpu.with_memory_space_constraint(x, pltpu.VMEM) for x in [other, *after]]
    return pl.pallas_call(
        hold_kernel,
        in_specs=[hbm, VMEM] + [VMEM] * len(after),
        out_specs=[hbm, VMEM],
        out_shape=[jax.ShapeDtypeStruct(x.shape, x.dtype) for x in [array, other]],
        input_output_aliases={0: 0, 1: 1},
        compiler_params=pltpu.CompilerParams(vmem_limit_bytes=1024 * 1024),
        name="hold",
    )(array, other, *after)


def attend_kernel(place_ref, q_ref, own_ref, prev_ref, far_ref, *out_refs):
    place = place_ref[0]
    prev_bias = jnp.where(place >= 1, 0.0, LOW)
    far_bias = jnp.where(place >= 2, 0.0, LOW)
    c = SCALE * LOG2E
    row = lax.broadcasted_iota(jnp.int32, (QB, QB), 0)
    col = lax.broadcasted_iota(jnp.int32, (QB, QB), 1)
    seen = row <= col
    blocks = ROWS // QB
    for n in range(PIECES):
        g = n // GROUP
        k_own, k_prev, k_far = own_ref[g, 0], prev_ref[g, 0], far_ref[g, 0]
        v_own = own_ref[g, 1].T
        v_prev = prev_ref[g, 1].T
        v_far = far_ref[g, 1].T
        q_all = q_ref[:, n * HEAD_SIZE : (n + 1) * HEAD_SIZE]
        for b in range(blocks):
            q = q_all[b * QB : (b + 1) * QB]
            lo, hi = b * QB, (b + 1) * QB
            prev = dot_nt(k_prev, q)
            own = dot_nt(k_own[0:hi], q)
            far = dot_nt(k_far[lo:ROWS], q)
            mixed = jnp.where(seen, own[lo:hi], far[0:QB] + far_bias)
            top = jnp.maximum(
                jnp.max(prev, axis=0, keepdims=True) + prev_bias,
                jnp.max(mixed, axis=0, keepdims=True),
            )
            if lo > 0:
                top = jnp.maximum(top, jnp.max(own[0:lo], axis=0, keepdims=True))
            if hi < ROWS:
                top = jnp.maximum(top, jnp.max(far[QB:], axis=0, keepdims=True) + far_bias)
            top = top * c
            p_prev = jnp.exp2(prev * c - (top - prev_bias))
            p_mixed = jnp.exp2(mixed * c - top)
            total = jnp.sum(p_prev, axis=0, keepdims=True) + jnp.sum(p_mixed, axis=0, keepdims=True)
            own_parts = [jnp.where(seen, p_mixed, 0.0).astype(jnp.bfloat16)]
            far_parts = [jnp.where(seen, 0.0, p_mixed).astype(jnp.bfloat16)]
            if lo > 0:
                p = jnp.exp2(own[0:lo] * c - top)
                total = total + jnp.sum(p, axis=0, keepdims=True)
                own_parts.insert(0, p.astype(jnp.bfloat16))
            if hi < ROWS:
                p = jnp.exp2(far[QB:] * c - (top - far_bias))
                total = total + jnp.sum(p, axis=0, keepdims=True)
                far_parts.append(p.astype(jnp.bfloat16))
            context = jnp.dot(v_prev, p_prev.astype(jnp.bfloat16), preferred_element_type=jnp.float32)
            context += jnp.dot(
                v_own[:, 0:hi], jnp.concatenate(own_parts, 0), preferred_element_type=jnp.float32
            )
            context += jnp.dot(
                v_far[:, lo:], jnp.concatenate(far_parts, 0), preferred_element_type=jnp.float32
            )
            out_refs[n][:, lo:hi] = (context / total).astype(jnp.bfloat16)


def attend(place, *arrays):
    arrays = [pltpu.with_memory_space_constraint(x, pltpu.VMEM) for x in arrays]
    return pl.pallas_call(
        attend_kernel,
        in_specs=[pl.BlockSpec(memory_space=pltpu.SMEM)] + [VMEM] * len(arrays),
        out_specs=[VMEM] * PIECES,
        out_shape=[jax.ShapeDtypeStruct((PIECE, ROWS), jnp.bfloat16)] * PIECES,
        compiler_params=pltpu.CompilerParams(vmem_limit_bytes=16 * 1024 * 1024),
        name="attend",
    )(place, *arrays)


def project_kernel(order_ref, w_ref, *refs):
    ctx_refs = refs[: PIECES * N_HEAD]
    acc_ref, sq_ref, w_buffer, ctx_buffer, arrived = refs[PIECES * N_HEAD :]
    copies = []
    for k in range(N_HEAD):
        copies.append(
            [pltpu.make_async_copy(w_ref.at[order_ref[k]], w_buffer.at[k], arrived.at[k, PIECES])]
            + [
                pltpu.make_async_copy(
                    ctx_refs[k * PIECES + g],
                    ctx_buffer.at[k, g * PIECE : (g + 1) * PIECE],
                    arrived.at[k, g],
                )
                for g in range(PIECES)
            ]
        )
        for copy in copies[k]:
            copy.start()
    for k in range(N_HEAD):
        for copy in copies[k]:
            copy.wait()
        value = jnp.dot(w_buffer[k], ctx_buffer[k], preferred_element_type=jnp.float32)
        if k > 0:
            value = acc_ref[...] + value
        acc_ref[...] = value
        if k == N_HEAD - 1:
            total = jnp.sum(value * value, axis=0, keepdims=True)
            sq_ref[...] = jnp.broadcast_to(total[None], sq_ref.shape)


def project(order, weights, blocks):
    hbm = pl.BlockSpec(memory_space=pltpu.HBM)
    arrays = [pltpu.with_memory_space_constraint(x, pltpu.HBM) for x in [weights, *blocks]]
    return pl.pallas_call(
        project_kernel,
        in_specs=[pl.BlockSpec(memory_space=pltpu.SMEM)] + [hbm] * len(arrays),
        out_specs=[VMEM, VMEM],
        out_shape=[
            jax.ShapeDtypeStruct((FEATURES, ROWS), jnp.float32),
            jax.ShapeDtypeStruct((N_HEAD, 1, ROWS), jnp.float32),
        ],
        scratch_shapes=[
            pltpu.VMEM((N_HEAD, FEATURES, WIDTH), jnp.bfloat16),
            pltpu.VMEM((N_HEAD, WIDTH, ROWS), jnp.bfloat16),
            pltpu.SemaphoreType.DMA((N_HEAD, PIECES + 1)),
        ],
        compiler_params=pltpu.CompilerParams(vmem_limit_bytes=20 * 1024 * 1024),
        name="project",
    )(order, *arrays)


def finish_kernel(acc_ref, sq_ref, gain_ref, res_ref, out_ref):
    squares = jnp.sum(sq_ref[...], axis=0)
    scale = lax.rsqrt(squares / D + EPS)
    value = res_ref[...].astype(jnp.float32) + gain_ref[...] * (acc_ref[...] * scale)
    out_ref[...] = value.astype(jnp.bfloat16)


def finish(attended, squares, gain, residual):
    return pl.pallas_call(
        finish_kernel,
        in_specs=[VMEM] * 4,
        out_shape=jax.ShapeDtypeStruct((FEATURES, ROWS), jnp.bfloat16),
        compiler_params=pltpu.CompilerParams(vmem_limit_bytes=12 * 1024 * 1024),
        name="finish",
    )(attended, squares, gain, residual)


def device(x, y, core, head):
    return ((x % SIDE * SIDE + y % SIDE) * 2 + core) * N_HEAD + head % N_HEAD


def moved(array, rule):
    pairs = [
        (device(x, y, core, head), device(*rule(x, y, core, head)))
        for x in range(SIDE)
        for y in range(SIDE)
        for core in range(2)
        for head in range(N_HEAD)
    ]
    return lax.ppermute(array, ("seq", "head"), pairs)


def sense(core):
    return 1 - 2 * core


def spread(x, y, core, head):
    feature = 2 * x + y // 2
    group = (feature + head) % N_HEAD
    return group // 2, group % 2 * 2 + y % 2, core, feature


def on_device(positions, queries, keys, values, out_weight, post_gain, residual):
    seq = lax.axis_index("seq").astype(jnp.int32)
    head = lax.axis_index("head").astype(jnp.int32)
    shard = moved(out_weight.T, spread)

    half = HEAD_SIZE // 2
    inverse = 10000.0 ** (-2.0 * jnp.arange(half, dtype=jnp.float32) / HEAD_SIZE)
    inverse = jnp.concatenate([inverse, inverse])[None]
    own, cosine, sine = prepare(
        positions[None], inverse, keys.transpose(1, 0, 2), values.transpose(1, 0, 2)
    )
    far = lax.ppermute(own, "seq", [(i, i + 2) for i in range(N_SEQ - 2)])
    q = rotate(queries.reshape(ROWS, WIDTH), cosine, sine)
    shard, far = held(shard, far, after=[q])
    given = jnp.where(seq % 2 == 0, own, far)
    prev = lax.ppermute(given, "seq", [(i, i ^ 1) for i in range(N_SEQ)])
    weights = lax.all_gather(shard, "seq", axis=0).reshape(N_HEAD, FEATURES, WIDTH)

    blocks = [[] for _ in range(N_HEAD)]
    place = seq.reshape(1)
    for carried in attend(place, q, own, prev, far):
        blocks[0].append(carried)
        for k in range(1, N_HEAD):
            carried = moved(carried, lambda x, y, core, head: (x, y, core, head + sense(core)))
            blocks[k].append(carried)

    source = head - sense(seq % 2) * jnp.arange(N_HEAD, dtype=jnp.int32)
    order = ((source + head) % N_HEAD).astype(jnp.int32)
    attended, squares = project(order, weights, [x for row in blocks for x in row])
    squares = lax.all_to_all(squares, "head", 0, 0, tiled=True)
    return finish(attended, squares, post_gain[:, None], residual.T).T


def solution(mesh):
    return jax.shard_map(
        on_device,
        mesh=mesh,
        in_specs=(
            P("seq"),
            P("seq", "head", None),
            P("seq", "head", None),
            P("seq", "head", None),
            P("head", "seq"),
            P("head"),
            P("seq", "head"),
        ),
        out_specs=P("seq", "head"),
        check_vma=False,
    )
```

```python
import functools
import math

import jax
import jax.numpy as jnp
from jax import lax
from jax.experimental import pallas as pl
from jax.experimental.pallas import tpu as pltpu
from jax.sharding import PartitionSpec as P

D = 5376
HEAD_SIZE = 128
VISIBLE_SPAN = 1024
EPS = 1e-06
SCALE = 168.0 ** (-0.5)
LOG2E = math.log2(math.e)
ROWS = 512
KV = 2
GROUP = 2
N_SEQ = 32
N_HEAD = 8
FEATURES = D // N_HEAD
SHARD = D // N_SEQ
SIDE = 4
QB = 256
WIDTH = KV * GROUP * HEAD_SIZE
PIECE = 128
PIECES = WIDTH // PIECE
LOW = -1e30
VMEM = pl.BlockSpec(memory_space=pltpu.VMEM)


def cos_and_sin(angle):
    turns = jnp.floor(angle * (2.0 / math.pi) + 0.5)
    x = angle - turns * 1.5703125
    x = x - turns * 4.8351287841796875e-4
    x = x - turns * 3.1385570764541626e-07
    x = x - turns * 6.0771005065061922e-11
    z = x * x
    sine = ((-1.9515295891e-4 * z + 8.3321608736e-3) * z - 1.6666654611e-1) * z * x + x
    cosine = ((2.443315711809948e-5 * z - 1.388731625493765e-3) * z + 4.166664568298827e-2) * z * z
    cosine = cosine - 0.5 * z + 1.0
    quadrant = turns.astype(jnp.int32) & 3
    odd = (quadrant & 1) == 1
    first = jnp.where(odd, sine, cosine)
    second = jnp.where(odd, cosine, sine)
    first = jnp.where((quadrant == 1) | (quadrant == 2), -first, first)
    second = jnp.where(quadrant >= 2, -second, second)
    return first, second


def rotated(x, cosine, sine):
    x = x.astype(jnp.float32)
    return (x * cosine + pltpu.roll(x, 64, 1) * sine).astype(jnp.bfloat16)


def prepare_kernel(pos_ref, inverse_ref, k_ref, v_ref, kv_ref, cos_ref, sin_ref):
    place = jnp.broadcast_to(pos_ref[...].astype(jnp.float32), (HEAD_SIZE, ROWS)).T
    cosine, sine = cos_and_sin(place * inverse_ref[...])
    lane = lax.broadcasted_iota(jnp.int32, (ROWS, HEAD_SIZE), 1)
    sine = jnp.where(lane < HEAD_SIZE // 2, -sine, sine)
    cos_ref[...] = cosine
    sin_ref[...] = sine
    for g in range(KV):
        kv_ref[g, 0] = rotated(k_ref[g], cosine, sine)
        kv_ref[g, 1] = v_ref[g]


def prepare(positions, inverse, k, v):
    payload = jax.ShapeDtypeStruct((KV, 2, ROWS, HEAD_SIZE), jnp.bfloat16)
    table = jax.ShapeDtypeStruct((ROWS, HEAD_SIZE), jnp.float32)
    return pl.pallas_call(
        prepare_kernel,
        in_specs=[VMEM] * 4,
        out_specs=[VMEM] * 3,
        out_shape=[payload, table, table],
        compiler_params=pltpu.CompilerParams(vmem_limit_bytes=8 * 1024 * 1024),
        name="prepare",
    )(positions, inverse, k, v)


def rotate_kernel(q_ref, cos_ref, sin_ref, out_ref):
    for n in range(KV * GROUP):
        part = slice(n * HEAD_SIZE, (n + 1) * HEAD_SIZE)
        out_ref[:, part] = rotated(q_ref[:, part], cos_ref[...], sin_ref[...])


def rotate(q, cosine, sine):
    return pl.pallas_call(
        rotate_kernel,
        in_specs=[VMEM] * 3,
        out_specs=VMEM,
        out_shape=jax.ShapeDtypeStruct(q.shape, q.dtype),
        compiler_params=pltpu.CompilerParams(vmem_limit_bytes=4 * 1024 * 1024),
        name="rotate",
    )(q, cosine, sine)


def dot_nt(a, b):
    return lax.dot_general(a, b, (((1,), (1,)), ((), ())), preferred_element_type=jnp.float32)


def hold_kernel(*refs):
    pass


def held(array, other, after):
    hbm = pl.BlockSpec(memory_space=pltpu.HBM)
    other, *after = [pltpu.with_memory_space_constraint(x, pltpu.VMEM) for x in [other, *after]]
    return pl.pallas_call(
        hold_kernel,
        in_specs=[hbm, VMEM] + [VMEM] * len(after),
        out_specs=[hbm, VMEM],
        out_shape=[jax.ShapeDtypeStruct(x.shape, x.dtype) for x in [array, other]],
        input_output_aliases={0: 0, 1: 1},
        compiler_params=pltpu.CompilerParams(vmem_limit_bytes=1024 * 1024),
        name="hold",
    )(array, other, *after)


def held_alone(array, after):
    hbm = pl.BlockSpec(memory_space=pltpu.HBM)
    after = [pltpu.with_memory_space_constraint(x, pltpu.VMEM) for x in after]
    return pl.pallas_call(
        hold_kernel,
        in_specs=[hbm] + [VMEM] * len(after),
        out_specs=hbm,
        out_shape=jax.ShapeDtypeStruct(array.shape, array.dtype),
        input_output_aliases={0: 0},
        compiler_params=pltpu.CompilerParams(vmem_limit_bytes=1024 * 1024),
        name="hold",
    )(array, *after)


def attend_kernel(place_ref, q_ref, own_ref, prev_ref, far_ref, *out_refs):
    place = place_ref[0]
    prev_bias = jnp.where(place >= 1, 0.0, LOW)
    far_bias = jnp.where(place >= 2, 0.0, LOW)
    c = SCALE * LOG2E
    row = lax.broadcasted_iota(jnp.int32, (QB, QB), 0)
    col = lax.broadcasted_iota(jnp.int32, (QB, QB), 1)
    seen = row <= col
    blocks = ROWS // QB
    for n in range(PIECES):
        g = n // GROUP
        k_own, k_prev, k_far = own_ref[g, 0], prev_ref[g, 0], far_ref[g, 0]
        v_own = own_ref[g, 1].T
        v_prev = prev_ref[g, 1].T
        v_far = far_ref[g, 1].T
        q_all = q_ref[:, n * HEAD_SIZE : (n + 1) * HEAD_SIZE]
        for b in range(blocks):
            q = q_all[b * QB : (b + 1) * QB]
            lo, hi = b * QB, (b + 1) * QB
            prev = dot_nt(k_prev, q)
            own = dot_nt(k_own[0:hi], q)
            far = dot_nt(k_far[lo:ROWS], q)
            mixed = jnp.where(seen, own[lo:hi], far[0:QB] + far_bias)
            top = jnp.maximum(
                jnp.max(prev, axis=0, keepdims=True) + prev_bias,
                jnp.max(mixed, axis=0, keepdims=True),
            )
            if lo > 0:
                top = jnp.maximum(top, jnp.max(own[0:lo], axis=0, keepdims=True))
            if hi < ROWS:
                top = jnp.maximum(top, jnp.max(far[QB:], axis=0, keepdims=True) + far_bias)
            top = top * c
            p_prev = jnp.exp2(prev * c - (top - prev_bias))
            p_mixed = jnp.exp2(mixed * c - top)
            total = jnp.sum(p_prev, axis=0, keepdims=True) + jnp.sum(p_mixed, axis=0, keepdims=True)
            own_parts = [jnp.where(seen, p_mixed, 0.0).astype(jnp.bfloat16)]
            far_parts = [jnp.where(seen, 0.0, p_mixed).astype(jnp.bfloat16)]
            if lo > 0:
                p = jnp.exp2(own[0:lo] * c - top)
                total = total + jnp.sum(p, axis=0, keepdims=True)
                own_parts.insert(0, p.astype(jnp.bfloat16))
            if hi < ROWS:
                p = jnp.exp2(far[QB:] * c - (top - far_bias))
                total = total + jnp.sum(p, axis=0, keepdims=True)
                far_parts.append(p.astype(jnp.bfloat16))
            context = jnp.dot(v_prev, p_prev.astype(jnp.bfloat16), preferred_element_type=jnp.float32)
            context += jnp.dot(
                v_own[:, 0:hi], jnp.concatenate(own_parts, 0), preferred_element_type=jnp.float32
            )
            context += jnp.dot(
                v_far[:, lo:], jnp.concatenate(far_parts, 0), preferred_element_type=jnp.float32
            )
            out_refs[n][:, lo:hi] = (context / total).astype(jnp.bfloat16)


def attend(place, *arrays):
    arrays = [pltpu.with_memory_space_constraint(x, pltpu.VMEM) for x in arrays]
    return pl.pallas_call(
        attend_kernel,
        in_specs=[pl.BlockSpec(memory_space=pltpu.SMEM)] + [VMEM] * len(arrays),
        out_specs=[VMEM] * PIECES,
        out_shape=[jax.ShapeDtypeStruct((PIECE, ROWS), jnp.bfloat16)] * PIECES,
        compiler_params=pltpu.CompilerParams(vmem_limit_bytes=16 * 1024 * 1024),
        name="attend",
    )(place, *arrays)


def project_kernel(order_ref, w_ref, *refs):
    ctx_refs = refs[: PIECES * N_HEAD]
    acc_ref, sq_ref, w_buffer, ctx_buffer, arrived = refs[PIECES * N_HEAD :]
    copies = []
    for k in range(N_HEAD):
        copies.append(
            [
                pltpu.make_async_copy(
                    w_ref.at[order_ref[0, k], order_ref[1, k] ^ part],
                    w_buffer.at[k, part],
                    arrived.at[k, PIECES + part],
                )
                for part in range(2)
            ]
            + [
                pltpu.make_async_copy(
                    ctx_refs[k * PIECES + g],
                    ctx_buffer.at[k, g * PIECE : (g + 1) * PIECE],
                    arrived.at[k, g],
                )
                for g in range(PIECES)
            ]
        )
        for copy in copies[k]:
            copy.start()
    for k in range(N_HEAD):
        for copy in copies[k]:
            copy.wait()
        value = jnp.dot(
            w_buffer[k].reshape(FEATURES, WIDTH), ctx_buffer[k], preferred_element_type=jnp.float32
        )
        if k > 0:
            value = acc_ref[...] + value
        acc_ref[...] = value
        if k == N_HEAD - 1:
            total = jnp.sum(value * value, axis=0, keepdims=True)
            sq_ref[...] = jnp.broadcast_to(total[None], sq_ref.shape)


def project(order, weights, blocks):
    hbm = pl.BlockSpec(memory_space=pltpu.HBM)
    arrays = [pltpu.with_memory_space_constraint(x, pltpu.HBM) for x in [weights, *blocks]]
    return pl.pallas_call(
        project_kernel,
        in_specs=[pl.BlockSpec(memory_space=pltpu.SMEM)] + [hbm] * len(arrays),
        out_specs=[VMEM, VMEM],
        out_shape=[
            jax.ShapeDtypeStruct((FEATURES, ROWS), jnp.float32),
            jax.ShapeDtypeStruct((N_HEAD, 1, ROWS), jnp.float32),
        ],
        scratch_shapes=[
            pltpu.VMEM((N_HEAD, 2, FEATURES // 2, WIDTH), jnp.bfloat16),
            pltpu.VMEM((N_HEAD, WIDTH, ROWS), jnp.bfloat16),
            pltpu.SemaphoreType.DMA((N_HEAD, PIECES + 2)),
        ],
        compiler_params=pltpu.CompilerParams(vmem_limit_bytes=20 * 1024 * 1024),
        name="project",
    )(order, *arrays)


def finish_kernel(acc_ref, sq_ref, gain_ref, res_ref, out_ref):
    squares = jnp.sum(sq_ref[...], axis=0)
    scale = lax.rsqrt(squares / D + EPS)
    value = res_ref[...].astype(jnp.float32) + gain_ref[...] * (acc_ref[...] * scale)
    out_ref[...] = value.astype(jnp.bfloat16)


def finish(attended, squares, gain, residual):
    return pl.pallas_call(
        finish_kernel,
        in_specs=[VMEM] * 4,
        out_shape=jax.ShapeDtypeStruct((FEATURES, ROWS), jnp.bfloat16),
        compiler_params=pltpu.CompilerParams(vmem_limit_bytes=12 * 1024 * 1024),
        name="finish",
    )(attended, squares, gain, residual)


def device(x, y, core, head):
    return ((x % SIDE * SIDE + y % SIDE) * 2 + core) * N_HEAD + head % N_HEAD


def moved(array, rule):
    pairs = [
        (device(x, y, core, head), device(*rule(x, y, core, head)))
        for x in range(SIDE)
        for y in range(SIDE)
        for core in range(2)
        for head in range(N_HEAD)
    ]
    return lax.ppermute(array, ("seq", "head"), pairs)


def sense(core):
    return 1 - 2 * core


def spread(x, y, core, head):
    group = (2 * x + y // 2 + head) % N_HEAD
    return group // 2, group % 2 * 2 + (y + head) % 2, core, head


def lifted(x, y, core, head):
    return x, y, core, 2 * x + y // 2 - head


def on_device(positions, queries, keys, values, out_weight, post_gain, residual):
    seq = lax.axis_index("seq").astype(jnp.int32)
    head = lax.axis_index("head").astype(jnp.int32)
    shard = moved(out_weight.T, spread)

    half = HEAD_SIZE // 2
    inverse = 10000.0 ** (-2.0 * jnp.arange(half, dtype=jnp.float32) / HEAD_SIZE)
    inverse = jnp.concatenate([inverse, inverse])[None]
    own, cosine, sine = prepare(
        positions[None], inverse, keys.transpose(1, 0, 2), values.transpose(1, 0, 2)
    )
    far = lax.ppermute(own, "seq", [(i, i + 2) for i in range(N_SEQ - 2)])
    q = rotate(queries.reshape(ROWS, WIDTH), cosine, sine)
    shard, far = held(shard, far, after=[q])
    shard = moved(shard, lifted)
    given = jnp.where(seq % 2 == 0, own, far)
    prev = lax.ppermute(given, "seq", [(i, i ^ 1) for i in range(N_SEQ)])

    blocks = [[] for _ in range(N_HEAD)]
    place = seq.reshape(1)
    for carried in attend(place, q, own, prev, far):
        blocks[0].append(carried)
        for k in range(1, N_HEAD):
            carried = moved(carried, lambda x, y, core, head: (x, y, core, head + sense(core)))
            blocks[k].append(carried)

    shard = held_alone(shard, after=blocks[0])
    weights = lax.all_gather(shard, "seq", axis=0).reshape(N_HEAD, 2, FEATURES // 2, WIDTH)

    source = (head - sense(seq % 2) * jnp.arange(N_HEAD, dtype=jnp.int32)) % N_HEAD
    order = jnp.stack([(source + head) % N_HEAD, source % 2]).astype(jnp.int32)
    attended, squares = project(order, weights, [x for row in blocks for x in row])
    squares = lax.all_to_all(squares, "head", 0, 0, tiled=True)
    return finish(attended, squares, post_gain[:, None], residual.T).T


def solution(mesh):
    return jax.shard_map(
        on_device,
        mesh=mesh,
        in_specs=(
            P("seq"),
            P("seq", "head", None),
            P("seq", "head", None),
            P("seq", "head", None),
            P("head", "seq"),
            P("head"),
            P("seq", "head"),
        ),
        out_specs=P("seq", "head"),
        check_vma=False,
    )
```

```python
import functools
import math

import jax
import jax.numpy as jnp
from jax import lax
from jax.experimental import pallas as pl
from jax.experimental.pallas import tpu as pltpu
from jax.sharding import PartitionSpec as P

D = 5376
HEAD_SIZE = 128
VISIBLE_SPAN = 1024
EPS = 1e-06
SCALE = 168.0 ** (-0.5)
LOG2E = math.log2(math.e)
ROWS = 512
KV = 2
GROUP = 2
N_SEQ = 32
N_HEAD = 8
FEATURES = D // N_HEAD
SHARD = D // N_SEQ
SIDE = 4
QB = 256
WIDTH = KV * GROUP * HEAD_SIZE
PIECE = 128
PIECES = WIDTH // PIECE
LOW = -1e30
VMEM = pl.BlockSpec(memory_space=pltpu.VMEM)


def cos_and_sin(angle):
    turns = jnp.floor(angle * (2.0 / math.pi) + 0.5)
    x = angle - turns * 1.5703125
    x = x - turns * 4.8351287841796875e-4
    x = x - turns * 3.1385570764541626e-07
    x = x - turns * 6.0771005065061922e-11
    z = x * x
    sine = ((-1.9515295891e-4 * z + 8.3321608736e-3) * z - 1.6666654611e-1) * z * x + x
    cosine = ((2.443315711809948e-5 * z - 1.388731625493765e-3) * z + 4.166664568298827e-2) * z * z
    cosine = cosine - 0.5 * z + 1.0
    quadrant = turns.astype(jnp.int32) & 3
    odd = (quadrant & 1) == 1
    first = jnp.where(odd, sine, cosine)
    second = jnp.where(odd, cosine, sine)
    first = jnp.where((quadrant == 1) | (quadrant == 2), -first, first)
    second = jnp.where(quadrant >= 2, -second, second)
    return first, second


def rotated(x, cosine, sine):
    x = x.astype(jnp.float32)
    return (x * cosine + pltpu.roll(x, 64, 1) * sine).astype(jnp.bfloat16)


def prepare_kernel(pos_ref, inverse_ref, k_ref, v_ref, kv_ref, cos_ref, sin_ref):
    place = jnp.broadcast_to(pos_ref[...].astype(jnp.float32), (HEAD_SIZE, ROWS)).T
    cosine, sine = cos_and_sin(place * inverse_ref[...])
    lane = lax.broadcasted_iota(jnp.int32, (ROWS, HEAD_SIZE), 1)
    sine = jnp.where(lane < HEAD_SIZE // 2, -sine, sine)
    cos_ref[...] = cosine
    sin_ref[...] = sine
    for g in range(KV):
        kv_ref[g, 0] = rotated(k_ref[g], cosine, sine)
        kv_ref[g, 1] = v_ref[g]


def prepare(positions, inverse, k, v):
    payload = jax.ShapeDtypeStruct((KV, 2, ROWS, HEAD_SIZE), jnp.bfloat16)
    table = jax.ShapeDtypeStruct((ROWS, HEAD_SIZE), jnp.float32)
    return pl.pallas_call(
        prepare_kernel,
        in_specs=[VMEM] * 4,
        out_specs=[VMEM] * 3,
        out_shape=[payload, table, table],
        compiler_params=pltpu.CompilerParams(vmem_limit_bytes=8 * 1024 * 1024),
        name="prepare",
    )(positions, inverse, k, v)


def rotate_kernel(q_ref, cos_ref, sin_ref, out_ref):
    for n in range(KV * GROUP):
        part = slice(n * HEAD_SIZE, (n + 1) * HEAD_SIZE)
        out_ref[:, part] = rotated(q_ref[:, part], cos_ref[...], sin_ref[...])


def rotate(q, cosine, sine):
    return pl.pallas_call(
        rotate_kernel,
        in_specs=[VMEM] * 3,
        out_specs=VMEM,
        out_shape=jax.ShapeDtypeStruct(q.shape, q.dtype),
        compiler_params=pltpu.CompilerParams(vmem_limit_bytes=4 * 1024 * 1024),
        name="rotate",
    )(q, cosine, sine)


def dot_nt(a, b):
    return lax.dot_general(a, b, (((1,), (1,)), ((), ())), preferred_element_type=jnp.float32)


def hold_kernel(*refs):
    pass


def held(array, other, after):
    hbm = pl.BlockSpec(memory_space=pltpu.HBM)
    other, *after = [pltpu.with_memory_space_constraint(x, pltpu.VMEM) for x in [other, *after]]
    return pl.pallas_call(
        hold_kernel,
        in_specs=[hbm, VMEM] + [VMEM] * len(after),
        out_specs=[hbm, VMEM],
        out_shape=[jax.ShapeDtypeStruct(x.shape, x.dtype) for x in [array, other]],
        input_output_aliases={0: 0, 1: 1},
        compiler_params=pltpu.CompilerParams(vmem_limit_bytes=1024 * 1024),
        name="hold",
    )(array, other, *after)


def held_alone(array, after):
    hbm = pl.BlockSpec(memory_space=pltpu.HBM)
    after = [pltpu.with_memory_space_constraint(x, pltpu.VMEM) for x in after]
    return pl.pallas_call(
        hold_kernel,
        in_specs=[hbm] + [VMEM] * len(after),
        out_specs=hbm,
        out_shape=jax.ShapeDtypeStruct(array.shape, array.dtype),
        input_output_aliases={0: 0},
        compiler_params=pltpu.CompilerParams(vmem_limit_bytes=1024 * 1024),
        name="hold",
    )(array, *after)


def attend_kernel(n, place_ref, q_ref, own_ref, prev_ref, far_ref, out_ref):
    g = n // GROUP
    place = place_ref[0]
    prev_bias = jnp.where(place >= 1, 0.0, LOW)
    far_bias = jnp.where(place >= 2, 0.0, LOW)
    c = SCALE * LOG2E
    k_own, k_prev, k_far = own_ref[g, 0], prev_ref[g, 0], far_ref[g, 0]
    v_own = own_ref[g, 1].T
    v_prev = prev_ref[g, 1].T
    v_far = far_ref[g, 1].T
    row = lax.broadcasted_iota(jnp.int32, (QB, QB), 0)
    col = lax.broadcasted_iota(jnp.int32, (QB, QB), 1)
    seen = row <= col
    blocks = ROWS // QB
    q_all = q_ref[:, n * HEAD_SIZE : (n + 1) * HEAD_SIZE]
    for b in range(blocks):
        q = q_all[b * QB : (b + 1) * QB]
        lo, hi = b * QB, (b + 1) * QB
        prev = dot_nt(k_prev, q)
        own = dot_nt(k_own[0:hi], q)
        far = dot_nt(k_far[lo:ROWS], q)
        mixed = jnp.where(seen, own[lo:hi], far[0:QB] + far_bias)
        top = jnp.maximum(
            jnp.max(prev, axis=0, keepdims=True) + prev_bias,
            jnp.max(mixed, axis=0, keepdims=True),
        )
        if lo > 0:
            top = jnp.maximum(top, jnp.max(own[0:lo], axis=0, keepdims=True))
        if hi < ROWS:
            top = jnp.maximum(top, jnp.max(far[QB:], axis=0, keepdims=True) + far_bias)
        top = top * c
        p_prev = jnp.exp2(prev * c - (top - prev_bias))
        p_mixed = jnp.exp2(mixed * c - top)
        total = jnp.sum(p_prev, axis=0, keepdims=True) + jnp.sum(p_mixed, axis=0, keepdims=True)
        own_parts = [jnp.where(seen, p_mixed, 0.0).astype(jnp.bfloat16)]
        far_parts = [jnp.where(seen, 0.0, p_mixed).astype(jnp.bfloat16)]
        if lo > 0:
            p = jnp.exp2(own[0:lo] * c - top)
            total = total + jnp.sum(p, axis=0, keepdims=True)
            own_parts.insert(0, p.astype(jnp.bfloat16))
        if hi < ROWS:
            p = jnp.exp2(far[QB:] * c - (top - far_bias))
            total = total + jnp.sum(p, axis=0, keepdims=True)
            far_parts.append(p.astype(jnp.bfloat16))
        context = jnp.dot(v_prev, p_prev.astype(jnp.bfloat16), preferred_element_type=jnp.float32)
        context += jnp.dot(
            v_own[:, 0:hi], jnp.concatenate(own_parts, 0), preferred_element_type=jnp.float32
        )
        context += jnp.dot(
            v_far[:, lo:], jnp.concatenate(far_parts, 0), preferred_element_type=jnp.float32
        )
        out_ref[:, lo:hi] = (context / total).astype(jnp.bfloat16)


def attend(n, place, *arrays):
    arrays = [pltpu.with_memory_space_constraint(x, pltpu.VMEM) for x in arrays]
    return pl.pallas_call(
        functools.partial(attend_kernel, n),
        in_specs=[pl.BlockSpec(memory_space=pltpu.SMEM)] + [VMEM] * len(arrays),
        out_specs=VMEM,
        out_shape=jax.ShapeDtypeStruct((PIECE, ROWS), jnp.bfloat16),
        compiler_params=pltpu.CompilerParams(vmem_limit_bytes=16 * 1024 * 1024),
        name="attend",
    )(place, *arrays)


def project_kernel(order_ref, w_ref, *refs):
    ctx_refs = refs[: PIECES * N_HEAD]
    acc_ref, sq_ref, w_buffer, ctx_buffer, arrived = refs[PIECES * N_HEAD :]
    copies = []
    for k in range(N_HEAD):
        copies.append(
            [
                pltpu.make_async_copy(
                    w_ref.at[order_ref[0, k], order_ref[1, k] ^ part],
                    w_buffer.at[k, part],
                    arrived.at[k, PIECES + part],
                )
                for part in range(2)
            ]
            + [
                pltpu.make_async_copy(
                    ctx_refs[k * PIECES + g],
                    ctx_buffer.at[k, g * PIECE : (g + 1) * PIECE],
                    arrived.at[k, g],
                )
                for g in range(PIECES)
            ]
        )
        for copy in copies[k]:
            copy.start()
    for k in range(N_HEAD):
        for copy in copies[k]:
            copy.wait()
        value = jnp.dot(
            w_buffer[k].reshape(FEATURES, WIDTH), ctx_buffer[k], preferred_element_type=jnp.float32
        )
        if k > 0:
            value = acc_ref[...] + value
        acc_ref[...] = value
        if k == N_HEAD - 1:
            total = jnp.sum(value * value, axis=0, keepdims=True)
            sq_ref[...] = jnp.broadcast_to(total[None], sq_ref.shape)


def project(order, weights, blocks):
    hbm = pl.BlockSpec(memory_space=pltpu.HBM)
    arrays = [pltpu.with_memory_space_constraint(x, pltpu.HBM) for x in [weights, *blocks]]
    return pl.pallas_call(
        project_kernel,
        in_specs=[pl.BlockSpec(memory_space=pltpu.SMEM)] + [hbm] * len(arrays),
        out_specs=[VMEM, VMEM],
        out_shape=[
            jax.ShapeDtypeStruct((FEATURES, ROWS), jnp.float32),
            jax.ShapeDtypeStruct((N_HEAD, 1, ROWS), jnp.float32),
        ],
        scratch_shapes=[
            pltpu.VMEM((N_HEAD, 2, FEATURES // 2, WIDTH), jnp.bfloat16),
            pltpu.VMEM((N_HEAD, WIDTH, ROWS), jnp.bfloat16),
            pltpu.SemaphoreType.DMA((N_HEAD, PIECES + 2)),
        ],
        compiler_params=pltpu.CompilerParams(vmem_limit_bytes=20 * 1024 * 1024),
        name="project",
    )(order, *arrays)


def finish_kernel(acc_ref, sq_ref, gain_ref, res_ref, out_ref):
    squares = jnp.sum(sq_ref[...], axis=0)
    scale = lax.rsqrt(squares / D + EPS)
    value = res_ref[...].astype(jnp.float32) + gain_ref[...] * (acc_ref[...] * scale)
    out_ref[...] = value.astype(jnp.bfloat16)


def finish(attended, squares, gain, residual):
    return pl.pallas_call(
        finish_kernel,
        in_specs=[VMEM] * 4,
        out_shape=jax.ShapeDtypeStruct((FEATURES, ROWS), jnp.bfloat16),
        compiler_params=pltpu.CompilerParams(vmem_limit_bytes=12 * 1024 * 1024),
        name="finish",
    )(attended, squares, gain, residual)


def device(x, y, core, head):
    return ((x % SIDE * SIDE + y % SIDE) * 2 + core) * N_HEAD + head % N_HEAD


def moved(array, rule):
    pairs = [
        (device(x, y, core, head), device(*rule(x, y, core, head)))
        for x in range(SIDE)
        for y in range(SIDE)
        for core in range(2)
        for head in range(N_HEAD)
    ]
    return lax.ppermute(array, ("seq", "head"), pairs)


def sense(core):
    return 1 - 2 * core


def spread(x, y, core, head):
    group = (2 * x + y // 2 + head) % N_HEAD
    return group // 2, group % 2 * 2 + (y + head) % 2, core, head


def lifted(x, y, core, head):
    return x, y, core, 2 * x + y // 2 - head


def on_device(positions, queries, keys, values, out_weight, post_gain, residual):
    seq = lax.axis_index("seq").astype(jnp.int32)
    head = lax.axis_index("head").astype(jnp.int32)
    shard = moved(out_weight.T, spread)

    half = HEAD_SIZE // 2
    inverse = 10000.0 ** (-2.0 * jnp.arange(half, dtype=jnp.float32) / HEAD_SIZE)
    inverse = jnp.concatenate([inverse, inverse])[None]
    own, cosine, sine = prepare(
        positions[None], inverse, keys.transpose(1, 0, 2), values.transpose(1, 0, 2)
    )
    far = lax.ppermute(own, "seq", [(i, i + 2) for i in range(N_SEQ - 2)])
    q = rotate(queries.reshape(ROWS, WIDTH), cosine, sine)
    shard, far = held(shard, far, after=[q])
    shard = moved(shard, lifted)
    given = jnp.where(seq % 2 == 0, own, far)
    prev = lax.ppermute(given, "seq", [(i, i ^ 1) for i in range(N_SEQ)])

    blocks = [[] for _ in range(N_HEAD)]
    place = seq.reshape(1)
    for n in range(PIECES):
        carried = attend(n, place, q, own, prev, far)
        blocks[0].append(carried)
        for k in range(1, N_HEAD):
            carried = moved(carried, lambda x, y, core, head: (x, y, core, head + sense(core)))
            blocks[k].append(carried)

    shard = held_alone(shard, after=blocks[0][-1:])
    weights = lax.all_gather(shard, "seq", axis=0).reshape(N_HEAD, 2, FEATURES // 2, WIDTH)

    source = (head - sense(seq % 2) * jnp.arange(N_HEAD, dtype=jnp.int32)) % N_HEAD
    order = jnp.stack([(source + head) % N_HEAD, source % 2]).astype(jnp.int32)
    attended, squares = project(order, weights, [x for row in blocks for x in row])
    squares = lax.all_to_all(squares, "head", 0, 0, tiled=True)
    return finish(attended, squares, post_gain[:, None], residual.T).T


def solution(mesh):
    return jax.shard_map(
        on_device,
        mesh=mesh,
        in_specs=(
            P("seq"),
            P("seq", "head", None),
            P("seq", "head", None),
            P("seq", "head", None),
            P("head", "seq"),
            P("head"),
            P("seq", "head"),
        ),
        out_specs=P("seq", "head"),
        check_vma=False,
    )
```

```python
import functools
import math

import jax
import jax.numpy as jnp
from jax import lax
from jax.experimental import pallas as pl
from jax.experimental.pallas import tpu as pltpu
from jax.sharding import PartitionSpec as P

D = 5376
HEAD_SIZE = 128
VISIBLE_SPAN = 1024
EPS = 1e-06
SCALE = 168.0 ** (-0.5)
LOG2E = math.log2(math.e)
ROWS = 512
KV = 2
GROUP = 2
N_SEQ = 32
N_HEAD = 8
FEATURES = D // N_HEAD
SHARD = D // N_SEQ
SIDE = 4
QB = 256
WIDTH = KV * GROUP * HEAD_SIZE
PIECE = 128
PIECES = WIDTH // PIECE
LOW = -1e30
VMEM = pl.BlockSpec(memory_space=pltpu.VMEM)


def cos_and_sin(angle):
    turns = jnp.floor(angle * (2.0 / math.pi) + 0.5)
    x = angle - turns * 1.5703125
    x = x - turns * 4.8351287841796875e-4
    x = x - turns * 3.1385570764541626e-07
    x = x - turns * 6.0771005065061922e-11
    z = x * x
    sine = ((-1.9515295891e-4 * z + 8.3321608736e-3) * z - 1.6666654611e-1) * z * x + x
    cosine = ((2.443315711809948e-5 * z - 1.388731625493765e-3) * z + 4.166664568298827e-2) * z * z
    cosine = cosine - 0.5 * z + 1.0
    quadrant = turns.astype(jnp.int32) & 3
    odd = (quadrant & 1) == 1
    first = jnp.where(odd, sine, cosine)
    second = jnp.where(odd, cosine, sine)
    first = jnp.where((quadrant == 1) | (quadrant == 2), -first, first)
    second = jnp.where(quadrant >= 2, -second, second)
    return first, second


def rotated(x, cosine, sine):
    x = x.astype(jnp.float32)
    return (x * cosine + pltpu.roll(x, 64, 1) * sine).astype(jnp.bfloat16)


def prepare_kernel(pos_ref, inverse_ref, k_ref, v_ref, kv_ref, cos_ref, sin_ref):
    place = jnp.broadcast_to(pos_ref[...].astype(jnp.float32), (HEAD_SIZE, ROWS)).T
    cosine, sine = cos_and_sin(place * inverse_ref[...])
    lane = lax.broadcasted_iota(jnp.int32, (ROWS, HEAD_SIZE), 1)
    sine = jnp.where(lane < HEAD_SIZE // 2, -sine, sine)
    cos_ref[...] = cosine
    sin_ref[...] = sine
    for g in range(KV):
        kv_ref[g, 0] = rotated(k_ref[g], cosine, sine)
        kv_ref[g, 1] = v_ref[g]


def prepare(positions, inverse, k, v):
    payload = jax.ShapeDtypeStruct((KV, 2, ROWS, HEAD_SIZE), jnp.bfloat16)
    table = jax.ShapeDtypeStruct((ROWS, HEAD_SIZE), jnp.float32)
    return pl.pallas_call(
        prepare_kernel,
        in_specs=[VMEM] * 4,
        out_specs=[VMEM] * 3,
        out_shape=[payload, table, table],
        compiler_params=pltpu.CompilerParams(vmem_limit_bytes=8 * 1024 * 1024),
        name="prepare",
    )(positions, inverse, k, v)


def rotate_kernel(q_ref, cos_ref, sin_ref, out_ref):
    for n in range(KV * GROUP):
        part = slice(n * HEAD_SIZE, (n + 1) * HEAD_SIZE)
        out_ref[:, part] = rotated(q_ref[:, part], cos_ref[...], sin_ref[...])


def rotate(q, cosine, sine):
    return pl.pallas_call(
        rotate_kernel,
        in_specs=[VMEM] * 3,
        out_specs=VMEM,
        out_shape=jax.ShapeDtypeStruct(q.shape, q.dtype),
        compiler_params=pltpu.CompilerParams(vmem_limit_bytes=4 * 1024 * 1024),
        name="rotate",
    )(q, cosine, sine)


def dot_nt(a, b):
    return lax.dot_general(a, b, (((1,), (1,)), ((), ())), preferred_element_type=jnp.float32)


def hold_kernel(*refs):
    pass


def held(array, other, after):
    hbm = pl.BlockSpec(memory_space=pltpu.HBM)
    other, *after = [pltpu.with_memory_space_constraint(x, pltpu.VMEM) for x in [other, *after]]
    return pl.pallas_call(
        hold_kernel,
        in_specs=[hbm, VMEM] + [VMEM] * len(after),
        out_specs=[hbm, VMEM],
        out_shape=[jax.ShapeDtypeStruct(x.shape, x.dtype) for x in [array, other]],
        input_output_aliases={0: 0, 1: 1},
        compiler_params=pltpu.CompilerParams(vmem_limit_bytes=1024 * 1024),
        name="hold",
    )(array, other, *after)


def held_alone(array, after):
    hbm = pl.BlockSpec(memory_space=pltpu.HBM)
    after = [pltpu.with_memory_space_constraint(x, pltpu.VMEM) for x in after]
    return pl.pallas_call(
        hold_kernel,
        in_specs=[hbm] + [VMEM] * len(after),
        out_specs=hbm,
        out_shape=jax.ShapeDtypeStruct(array.shape, array.dtype),
        input_output_aliases={0: 0},
        compiler_params=pltpu.CompilerParams(vmem_limit_bytes=1024 * 1024),
        name="hold",
    )(array, *after)


def attend_kernel(first, place_ref, q_ref, own_ref, prev_ref, far_ref, *out_refs):
    place = place_ref[0]
    prev_bias = jnp.where(place >= 1, 0.0, LOW)
    far_bias = jnp.where(place >= 2, 0.0, LOW)
    c = SCALE * LOG2E
    row = lax.broadcasted_iota(jnp.int32, (QB, QB), 0)
    col = lax.broadcasted_iota(jnp.int32, (QB, QB), 1)
    seen = row <= col
    blocks = ROWS // QB
    for n in range(first, first + GROUP):
        g = n // GROUP
        k_own, k_prev, k_far = own_ref[g, 0], prev_ref[g, 0], far_ref[g, 0]
        v_own = own_ref[g, 1].T
        v_prev = prev_ref[g, 1].T
        v_far = far_ref[g, 1].T
        q_all = q_ref[:, n * HEAD_SIZE : (n + 1) * HEAD_SIZE]
        for b in range(blocks):
            q = q_all[b * QB : (b + 1) * QB]
            lo, hi = b * QB, (b + 1) * QB
            prev = dot_nt(k_prev, q)
            own = dot_nt(k_own[0:hi], q)
            far = dot_nt(k_far[lo:ROWS], q)
            mixed = jnp.where(seen, own[lo:hi], far[0:QB] + far_bias)
            top = jnp.maximum(
                jnp.max(prev, axis=0, keepdims=True) + prev_bias,
                jnp.max(mixed, axis=0, keepdims=True),
            )
            if lo > 0:
                top = jnp.maximum(top, jnp.max(own[0:lo], axis=0, keepdims=True))
            if hi < ROWS:
                top = jnp.maximum(top, jnp.max(far[QB:], axis=0, keepdims=True) + far_bias)
            top = top * c
            p_prev = jnp.exp2(prev * c - (top - prev_bias))
            p_mixed = jnp.exp2(mixed * c - top)
            total = jnp.sum(p_prev, axis=0, keepdims=True) + jnp.sum(p_mixed, axis=0, keepdims=True)
            own_parts = [jnp.where(seen, p_mixed, 0.0).astype(jnp.bfloat16)]
            far_parts = [jnp.where(seen, 0.0, p_mixed).astype(jnp.bfloat16)]
            if lo > 0:
                p = jnp.exp2(own[0:lo] * c - top)
                total = total + jnp.sum(p, axis=0, keepdims=True)
                own_parts.insert(0, p.astype(jnp.bfloat16))
            if hi < ROWS:
                p = jnp.exp2(far[QB:] * c - (top - far_bias))
                total = total + jnp.sum(p, axis=0, keepdims=True)
                far_parts.append(p.astype(jnp.bfloat16))
            context = jnp.dot(v_prev, p_prev.astype(jnp.bfloat16), preferred_element_type=jnp.float32)
            context += jnp.dot(
                v_own[:, 0:hi], jnp.concatenate(own_parts, 0), preferred_element_type=jnp.float32
            )
            context += jnp.dot(
                v_far[:, lo:], jnp.concatenate(far_parts, 0), preferred_element_type=jnp.float32
            )
            out_refs[n - first][:, lo:hi] = (context / total).astype(jnp.bfloat16)


def attend(first, place, *arrays):
    arrays = [pltpu.with_memory_space_constraint(x, pltpu.VMEM) for x in arrays]
    return pl.pallas_call(
        functools.partial(attend_kernel, first),
        in_specs=[pl.BlockSpec(memory_space=pltpu.SMEM)] + [VMEM] * len(arrays),
        out_specs=[VMEM] * GROUP,
        out_shape=[jax.ShapeDtypeStruct((PIECE, ROWS), jnp.bfloat16)] * GROUP,
        compiler_params=pltpu.CompilerParams(vmem_limit_bytes=16 * 1024 * 1024),
        name="attend",
    )(place, *arrays)


def project_kernel(order_ref, w_ref, *refs):
    ctx_refs = refs[: PIECES * N_HEAD]
    acc_ref, sq_ref, w_buffer, ctx_buffer, arrived = refs[PIECES * N_HEAD :]
    copies = []
    for k in range(N_HEAD):
        copies.append(
            [
                pltpu.make_async_copy(
                    w_ref.at[order_ref[0, k], order_ref[1, k] ^ part],
                    w_buffer.at[k, part],
                    arrived.at[k, PIECES + part],
                )
                for part in range(2)
            ]
            + [
                pltpu.make_async_copy(
                    ctx_refs[k * PIECES + g],
                    ctx_buffer.at[k, g * PIECE : (g + 1) * PIECE],
                    arrived.at[k, g],
                )
                for g in range(PIECES)
            ]
        )
        for copy in copies[k]:
            copy.start()
    for k in range(N_HEAD):
        for copy in copies[k]:
            copy.wait()
        value = jnp.dot(
            w_buffer[k].reshape(FEATURES, WIDTH), ctx_buffer[k], preferred_element_type=jnp.float32
        )
        if k > 0:
            value = acc_ref[...] + value
        acc_ref[...] = value
        if k == N_HEAD - 1:
            total = jnp.sum(value * value, axis=0, keepdims=True)
            sq_ref[...] = jnp.broadcast_to(total[None], sq_ref.shape)


def project(order, weights, blocks):
    hbm = pl.BlockSpec(memory_space=pltpu.HBM)
    arrays = [pltpu.with_memory_space_constraint(x, pltpu.HBM) for x in [weights, *blocks]]
    return pl.pallas_call(
        project_kernel,
        in_specs=[pl.BlockSpec(memory_space=pltpu.SMEM)] + [hbm] * len(arrays),
        out_specs=[VMEM, VMEM],
        out_shape=[
            jax.ShapeDtypeStruct((FEATURES, ROWS), jnp.float32),
            jax.ShapeDtypeStruct((N_HEAD, 1, ROWS), jnp.float32),
        ],
        scratch_shapes=[
            pltpu.VMEM((N_HEAD, 2, FEATURES // 2, WIDTH), jnp.bfloat16),
            pltpu.VMEM((N_HEAD, WIDTH, ROWS), jnp.bfloat16),
            pltpu.SemaphoreType.DMA((N_HEAD, PIECES + 2)),
        ],
        compiler_params=pltpu.CompilerParams(vmem_limit_bytes=20 * 1024 * 1024),
        name="project",
    )(order, *arrays)


def finish_kernel(acc_ref, sq_ref, gain_ref, res_ref, out_ref):
    squares = jnp.sum(sq_ref[...], axis=0)
    scale = lax.rsqrt(squares / D + EPS)
    value = res_ref[...].astype(jnp.float32) + gain_ref[...] * (acc_ref[...] * scale)
    out_ref[...] = value.astype(jnp.bfloat16)


def finish(attended, squares, gain, residual):
    return pl.pallas_call(
        finish_kernel,
        in_specs=[VMEM] * 4,
        out_shape=jax.ShapeDtypeStruct((FEATURES, ROWS), jnp.bfloat16),
        compiler_params=pltpu.CompilerParams(vmem_limit_bytes=12 * 1024 * 1024),
        name="finish",
    )(attended, squares, gain, residual)


def device(x, y, core, head):
    return ((x % SIDE * SIDE + y % SIDE) * 2 + core) * N_HEAD + head % N_HEAD


def moved(array, rule):
    pairs = [
        (device(x, y, core, head), device(*rule(x, y, core, head)))
        for x in range(SIDE)
        for y in range(SIDE)
        for core in range(2)
        for head in range(N_HEAD)
    ]
    return lax.ppermute(array, ("seq", "head"), pairs)


def sense(core):
    return 1 - 2 * core


def spread(x, y, core, head):
    group = (2 * x + y // 2 + head) % N_HEAD
    return group // 2, group % 2 * 2 + (y + head) % 2, core, head


def lifted(x, y, core, head):
    return x, y, core, 2 * x + y // 2 - head


def on_device(positions, queries, keys, values, out_weight, post_gain, residual):
    seq = lax.axis_index("seq").astype(jnp.int32)
    head = lax.axis_index("head").astype(jnp.int32)
    shard = moved(out_weight.T, spread)

    half = HEAD_SIZE // 2
    inverse = 10000.0 ** (-2.0 * jnp.arange(half, dtype=jnp.float32) / HEAD_SIZE)
    inverse = jnp.concatenate([inverse, inverse])[None]
    own, cosine, sine = prepare(
        positions[None], inverse, keys.transpose(1, 0, 2), values.transpose(1, 0, 2)
    )
    far = lax.ppermute(own, "seq", [(i, i + 2) for i in range(N_SEQ - 2)])
    q = rotate(queries.reshape(ROWS, WIDTH), cosine, sine)
    shard, far = held(shard, far, after=[q])
    shard = moved(shard, lifted)
    given = jnp.where(seq % 2 == 0, own, far)
    prev = lax.ppermute(given, "seq", [(i, i ^ 1) for i in range(N_SEQ)])

    blocks = [[] for _ in range(N_HEAD)]
    place = seq.reshape(1)
    pieces = [x for n in range(0, PIECES, GROUP) for x in attend(n, place, q, own, prev, far)]
    for carried in pieces:
        blocks[0].append(carried)
        for k in range(1, N_HEAD):
            carried = moved(carried, lambda x, y, core, head: (x, y, core, head + sense(core)))
            blocks[k].append(carried)

    shard = held_alone(shard, after=blocks[0][-1:])
    weights = lax.all_gather(shard, "seq", axis=0).reshape(N_HEAD, 2, FEATURES // 2, WIDTH)

    source = (head - sense(seq % 2) * jnp.arange(N_HEAD, dtype=jnp.int32)) % N_HEAD
    order = jnp.stack([(source + head) % N_HEAD, source % 2]).astype(jnp.int32)
    attended, squares = project(order, weights, [x for row in blocks for x in row])
    squares = lax.all_to_all(squares, "head", 0, 0, tiled=True)
    return finish(attended, squares, post_gain[:, None], residual.T).T


def solution(mesh):
    return jax.shard_map(
        on_device,
        mesh=mesh,
        in_specs=(
            P("seq"),
            P("seq", "head", None),
            P("seq", "head", None),
            P("seq", "head", None),
            P("head", "seq"),
            P("head"),
            P("seq", "head"),
        ),
        out_specs=P("seq", "head"),
        check_vma=False,
    )
```
